128 devices in a mesh: slab: 16 (over x, z_lo, core), tile: 8 (over y, z_hi).
Axes of the slice: x: 4, y: 4, z: 4 (z_hi: 2, z_lo: 2; z = z_hi * 2 + z_lo), core: 2. Of those that a mesh axis runs over, the one named last changes fastest.
Arguments:
- volume: float32 [128, 512, 1024], P('slab', 'tile'), may hold values from -0.3 to 0.3
- shears: float32 [16], replicated, may hold values from -0.4 to 0.4
- tile_shift: int32 [16, 8], P(None, 'tile'), may hold values from -1 to 1
- illumination: float32 [2, 128, 128], replicated, may hold values from -6 to 6
- measured: bfloat16 [4096, 128, 128], P(('slab', 'tile')), may hold values from 0.049804688 to 2.5
- frame_owner: int32 [4096, 1], P(('slab', 'tile')), may hold values from 0 to 15; in each aligned block of 32 rows (0 to 31, 32 to 63, ...) at most 4 rows name the same one
- frame_shift: int32 [4096], P(('slab', 'tile')), may hold values from -32 to 32
Outputs:
- volume_grad: float32 [128, 512, 1024], P('slab', 'tile')
The draws below stay inside these ranges and needn't reach their ends.
Inputs may be any that keep to these rules, and one draw needn't show every extreme that they name: `frame_owner`: the 32 frames of one device name each angle at most 4 times, a bound that some block reaches.
All inputs are finite; a program needn't handle non-finite values.
Results may differ from the reference program's by a relative error of at most 0.012.
Values may be sent and summed in bfloat16 or wider, within the bound.
No kernel may reach another device: no remote copies, remote signals or barrier semaphores. Data moves between devices by JAX's collectives and lax.ppermute only.
A program may use at most 256 MiB of HBM per device.

```python
import math
import jax
import jax.numpy as jnp
import numpy as np
from jax import lax

SIDE = 128
SLICES = 128
GRID = 1024
BLOCK = 128
HALO = 32
ZT_DEV = 64
FR_DEV = 32
NZ = 512
ANGLES = 16
NFR = 4096
CAP = 4
N_SLAB = 16
N_TILE = 8


def set_ends(values, key, least, top_value):
    longest = values.shape.index(max(values.shape))
    spots = []
    for shift in (0, 1):
        where = [jax.random.randint(jax.random.fold_in(key, axis), (), 0, length) for axis, length in enumerate(values.shape)]
        where[longest] = (where[longest] + shift) % values.shape[longest]
        spots.append(tuple(where))
    return values.at[spots[0]].set(least).at[spots[1]].set(top_value)


def levels(key, extent, shards, smallest, high):
    def one(dim, blocks):
        draws = jax.random.uniform(jax.random.fold_in(jax.random.fold_in(key, 6), dim), (blocks,), jnp.float32, smallest / len(shards), high / len(shards))
        return jnp.repeat(jnp.exp(draws), extent[dim] // blocks).reshape((-1,) + (1,) * (len(extent) - dim - 1))

    gain = one(*shards[0])
    for cut in shards[1:]:
        gain = gain * one(*cut)
    return gain


def assign_block(stream_key, own, number, rows, count, top, reach, slope):
    order = jax.random.permutation(stream_key, count)
    heavy_load, usual = shares(count, rows * top, reach, slope, True), shares(count, rows * top, reach, slope, False)
    places = jnp.arange(count)

    def named(tallies, turn):
        used = int((tallies > 0).sum())
        fixed = max(1, used // 4)
        moved = fixed + (places - fixed + turn * (used - fixed)) % max(1, count - fixed)
        return jnp.zeros((count,), jnp.int32).at[order[jnp.where(places < fixed, places, moved)]].set(jnp.asarray(tallies, jnp.int32))

    tallies = jnp.where(number % 4 == 0, named(heavy_load, number // 4), named(usual, number - number // 4 - 1))
    mixed = jax.random.permutation(jax.random.fold_in(own, 3), count)
    source_of, taker = mixed[0:count // 2 * 2:2], mixed[1:count // 2 * 2:2]
    room = jnp.minimum(tallies[source_of] - 1, reach - tallies[taker]) // 2
    room = jnp.where((source_of == order[0]) | (taker == order[0]) | (tallies[taker] == 0), 0, jnp.maximum(room, 0))
    moved = jax.random.randint(jax.random.fold_in(own, 4), (count // 2,), 0, 1 << 20) % (room + 1)
    tallies = tallies.at[source_of].add(-moved).at[taker].add(moved)
    items = jnp.searchsorted(jnp.cumsum(tallies), jnp.arange(rows * top), side="right").astype(jnp.int32)
    grid = items.reshape(top, rows).T
    grid = grid[jax.random.permutation(jax.random.fold_in(own, 1), rows)]
    turn = jax.random.randint(jax.random.fold_in(own, 2), (rows, 1), 0, top)
    return jnp.take_along_axis(grid, (jnp.arange(top)[None, :] + turn) % top, axis=1)


def shares(amount, total, bound, lean, full):
    portions = [(1 << 20) // math.isqrt(rank ** lean) + 1 for rank in range(1, amount + 1)]
    largest = bound if full else min(bound, max(-(-total // amount), total * portions[0] // sum(portions)))
    least = 1 if total - largest >= amount - 1 else 0
    holding, rest = [largest] + [least] * (amount - 1), total - largest - least * (amount - 1)
    while rest > 0:
        free = [i for i in range(1, amount) if holding[i] < largest] or [i for i in range(1, amount) if holding[i] < bound]
        pool, left = sum([portions[i] for i in free]), rest
        for i in free:
            more = min(bound - holding[i], max(1, left * portions[i] // pool), rest)
            holding[i] = holding[i] + more
            rest = rest - more
    return np.array(holding)


def bell_draw(stream_key, extent, width, bound, split=(), kind=jnp.bfloat16):
    entries = jax.random.normal(stream_key, extent, jnp.float32) * width
    if len(split) > 0:
        entries = levels(stream_key, extent, split, -0.22, 0.18) * entries
    return jnp.clip(entries, min=-bound, max=bound).astype(kind)


def setup_inputs(seed: int = 0) -> dict:
    splits = jax.random.split(jax.random.key(seed), 8)
    volume = bell_draw(splits[0], (SLICES, NZ, GRID), 0.05, 0.3, ((0, 16), (1, 8)), jnp.float32)
    shears = jnp.clip(jax.random.uniform(splits[1], (ANGLES,), jnp.float32, -0.4, 0.4), -0.4, 0.4)
    tile_shift = set_ends(jax.random.randint(splits[2], (ANGLES, N_TILE), -1, 2), jax.random.fold_in(splits[2], 1), -1, 1).astype(jnp.int32)
    illumination = bell_draw(splits[3], (2, SIDE, SIDE), 1.0, 6.0, (), jnp.float32)
    measured = jnp.clip(0.049804688 + 2.4501953 * jax.random.uniform(splits[4], (NFR, SIDE, SIDE), jnp.float32) ** levels(splits[4], (NFR, SIDE, SIDE), ((0, 128),), -0.2, 0.2), 0.049804688, 2.5).astype(jnp.bfloat16)
    frame_owner_keys = jax.random.split(jax.random.fold_in(splits[5], 1), NFR // FR_DEV)
    frame_owner_turns = jax.random.permutation(jax.random.fold_in(splits[5], 3), NFR // FR_DEV)
    frame_owner = jax.vmap(lambda own, number: assign_block(jax.random.fold_in(splits[5], 2), own, number, FR_DEV, N_SLAB, 1, CAP, 2))(frame_owner_keys, frame_owner_turns).reshape((NFR, 1))
    frame_shift = set_ends(jax.random.randint(splits[6], (NFR,), -HALO, GRID // N_TILE - SIDE + HALO + 1), jax.random.fold_in(splits[6], 1), -HALO, (GRID // N_TILE - SIDE + HALO + 1) - 1).astype(jnp.int32)
    return dict(volume=volume, shears=shears, tile_shift=tile_shift, illumination=illumination, measured=measured, frame_owner=frame_owner, frame_shift=frame_shift)


smoothing = 0.25
highest = lax.Precision.HIGHEST

def beam_kernel(shear_one, beam_depth, block_width):
    beam_pos = jnp.arange(beam_depth, dtype=jnp.float32)
    centre = block_width * 0.5 + (beam_pos - (beam_depth - 1) * 0.5) * shear_one
    source = jnp.arange(block_width, dtype=jnp.float32)
    target = jnp.arange(2 * block_width, dtype=jnp.float32)
    spread = target[None, None, :] - source[None, :, None] - centre[:, None, None]
    values = jnp.exp(-0.5 * spread * spread).astype(jnp.bfloat16)
    return values.reshape(beam_depth * block_width, 2 * block_width)

def dft_tables(length):
    indices = jnp.arange(length, dtype=jnp.int32)
    product = indices[:, None] * indices[None, :] % length
    phases = product.astype(jnp.float32) * (2.0 * math.pi / length)
    return (jnp.cos(phases), jnp.sin(phases))

def left_mul(matrix, frames_in):
    return jnp.einsum('jk,nkl->njl', matrix, frames_in, precision=highest)

def right_mul(frames_in, matrix):
    return jnp.einsum('njk,kl->njl', frames_in, matrix, precision=highest)

def phase_gradient(windows, illumination, amplitude, dft_cos, dft_sin):
    length = dft_cos.shape[0]
    object_re = jnp.cos(windows)
    object_im = jnp.sin(windows)
    probe_re = illumination[0]
    probe_im = illumination[1]
    wave_re = probe_re * object_re - probe_im * object_im
    wave_im = probe_re * object_im + probe_im * object_re
    half_re = left_mul(dft_cos, wave_re) + left_mul(dft_sin, wave_im)
    half_im = left_mul(dft_cos, wave_im) - left_mul(dft_sin, wave_re)
    far_re = (right_mul(half_re, dft_cos) + right_mul(half_im, dft_sin)) / length
    far_im = (right_mul(half_im, dft_cos) - right_mul(half_re, dft_sin)) / length
    modulus = jnp.sqrt(far_re * far_re + far_im * far_im + smoothing)
    factor = 1.0 - amplitude / modulus
    resid_re = far_re * factor
    resid_im = far_im * factor
    back_re = left_mul(dft_cos, resid_re) - left_mul(dft_sin, resid_im)
    back_im = left_mul(dft_cos, resid_im) + left_mul(dft_sin, resid_re)
    near_re = (right_mul(back_re, dft_cos) - right_mul(back_im, dft_sin)) / length
    near_im = (right_mul(back_im, dft_cos) + right_mul(back_re, dft_sin)) / length
    grad_re = probe_re * near_re + probe_im * near_im
    grad_im = probe_re * near_im - probe_im * near_re
    return grad_im * object_re - grad_re * object_im

def reference(volume, shears, tile_shift, illumination, measured, frame_owner, frame_shift):
    blocks_row = GRID // BLOCK
    own_width = GRID // N_TILE
    block_ids = jnp.arange(blocks_row, dtype=jnp.int32)
    volume_half = lax.optimization_barrier(volume.astype(jnp.bfloat16))

    def make_kernel(shear_one):
        return beam_kernel(shear_one, ZT_DEV, BLOCK)
    kernels = lax.optimization_barrier(lax.map(make_kernel, shears))

    def selector(offset, plus_one):
        return (block_ids[:, None] == block_ids[None, :] + offset + plus_one).astype(jnp.float32)

    def project_angle(angle_id):
        kernel_wide = kernels[angle_id].astype(jnp.float32)

        def per_tile(running, tile_id):
            part_volume = lax.dynamic_slice_in_dim(volume_half, tile_id * ZT_DEV, ZT_DEV, 1)
            rows_matrix = part_volume.reshape(SLICES, ZT_DEV, blocks_row, BLOCK).transpose(0, 2, 1, 3)
            rows_matrix = rows_matrix.reshape(SLICES * blocks_row, ZT_DEV * BLOCK).astype(jnp.float32)
            partial_sum = jnp.dot(rows_matrix, kernel_wide, precision=highest).reshape(SLICES, blocks_row, 2, BLOCK)
            offset = tile_shift[angle_id, tile_id]
            shifted = jnp.einsum('ki,sib->skb', selector(offset, 0), partial_sum[:, :, 0], precision=highest)
            shifted = shifted + jnp.einsum('ki,sib->skb', selector(offset, 1), partial_sum[:, :, 1], precision=highest)
            return (running + shifted, None)
        initial = jnp.zeros((SLICES, blocks_row, BLOCK), jnp.float32)
        running, unused = lax.scan(per_tile, initial, jnp.arange(N_TILE, dtype=jnp.int32))
        return running.reshape(SLICES, GRID)
    projection = lax.map(project_angle, jnp.arange(ANGLES, dtype=jnp.int32))
    phase_pad = jnp.pad(projection, ((0, 0), (0, 0), (HALO, HALO)))
    dft_cos, dft_sin = dft_tables(SIDE)
    frame_ids = jnp.arange(NFR, dtype=jnp.int32)
    starts = frame_ids // FR_DEV % N_TILE * own_width + frame_shift + HALO
    angles = frame_owner[:, 0]
    batches = NFR // FR_DEV
    zero_index = jnp.zeros((), jnp.int32)

    def one_batch(grad_pad, batch_data):
        angle_batch, start_batch, amp_batch = batch_data

        def cut_one(angle_id, start_col):
            return lax.dynamic_slice(phase_pad[angle_id], (zero_index, start_col), (SIDE, SIDE))
        windows = jax.vmap(cut_one)(angle_batch, start_batch)
        dphase = phase_gradient(windows, illumination, amp_batch.astype(jnp.float32), dft_cos, dft_sin)

        def add_one(member, current):
            corner = (angle_batch[member], zero_index, start_batch[member])
            current_piece = lax.dynamic_slice(current, corner, (1, SIDE, SIDE))
            return lax.dynamic_update_slice(current, current_piece + dphase[member][None], corner)
        return (lax.fori_loop(0, FR_DEV, add_one, grad_pad), None)
    grad_initial = jnp.zeros_like(phase_pad)
    batch_inputs = (angles.reshape(batches, FR_DEV), starts.reshape(batches, FR_DEV), measured.reshape(batches, FR_DEV, SIDE, SIDE))
    grad_pad, unused = lax.scan(one_batch, grad_initial, batch_inputs)
    proj_grad = lax.optimization_barrier(grad_pad[:, :, HALO:HALO + GRID].astype(jnp.bfloat16))
    proj_wide = proj_grad.astype(jnp.float32).reshape(ANGLES, SLICES, blocks_row, BLOCK)

    def back_tile(tile_id):

        def per_angle(running, angle_id):
            kernel_wide = kernels[angle_id].astype(jnp.float32)
            offset = tile_shift[angle_id, tile_id]
            grad_rows = proj_wide[angle_id]
            pick_low = jnp.einsum('ki,skb->sib', selector(offset, 0), grad_rows, precision=highest)
            pick_high = jnp.einsum('ki,skb->sib', selector(offset, 1), grad_rows, precision=highest)
            stacked = jnp.concatenate([pick_low, pick_high], axis=2).reshape(SLICES * blocks_row, 2 * BLOCK)
            return (running + jnp.dot(stacked, kernel_wide.T, precision=highest), None)
        initial = jnp.zeros((SLICES * blocks_row, ZT_DEV * BLOCK), jnp.float32)
        running, unused = lax.scan(per_angle, initial, jnp.arange(ANGLES, dtype=jnp.int32))
        return running.reshape(SLICES, blocks_row, ZT_DEV, BLOCK).transpose(0, 2, 1, 3).reshape(SLICES, ZT_DEV, GRID)
    tile_grads = lax.map(back_tile, jnp.arange(N_TILE, dtype=jnp.int32))
    return tile_grads.transpose(1, 0, 2, 3).reshape(SLICES, NZ, GRID)
```

```python
import math

import jax
import jax.numpy as jnp
import numpy as np
from jax import lax
from jax.experimental import pallas as pl
from jax.experimental.pallas import tpu as pltpu
from jax.sharding import PartitionSpec as P

SIDE = 128
BLOCK = 128
HALO = 32
ANGLES = 16
DEPTH = 64
SLICES_DEV = 8
BLOCKS = 8
SLABS = 16
TILES = 8
FRAMES = 32
FIRST = 38
WIDE = 9 * BLOCK
FWD_FINE, FWD_COARSE = 4, 14
BWD_FINE, BWD_COARSE = 16, 4
OWN_ROWS, EDGE_ROWS = 32, 16
PAIR_ROWS = OWN_ROWS + EDGE_ROWS
ROWS = (SLICES_DEV // 2) * PAIR_ROWS
VMEM_LIMIT = 40 * 1024 * 1024

SIN_TERMS = (3.14159264, -5.16771008, 2.55007752, -0.598291286, 0.0776576603)
COS_TERMS = (1.0, -4.93480214, 4.05870916, -1.335212, 0.234937314, -0.0243963244)


def iota(shape, dim):
    return lax.broadcasted_iota(jnp.int32, shape, dim)


def poly(terms, t):
    total = jnp.full_like(t, terms[-1])
    for term in reversed(terms[:-1]):
        total = total * t + term
    return total


def sine_and_cosine(turns):
    t = turns * turns
    half_sin = turns * poly(SIN_TERMS, t)
    half_cos = poly(COS_TERMS, t)
    return (2.0 * half_sin * half_cos, 1.0 - 2.0 * half_sin * half_sin)


def pick_rows(values, shape, dim, period):
    index = iota(shape, dim) % period
    total = jnp.zeros(shape, values[0].dtype)
    for i, value in enumerate(values):
        total = jnp.where(index == i, value, total)
    return total


def bell(offset, centre):
    spread = offset - centre
    return jnp.exp(-0.5 * spread * spread).astype(jnp.bfloat16)


def left(value, steps):
    return pltpu.roll(value, value.shape[1] - steps, 1)


def project_kernel(shears, shifts, volume, out, table, stack):
    @pl.when(pl.program_id(0) == 0)
    def _():
        shape = (ANGLES, FWD_FINE * DEPTH)
        shear = pick_rows([shears[i] for i in range(ANGLES)], shape, 0, ANGLES)
        lane = iota(shape, 1)
        beam = (lane % DEPTH).astype(jnp.float32)
        centre = BLOCK * 0.5 + (beam - (DEPTH - 1) * 0.5) * shear
        fine = (lane // DEPTH).astype(jnp.float32)
        for j in range(FWD_COARSE):
            table[j * ANGLES : (j + 1) * ANGLES] = bell(fine + float(FIRST + FWD_FINE * j), centre)

    shape = (ANGLES, BLOCK)
    shift = pick_rows([shifts[i, 0] for i in range(ANGLES)], shape, 0, ANGLES)
    lane = iota((8, BLOCK), 1)
    edges = [[] for k in range(BLOCKS)]
    for half in range(2):
        rows = jnp.concatenate(
            [volume[half], jnp.zeros((DEPTH, WIDE - BLOCKS * BLOCK), jnp.float32)], axis=1
        )
        stack[half, 0:DEPTH] = rows.astype(jnp.bfloat16)
        for r in range(1, FWD_FINE):
            stack[half, r * DEPTH : (r + 1) * DEPTH] = pltpu.roll(rows, r, 1).astype(jnp.bfloat16)
        sums = jnp.dot(table[...], stack[half], preferred_element_type=jnp.float32)
        total = pltpu.roll(sums[0:ANGLES], FIRST, 1)
        for j in range(1, FWD_COARSE):
            part = sums[j * ANGLES : (j + 1) * ANGLES]
            total = total + pltpu.roll(part, FIRST + FWD_FINE * j, 1)
        turns = total * (1.0 / (2.0 * math.pi))
        turns = turns - jnp.floor(turns + 0.5)
        fixed = jnp.minimum(jnp.floor(turns * 65536.0 + 0.5), 32767.0)
        zero = jnp.zeros((ANGLES, BLOCK), jnp.float32)
        block = [fixed[:, k * BLOCK : (k + 1) * BLOCK] for k in range(BLOCKS + 1)]
        block = [zero] + block + [zero]
        placed = []
        for k in range(BLOCKS):
            here = jnp.where(shift == 0, block[k + 1], jnp.where(shift > 0, block[k], block[k + 2]))
            placed.append(here.astype(jnp.int32))
        zero = jnp.zeros((ANGLES, BLOCK), jnp.int32)
        around = [zero] + placed + [zero]
        for k in range(BLOCKS):
            out[k, half * ANGLES : (half + 1) * ANGLES] = placed[k].astype(jnp.int16)
            after, before = around[k + 2], around[k]
            low = jnp.where(lane < HALO, after[:8], before[:8])
            high = jnp.where(lane < HALO, after[8:], before[8:])
            outer = (lane < HALO) | (lane >= BLOCK - HALO)
            edge = jnp.where(outer, low, pltpu.roll(high, BLOCK // 2, 1))
            edges[k].append(edge)
    for k in range(BLOCKS):
        out[k, OWN_ROWS:PAIR_ROWS] = jnp.concatenate(edges[k], axis=0).astype(jnp.int16)


def project(shears, shifts, volume):
    return pl.pallas_call(
        project_kernel,
        name="project",
        grid=(SLICES_DEV // 2,),
        in_specs=[
            pl.BlockSpec(memory_space=pltpu.SMEM),
            pl.BlockSpec(memory_space=pltpu.SMEM),
            pl.BlockSpec((2, DEPTH, BLOCKS * BLOCK), lambda p: (p, 0, 0)),
        ],
        out_specs=pl.BlockSpec((TILES, PAIR_ROWS, BLOCK), lambda p: (0, p, 0)),
        out_shape=jax.ShapeDtypeStruct((TILES, ROWS, BLOCK), jnp.int16),
        scratch_shapes=[
            pltpu.VMEM((FWD_COARSE * ANGLES, FWD_FINE * DEPTH), jnp.bfloat16),
            pltpu.VMEM((2, FWD_FINE * DEPTH, WIDE), jnp.bfloat16),
        ],
        compiler_params=pltpu.CompilerParams(vmem_limit_bytes=VMEM_LIMIT),
    )(shears, shifts, volume)


def frames_kernel(owners, shifts, phases, probe, measured, spread, gather, out, own, edge, own_sum, edge_sum):
    lane = iota((8, BLOCK), 1)
    outer = (lane < HALO) | (lane >= BLOCK - HALO)

    def unpack(slab, carried):
        for p in range(SLICES_DEV // 2):
            base = pl.multiple_of(slab * BLOCK + p * OWN_ROWS, OWN_ROWS)
            rows = phases[slab, p * PAIR_ROWS : (p + 1) * PAIR_ROWS].astype(jnp.int32)
            rows = rows.astype(jnp.float32) * (1.0 / 65536.0)
            own[pl.ds(base, OWN_ROWS), :] = rows[:OWN_ROWS]
            for half in range(2):
                packed = rows[OWN_ROWS + half * 8 : OWN_ROWS + half * 8 + 8]
                edge[pl.ds(base + half * 16, 8), :] = packed
                edge[pl.ds(base + half * 16 + 8, 8), :] = pltpu.roll(packed, BLOCK // 2, 1)
        own_sum[pl.ds(pl.multiple_of(slab * BLOCK, BLOCK), BLOCK), :] = jnp.zeros((BLOCK, BLOCK), jnp.float32)
        edge_sum[pl.ds(pl.multiple_of(slab * BLOCK, BLOCK), BLOCK), :] = jnp.zeros((BLOCK, BLOCK), jnp.float32)
        return carried

    lax.fori_loop(0, SLABS, unpack, 0)

    wide_lane = iota((SIDE, BLOCK), 1)
    probe_re, probe_im = probe[0], probe[1]

    def pair(step, carried):
        waves, inside, rows_of, amount = [], [], [], []
        for k in range(2):
            f = step * 2 + k
            shift = shifts[f]
            rows = pl.ds(owners[f, 0], SIDE, stride=ANGLES)
            bound = jnp.where(shift >= 0, shift, shift + BLOCK)
            within = (wide_lane >= bound) == (shift >= 0)
            turns = pltpu.roll(jnp.where(within, own[rows, :], edge[rows, :]), lax.rem(BLOCK - shift, BLOCK), 1)
            object_im, object_re = sine_and_cosine(turns)
            wave_re = probe_re * object_re - probe_im * object_im
            wave_im = probe_re * object_im + probe_im * object_re
            waves.append((wave_re, wave_im))
            inside.append(within)
            rows_of.append(rows)
            amount.append(lax.rem(shift + BLOCK, BLOCK))
        fields = jnp.concatenate(
            [jnp.concatenate([re.astype(jnp.bfloat16), im.astype(jnp.bfloat16)], axis=1) for re, im in waves], axis=0
        )
        half = jnp.dot(fields, spread[...], preferred_element_type=jnp.float32).astype(jnp.bfloat16)

        def turned(value):
            top = jnp.concatenate([value[:SIDE, :SIDE], value[SIDE:, :SIDE]], axis=1)
            bottom = jnp.concatenate([value[:SIDE, SIDE:], value[SIDE:, SIDE:]], axis=1)
            return jnp.concatenate([top, bottom], axis=0)

        far = jnp.dot(gather[...], turned(half), preferred_element_type=jnp.float32)
        far_re, far_im = far[:SIDE], far[SIDE:]
        amplitude = jnp.concatenate(
            [measured[step * 2].astype(jnp.float32), measured[step * 2 + 1].astype(jnp.float32)], axis=1
        )
        factor = 1.0 - amplitude * lax.rsqrt(far_re * far_re + far_im * far_im + 0.25)
        resid = jnp.concatenate(
            [(far_re * factor).astype(jnp.bfloat16), (far_im * factor).astype(jnp.bfloat16)], axis=0
        )
        back = jnp.dot(spread[...], resid, preferred_element_type=jnp.float32).astype(jnp.bfloat16)
        near = jnp.dot(turned(back), gather[...], preferred_element_type=jnp.float32)
        for k in range(2):
            near_re = near[k * SIDE : (k + 1) * SIDE, :SIDE]
            near_im = near[k * SIDE : (k + 1) * SIDE, SIDE:]
            wave_re, wave_im = waves[k]
            grad = pltpu.roll(near_im * wave_re - near_re * wave_im, amount[k], 1)
            rows = rows_of[k]
            own_sum[rows, :] = own_sum[rows, :] + jnp.where(inside[k], grad, 0.0)
            edge_sum[rows, :] = edge_sum[rows, :] + jnp.where(inside[k], 0.0, grad)
        return carried

    lax.fori_loop(0, FRAMES // 2, pair, 0)

    def pack(slab, carried):
        for p in range(SLICES_DEV // 2):
            base = pl.multiple_of(slab * BLOCK + p * OWN_ROWS, OWN_ROWS)
            out[slab, p * PAIR_ROWS : p * PAIR_ROWS + OWN_ROWS] = own_sum[pl.ds(base, OWN_ROWS), :].astype(jnp.bfloat16)
            packed = []
            for half in range(2):
                low = edge_sum[pl.ds(base + half * 16, 8), :]
                high = edge_sum[pl.ds(base + half * 16 + 8, 8), :]
                packed.append(jnp.where(outer, low, pltpu.roll(high, BLOCK // 2, 1)))
            out[slab, p * PAIR_ROWS + OWN_ROWS : (p + 1) * PAIR_ROWS] = jnp.concatenate(packed, axis=0).astype(jnp.bfloat16)
        return carried

    lax.fori_loop(0, SLABS, pack, 0)


def frame_gradients(owners, shifts, phases, probe, measured, spread, gather):
    smem = pl.BlockSpec(memory_space=pltpu.SMEM)
    vmem = pl.BlockSpec(memory_space=pltpu.VMEM)
    table = pltpu.VMEM((SLABS * SLICES_DEV * ANGLES, BLOCK), jnp.float32)
    return pl.pallas_call(
        frames_kernel,
        name="frame_gradients",
        in_specs=[smem, smem, vmem, vmem, vmem, vmem, vmem],
        out_specs=vmem,
        out_shape=jax.ShapeDtypeStruct((SLABS, ROWS, BLOCK), jnp.bfloat16),
        scratch_shapes=[table, table, table, table],
        compiler_params=pltpu.CompilerParams(vmem_limit_bytes=VMEM_LIMIT),
    )(owners, shifts, phases, probe, measured, spread, gather)


def back_kernel(shears, shifts, tiles, out, table, stack):
    @pl.when(pl.program_id(0) == 0)
    def _():
        shape = (DEPTH, BWD_FINE * ANGLES)
        shear = pick_rows([shears[i] for i in range(ANGLES)], shape, 1, ANGLES)
        beam = iota(shape, 0).astype(jnp.float32)
        centre = BLOCK * 0.5 + (beam - (DEPTH - 1) * 0.5) * shear
        fine = (iota(shape, 1) // ANGLES).astype(jnp.float32)
        for j in range(BWD_COARSE):
            table[j * DEPTH : (j + 1) * DEPTH] = bell(fine + float(FIRST + BWD_FINE * j), centre)

    shape = (ANGLES, BLOCK)
    shift = pick_rows([shifts[i, 0] for i in range(ANGLES)], shape, 0, ANGLES)
    lane = iota(shape, 1)
    for half in range(2):
        own, margin = [], []
        for k in range(TILES):
            own.append(tiles[k, half * ANGLES : (half + 1) * ANGLES].astype(jnp.float32))
            packed = tiles[k, OWN_ROWS:PAIR_ROWS].astype(jnp.float32)[half * 8 : half * 8 + 8]
            margin.append(jnp.concatenate([packed, pltpu.roll(packed, BLOCK // 2, 1)], axis=0))
        whole = []
        for k in range(TILES):
            total = own[k]
            if k > 0:
                total = total + jnp.where(lane < HALO, margin[k - 1], 0.0)
            if k < TILES - 1:
                total = total + jnp.where(lane >= BLOCK - HALO, margin[k + 1], 0.0)
            whole.append(total.astype(jnp.bfloat16).astype(jnp.float32))
        zero = jnp.zeros(shape, jnp.float32)
        whole = [zero] + whole + [zero, zero]
        placed = [
            jnp.where(shift == 0, whole[k + 1], jnp.where(shift > 0, whole[k + 2], whole[k])) for k in range(BLOCKS + 1)
        ]
        placed = jnp.concatenate(placed, axis=1)
        stack[half, 0:ANGLES] = placed.astype(jnp.bfloat16)
        for r in range(1, BWD_FINE):
            stack[half, r * ANGLES : (r + 1) * ANGLES] = left(placed, r).astype(jnp.bfloat16)
        sums = jnp.dot(table[...], stack[half], preferred_element_type=jnp.float32)
        total = left(sums[0:DEPTH], FIRST)
        for j in range(1, BWD_COARSE):
            total = total + left(sums[j * DEPTH : (j + 1) * DEPTH], FIRST + BWD_FINE * j)
        out[half] = total[:, : BLOCKS * BLOCK]


def back_project(shears, shifts, tiles):
    return pl.pallas_call(
        back_kernel,
        name="back_project",
        grid=(SLICES_DEV // 2,),
        in_specs=[
            pl.BlockSpec(memory_space=pltpu.SMEM),
            pl.BlockSpec(memory_space=pltpu.SMEM),
            pl.BlockSpec((TILES, PAIR_ROWS, BLOCK), lambda p: (0, p, 0)),
        ],
        out_specs=pl.BlockSpec((2, DEPTH, BLOCKS * BLOCK), lambda p: (p, 0, 0)),
        out_shape=jax.ShapeDtypeStruct((SLICES_DEV, DEPTH, BLOCKS * BLOCK), jnp.float32),
        scratch_shapes=[
            pltpu.VMEM((BWD_COARSE * DEPTH, BWD_FINE * ANGLES), jnp.bfloat16),
            pltpu.VMEM((2, BWD_FINE * ANGLES, WIDE), jnp.bfloat16),
        ],
        compiler_params=pltpu.CompilerParams(vmem_limit_bytes=VMEM_LIMIT),
    )(shears, shifts, tiles)


def dft_matrices():
    index = np.arange(SIDE)
    phase = (np.outer(index, index) % SIDE) * (2.0 * np.pi / SIDE)
    cos, sin = np.cos(phase), np.sin(phase)
    spread = np.block([[cos, -sin], [sin, cos]])
    gather = np.block([[cos, sin], [-sin, cos]]) / SIDE
    return jnp.asarray(spread, jnp.bfloat16), jnp.asarray(gather, jnp.bfloat16)


def from_everyone(value, axis):
    copies = jnp.broadcast_to(value, (lax.axis_size(axis), *value.shape))
    return lax.all_to_all(copies, axis, split_axis=0, concat_axis=0, tiled=True)


def body(volume, shears, tile_shift, illumination, measured, frame_owner, frame_shift):
    spread, gather = dft_matrices()
    partials = project(shears, tile_shift, volume)
    landed = lax.all_to_all(partials, "tile", 0, 0, tiled=True)
    phase = jnp.sum(landed.astype(jnp.int32), axis=0)
    phase = (((phase + 32768) & 65535) - 32768).astype(jnp.int16)
    phases = from_everyone(phase, "slab")
    grads = frame_gradients(frame_owner, frame_shift, phases, illumination, measured, spread, gather)
    landed = lax.all_to_all(grads, "slab", 0, 0, tiled=True)
    grad = jnp.sum(landed.astype(jnp.float32), axis=0).astype(jnp.bfloat16)
    tiles = from_everyone(grad, "tile")
    return back_project(shears, tile_shift, tiles)


def solution(mesh):
    in_specs = (
        P("slab", "tile", None),
        P(),
        P(None, "tile"),
        P(),
        P(("slab", "tile"), None, None),
        P(("slab", "tile"), None),
        P(("slab", "tile")),
    )
    out_specs = P("slab", "tile", None)
    return jax.shard_map(body, mesh=mesh, in_specs=in_specs, out_specs=out_specs, check_vma=False)
```

```python
import math

import jax
import jax.numpy as jnp
import numpy as np
from jax import lax
from jax.experimental import pallas as pl
from jax.experimental.pallas import tpu as pltpu
from jax.sharding import PartitionSpec as P

SIDE = 128
BLOCK = 128
HALO = 32
ANGLES = 16
DEPTH = 64
SLICES_DEV = 8
BLOCKS = 8
SLABS = 16
TILES = 8
FRAMES = 32
FIRST = 38
WIDE = 9 * BLOCK
FWD_FINE, FWD_COARSE = 4, 14
BWD_FINE, BWD_COARSE = 16, 4
OWN_ROWS, EDGE_ROWS = 32, 16
PAIR_ROWS = OWN_ROWS + EDGE_ROWS
ROWS = (SLICES_DEV // 2) * PAIR_ROWS
GROUP = 8
UNPACK_UNROLL = 2
VMEM_LIMIT = 40 * 1024 * 1024

SIN_TERMS = (3.14159264, -5.16771008, 2.55007752, -0.598291286, 0.0776576603)
COS_TERMS = (1.0, -4.93480214, 4.05870916, -1.335212, 0.234937314, -0.0243963244)


def iota(shape, dim):
    return lax.broadcasted_iota(jnp.int32, shape, dim)


def poly(terms, t):
    total = jnp.full_like(t, terms[-1])
    for term in reversed(terms[:-1]):
        total = total * t + term
    return total


def sine_and_cosine(turns):
    t = turns * turns
    half_sin = turns * poly(SIN_TERMS, t)
    half_cos = poly(COS_TERMS, t)
    return (2.0 * half_sin * half_cos, 1.0 - 2.0 * half_sin * half_sin)


def pick_rows(values, shape, dim, period):
    index = iota(shape, dim) % period
    total = jnp.zeros(shape, values[0].dtype)
    for i, value in enumerate(values):
        total = jnp.where(index == i, value, total)
    return total


def bell(offset, centre):
    spread = offset - centre
    return jnp.exp(-0.5 * spread * spread).astype(jnp.bfloat16)


def left(value, steps):
    return pltpu.roll(value, value.shape[1] - steps, 1)


def project_kernel(shears, shifts, volume, out, table, stack):
    @pl.when(pl.program_id(0) == 0)
    def _():
        shape = (ANGLES, FWD_FINE * DEPTH)
        shear = pick_rows([shears[i] for i in range(ANGLES)], shape, 0, ANGLES)
        lane = iota(shape, 1)
        beam = (lane % DEPTH).astype(jnp.float32)
        centre = BLOCK * 0.5 + (beam - (DEPTH - 1) * 0.5) * shear
        fine = (lane // DEPTH).astype(jnp.float32)
        for j in range(FWD_COARSE):
            table[j * ANGLES : (j + 1) * ANGLES] = bell(fine + float(FIRST + FWD_FINE * j), centre)

    shape = (ANGLES, BLOCK)
    shift = pick_rows([shifts[i] for i in range(ANGLES)], shape, 0, ANGLES)
    lane = iota((8, BLOCK), 1)
    edges = [[] for k in range(BLOCKS)]
    for half in range(2):
        rows = jnp.concatenate(
            [volume[half], jnp.zeros((DEPTH, WIDE - BLOCKS * BLOCK), jnp.float32)], axis=1
        )
        stack[half, 0:DEPTH] = rows.astype(jnp.bfloat16)
        for r in range(1, FWD_FINE):
            stack[half, r * DEPTH : (r + 1) * DEPTH] = pltpu.roll(rows, r, 1).astype(jnp.bfloat16)
        sums = jnp.dot(table[...], stack[half], preferred_element_type=jnp.float32)
        total = pltpu.roll(sums[0:ANGLES], FIRST, 1)
        for j in range(1, FWD_COARSE):
            part = sums[j * ANGLES : (j + 1) * ANGLES]
            total = total + pltpu.roll(part, FIRST + FWD_FINE * j, 1)
        turns = total * (1.0 / (2.0 * math.pi))
        turns = turns - jnp.floor(turns + 0.5)
        fixed = jnp.minimum(jnp.floor(turns * 65536.0 + 0.5), 32767.0)
        zero = jnp.zeros((ANGLES, BLOCK), jnp.float32)
        block = [fixed[:, k * BLOCK : (k + 1) * BLOCK] for k in range(BLOCKS + 1)]
        block = [zero] + block + [zero]
        placed = []
        for k in range(BLOCKS):
            here = jnp.where(shift == 0, block[k + 1], jnp.where(shift > 0, block[k], block[k + 2]))
            placed.append(here.astype(jnp.int32))
        zero = jnp.zeros((ANGLES, BLOCK), jnp.int32)
        around = [zero] + placed + [zero]
        for k in range(BLOCKS):
            out[k, half * ANGLES : (half + 1) * ANGLES] = placed[k].astype(jnp.int16)
            after, before = around[k + 2], around[k]
            low = jnp.where(lane < HALO, after[:8], before[:8])
            high = jnp.where(lane < HALO, after[8:], before[8:])
            outer = (lane < HALO) | (lane >= BLOCK - HALO)
            edge = jnp.where(outer, low, pltpu.roll(high, BLOCK // 2, 1))
            edges[k].append(edge)
    for k in range(BLOCKS):
        out[k, OWN_ROWS:PAIR_ROWS] = jnp.concatenate(edges[k], axis=0).astype(jnp.int16)


def project(shears, shifts, volume):
    return pl.pallas_call(
        project_kernel,
        name="project",
        grid=(SLICES_DEV // 2,),
        in_specs=[
            pl.BlockSpec(memory_space=pltpu.SMEM),
            pl.BlockSpec(memory_space=pltpu.SMEM),
            pl.BlockSpec((2, DEPTH, BLOCKS * BLOCK), lambda p: (p, 0, 0)),
        ],
        out_specs=pl.BlockSpec((TILES, PAIR_ROWS, BLOCK), lambda p: (0, p, 0)),
        out_shape=jax.ShapeDtypeStruct((TILES, ROWS, BLOCK), jnp.int16),
        scratch_shapes=[
            pltpu.VMEM((FWD_COARSE * ANGLES, FWD_FINE * DEPTH), jnp.bfloat16),
            pltpu.VMEM((2, FWD_FINE * DEPTH, WIDE), jnp.bfloat16),
        ],
        compiler_params=pltpu.CompilerParams(vmem_limit_bytes=VMEM_LIMIT),
    )(shears, shifts, volume)


def frames_kernel(
    parity, owners_in, shifts_in, near_phases, far_phases, probe, measured, spread, gather,
    near_out, far_out, own, edge, own_sum, edge_sum, owners, shifts, sems,
):
    copies = [
        pltpu.make_async_copy(owners_in, owners, sems.at[0]),
        pltpu.make_async_copy(shifts_in, shifts, sems.at[1]),
    ]
    for copy in copies:
        copy.start()
    lane = iota((8, BLOCK), 1)
    outer = (lane < HALO) | (lane >= BLOCK - HALO)
    core = parity[0]

    def unpack(chip, carried):
        for which, phases in ((core, near_phases), (1 - core, far_phases)):
            start = pl.multiple_of((chip * 2 + which) * BLOCK, BLOCK)
            for p in range(SLICES_DEV // 2):
                base = pl.multiple_of(start + p * OWN_ROWS, OWN_ROWS)
                rows = phases[chip, p * PAIR_ROWS : (p + 1) * PAIR_ROWS].astype(jnp.int32).astype(jnp.float32)
                own[pl.ds(base, OWN_ROWS), :] = rows[:OWN_ROWS]
                for half in range(2):
                    packed = rows[OWN_ROWS + half * 8 : OWN_ROWS + half * 8 + 8]
                    edge[pl.ds(base + half * 16, 8), :] = packed
                    edge[pl.ds(base + half * 16 + 8, 8), :] = pltpu.roll(packed, BLOCK // 2, 1)
            own_sum[pl.ds(start, BLOCK), :] = jnp.zeros((BLOCK, BLOCK), jnp.float32)
            edge_sum[pl.ds(start, BLOCK), :] = jnp.zeros((BLOCK, BLOCK), jnp.float32)
        return carried

    lax.fori_loop(0, SLABS // 2, unpack, 0, unroll=UNPACK_UNROLL)
    for copy in copies:
        copy.wait()

    def tiled(value):
        return value.reshape(SIDE // 8, 8, BLOCK)

    def turned(value):
        top = jnp.concatenate([value[:SIDE, :SIDE], value[SIDE:, :SIDE]], axis=1)
        bottom = jnp.concatenate([value[:SIDE, SIDE:], value[SIDE:, SIDE:]], axis=1)
        return jnp.concatenate([top, bottom], axis=0)

    def group(step, carried):
        first = step * GROUP
        rows, inside, amount, waves, fields = [], [], [], [], []
        for k in range(GROUP):
            shift = shifts[first + k]
            rows.append(pl.ds(owners[first + k], SIDE, stride=ANGLES))
            bound = jnp.where(shift >= 0, shift, shift + BLOCK)
            inside.append((lane >= bound) == (shift >= 0))
            amount.append(bound)
        for k in range(GROUP):
            chosen = jnp.where(inside[k], tiled(own[rows[k], :]), tiled(edge[rows[k], :])).reshape(SIDE, BLOCK)
            turns = pltpu.roll(chosen, lax.rem(BLOCK - amount[k], BLOCK), 1) * (1.0 / 65536.0)
            object_im, object_re = sine_and_cosine(turns)
            wave_re = probe[0] * object_re - probe[1] * object_im
            wave_im = probe[0] * object_im + probe[1] * object_re
            waves.append((wave_re, wave_im))
            fields.append(jnp.concatenate([wave_re.astype(jnp.bfloat16), wave_im.astype(jnp.bfloat16)], axis=1))
        pairs = range(GROUP // 2)
        half = [
            jnp.dot(
                jnp.concatenate(fields[2 * g : 2 * g + 2], axis=0), spread[...], preferred_element_type=jnp.float32
            ).astype(jnp.bfloat16)
            for g in pairs
        ]
        far = [jnp.dot(gather[...], turned(half[g]), preferred_element_type=jnp.float32) for g in pairs]
        resid = []
        for g in pairs:
            far_re, far_im = far[g][:SIDE], far[g][SIDE:]
            amplitude = jnp.concatenate(
                [measured[first + 2 * g].astype(jnp.float32), measured[first + 2 * g + 1].astype(jnp.float32)], axis=1
            )
            factor = 1.0 - amplitude * lax.rsqrt(far_re * far_re + far_im * far_im + 0.25)
            resid.append(
                jnp.concatenate([(far_re * factor).astype(jnp.bfloat16), (far_im * factor).astype(jnp.bfloat16)], axis=0)
            )
        back = [
            jnp.dot(spread[...], resid[g], preferred_element_type=jnp.float32).astype(jnp.bfloat16) for g in pairs
        ]
        near = [jnp.dot(turned(back[g]), gather[...], preferred_element_type=jnp.float32) for g in pairs]
        grads = []
        for k in range(GROUP):
            part = near[k // 2][(k % 2) * SIDE : (k % 2 + 1) * SIDE]
            wave_re, wave_im = waves[k]
            grads.append(pltpu.roll(part[:, SIDE:] * wave_re - part[:, :SIDE] * wave_im, amount[k], 1))
        for k in range(GROUP):
            grad = tiled(grads[k])
            own_sum[rows[k], :] = own_sum[rows[k], :] + jnp.where(inside[k], grad, 0.0).reshape(SIDE, BLOCK)
            edge_sum[rows[k], :] = edge_sum[rows[k], :] + jnp.where(inside[k], 0.0, grad).reshape(SIDE, BLOCK)
        return carried

    lax.fori_loop(0, FRAMES // GROUP, group, 0)

    def pack(chip, carried):
        for which, out in ((core, near_out), (1 - core, far_out)):
            start = pl.multiple_of((chip * 2 + which) * BLOCK, BLOCK)
            for p in range(SLICES_DEV // 2):
                base = pl.multiple_of(start + p * OWN_ROWS, OWN_ROWS)
                top = p * PAIR_ROWS
                out[chip, top : top + OWN_ROWS] = own_sum[pl.ds(base, OWN_ROWS), :].astype(jnp.bfloat16)
                packed = []
                for half in range(2):
                    low = edge_sum[pl.ds(base + half * 16, 8), :]
                    high = edge_sum[pl.ds(base + half * 16 + 8, 8), :]
                    packed.append(jnp.where(outer, low, pltpu.roll(high, BLOCK // 2, 1)))
                out[chip, top + OWN_ROWS : top + PAIR_ROWS] = jnp.concatenate(packed, axis=0).astype(jnp.bfloat16)
        return carried

    lax.fori_loop(0, SLABS // 2, pack, 0, unroll=UNPACK_UNROLL)


def frame_gradients(parity, owners, shifts, near_phases, far_phases, probe, measured, spread, gather):
    smem = pl.BlockSpec(memory_space=pltpu.SMEM)
    hbm = pl.BlockSpec(memory_space=pltpu.HBM)
    vmem = pl.BlockSpec(memory_space=pltpu.VMEM)
    table = pltpu.VMEM((SLABS * SLICES_DEV * ANGLES, BLOCK), jnp.float32)
    half = jax.ShapeDtypeStruct((SLABS // 2, ROWS, BLOCK), jnp.bfloat16)
    return pl.pallas_call(
        frames_kernel,
        name="frame_gradients",
        in_specs=[smem, hbm, hbm, vmem, vmem, vmem, vmem, vmem, vmem],
        out_specs=[vmem, vmem],
        out_shape=[half, half],
        scratch_shapes=[
            table, table, table, table,
            pltpu.SMEM((FRAMES,), jnp.int32), pltpu.SMEM((FRAMES,), jnp.int32), pltpu.SemaphoreType.DMA((2,)),
        ],
        compiler_params=pltpu.CompilerParams(vmem_limit_bytes=VMEM_LIMIT),
    )(parity, owners, shifts, near_phases, far_phases, probe, measured, spread, gather)


def back_kernel(shears, shifts, tiles, out, table, stack):
    @pl.when(pl.program_id(0) == 0)
    def _():
        shape = (DEPTH, BWD_FINE * ANGLES)
        shear = pick_rows([shears[i] for i in range(ANGLES)], shape, 1, ANGLES)
        beam = iota(shape, 0).astype(jnp.float32)
        centre = BLOCK * 0.5 + (beam - (DEPTH - 1) * 0.5) * shear
        fine = (iota(shape, 1) // ANGLES).astype(jnp.float32)
        for j in range(BWD_COARSE):
            table[j * DEPTH : (j + 1) * DEPTH] = bell(fine + float(FIRST + BWD_FINE * j), centre)

    shape = (ANGLES, BLOCK)
    shift = pick_rows([shifts[i] for i in range(ANGLES)], shape, 0, ANGLES)
    lane = iota(shape, 1)
    for half in range(2):
        own, margin = [], []
        for k in range(TILES):
            own.append(tiles[k, half * ANGLES : (half + 1) * ANGLES].astype(jnp.float32))
            packed = tiles[k, OWN_ROWS:PAIR_ROWS].astype(jnp.float32)[half * 8 : half * 8 + 8]
            margin.append(jnp.concatenate([packed, pltpu.roll(packed, BLOCK // 2, 1)], axis=0))
        whole = []
        for k in range(TILES):
            total = own[k]
            if k > 0:
                total = total + jnp.where(lane < HALO, margin[k - 1], 0.0)
            if k < TILES - 1:
                total = total + jnp.where(lane >= BLOCK - HALO, margin[k + 1], 0.0)
            whole.append(total.astype(jnp.bfloat16).astype(jnp.float32))
        zero = jnp.zeros(shape, jnp.float32)
        whole = [zero] + whole + [zero, zero]
        placed = [
            jnp.where(shift == 0, whole[k + 1], jnp.where(shift > 0, whole[k + 2], whole[k])) for k in range(BLOCKS + 1)
        ]
        placed = jnp.concatenate(placed, axis=1)
        stack[half, 0:ANGLES] = placed.astype(jnp.bfloat16)
        for r in range(1, BWD_FINE):
            stack[half, r * ANGLES : (r + 1) * ANGLES] = left(placed, r).astype(jnp.bfloat16)
        sums = jnp.dot(table[...], stack[half], preferred_element_type=jnp.float32)
        total = left(sums[0:DEPTH], FIRST)
        for j in range(1, BWD_COARSE):
            total = total + left(sums[j * DEPTH : (j + 1) * DEPTH], FIRST + BWD_FINE * j)
        out[half] = total[:, : BLOCKS * BLOCK]


def back_project(shears, shifts, tiles):
    return pl.pallas_call(
        back_kernel,
        name="back_project",
        grid=(SLICES_DEV // 2,),
        in_specs=[
            pl.BlockSpec(memory_space=pltpu.SMEM),
            pl.BlockSpec(memory_space=pltpu.SMEM),
            pl.BlockSpec((TILES, PAIR_ROWS, BLOCK), lambda p: (0, p, 0)),
        ],
        out_specs=pl.BlockSpec((2, DEPTH, BLOCKS * BLOCK), lambda p: (p, 0, 0)),
        out_shape=jax.ShapeDtypeStruct((SLICES_DEV, DEPTH, BLOCKS * BLOCK), jnp.float32),
        scratch_shapes=[
            pltpu.VMEM((BWD_COARSE * DEPTH, BWD_FINE * ANGLES), jnp.bfloat16),
            pltpu.VMEM((2, BWD_FINE * ANGLES, WIDE), jnp.bfloat16),
        ],
        compiler_params=pltpu.CompilerParams(vmem_limit_bytes=VMEM_LIMIT),
    )(shears, shifts, tiles)


def dft_matrices():
    index = np.arange(SIDE)
    phase = (np.outer(index, index) % SIDE) * (2.0 * np.pi / SIDE)
    cos, sin = np.cos(phase), np.sin(phase)
    spread = np.block([[cos, -sin], [sin, cos]])
    gather = np.block([[cos, sin], [-sin, cos]]) / SIDE
    return jnp.asarray(spread, jnp.bfloat16), jnp.asarray(gather, jnp.bfloat16)


def copies_of(value, count):
    return jnp.broadcast_to(value, (count, *value.shape))


def between_chips(value):
    count = lax.axis_size("slab")
    groups = [list(range(core, count, 2)) for core in range(2)]
    return lax.all_to_all(value, "slab", 0, 0, tiled=True, axis_index_groups=groups)


def between_cores(value):
    return lax.ppermute(value, "slab", [(i, i ^ 1) for i in range(lax.axis_size("slab"))])


def body(volume, shears, tile_shift, illumination, measured, frame_owner, frame_shift):
    spread, gather = dft_matrices()
    shifts = tile_shift.reshape(ANGLES)
    parity = (lax.axis_index("slab") % 2).astype(jnp.int32).reshape(1)
    partials = project(shears, shifts, volume)
    landed = lax.all_to_all(partials, "tile", 0, 0, tiled=True)
    phase = jnp.sum(landed.astype(jnp.int32), axis=0)
    phase = (((phase + 32768) & 65535) - 32768).astype(jnp.int16)
    near_phases = between_chips(copies_of(phase, SLABS // 2))
    far_phases = between_cores(near_phases)
    near_grads, far_grads = frame_gradients(
        parity, frame_owner.reshape(FRAMES), frame_shift, near_phases, far_phases, illumination, measured, spread, gather
    )
    grads = near_grads.astype(jnp.float32) + between_cores(far_grads).astype(jnp.float32)
    landed = between_chips(grads.astype(jnp.bfloat16)).astype(jnp.float32)
    grad = landed[0]
    for i in range(1, SLABS // 2):
        grad = grad + landed[i]
    tiles = lax.all_to_all(copies_of(grad.astype(jnp.bfloat16), TILES), "tile", 0, 0, tiled=True)
    return back_project(shears, shifts, tiles)


def solution(mesh):
    in_specs = (
        P("slab", "tile", None),
        P(),
        P(None, "tile"),
        P(),
        P(("slab", "tile"), None, None),
        P(("slab", "tile"), None),
        P(("slab", "tile")),
    )
    out_specs = P("slab", "tile", None)
    return jax.shard_map(body, mesh=mesh, in_specs=in_specs, out_specs=out_specs, check_vma=False)
```

```python
import math

import jax
import jax.numpy as jnp
import numpy as np
from jax import lax
from jax.experimental import pallas as pl
from jax.experimental.pallas import tpu as pltpu
from jax.sharding import PartitionSpec as P

SIDE = 128
BLOCK = 128
HALO = 32
ANGLES = 16
DEPTH = 64
SLICES_DEV = 8
BLOCKS = 8
SLABS = 16
TILES = 8
FRAMES = 32
FIRST = 38
WIDE = 9 * BLOCK
FWD_FINE, FWD_COARSE = 4, 14
BWD_FINE, BWD_COARSE = 16, 4
OWN_ROWS, EDGE_ROWS = 32, 16
PAIR_ROWS = OWN_ROWS + EDGE_ROWS
PAIRS = SLICES_DEV // 2
ROWS = PAIRS * PAIR_ROWS
GROUP = 16
UNPACK_UNROLL = 2
VMEM_LIMIT = 40 * 1024 * 1024

SIN_TERMS = (3.14159264, -5.16771008, 2.55007752, -0.598291286, 0.0776576603)
COS_TERMS = (1.0, -4.93480214, 4.05870916, -1.335212, 0.234937314, -0.0243963244)


def iota(shape, dim):
    return lax.broadcasted_iota(jnp.int32, shape, dim)


def poly(terms, t):
    total = jnp.full_like(t, terms[-1])
    for term in reversed(terms[:-1]):
        total = total * t + term
    return total


def sine_and_cosine(turns):
    t = turns * turns
    half_sin = turns * poly(SIN_TERMS, t)
    half_cos = poly(COS_TERMS, t)
    return (2.0 * half_sin * half_cos, 1.0 - 2.0 * half_sin * half_sin)


def pick_rows(values, shape, dim, period):
    index = iota(shape, dim) % period
    total = jnp.zeros(shape, values[0].dtype)
    for i, value in enumerate(values):
        total = jnp.where(index == i, value, total)
    return total


def bell(offset, centre):
    spread = offset - centre
    return jnp.exp(-0.5 * spread * spread).astype(jnp.bfloat16)


def left(value, steps):
    return pltpu.roll(value, value.shape[1] - steps, 1)


def project_kernel(shears_in, shifts_in, volume_in, out, table, stack, volume, shears, shifts, sems):
    copies = [
        pltpu.make_async_copy(shears_in, shears, sems.at[0]),
        pltpu.make_async_copy(shifts_in, shifts, sems.at[1]),
    ]
    for p in range(PAIRS):
        part = pl.ds(p * 2, 2)
        copies.append(pltpu.make_async_copy(volume_in.at[part], volume.at[part], sems.at[2 + p]))
    for copy in copies:
        copy.start()
    copies[0].wait()
    shape = (ANGLES, FWD_FINE * DEPTH)
    shear = pick_rows([shears[i] for i in range(ANGLES)], shape, 0, ANGLES)
    lane = iota(shape, 1)
    beam = (lane % DEPTH).astype(jnp.float32)
    centre = BLOCK * 0.5 + (beam - (DEPTH - 1) * 0.5) * shear
    fine = (lane // DEPTH).astype(jnp.float32)
    for j in range(FWD_COARSE):
        table[j * ANGLES : (j + 1) * ANGLES] = bell(fine + float(FIRST + FWD_FINE * j), centre)
    copies[1].wait()
    shape = (ANGLES, BLOCK)
    shift = pick_rows([shifts[i] for i in range(ANGLES)], shape, 0, ANGLES)
    lane = iota((8, BLOCK), 1)
    outer = (lane < HALO) | (lane >= BLOCK - HALO)
    zero = jnp.zeros(shape, jnp.float32)
    for p in range(PAIRS):
        copies[2 + p].wait()
        for half in range(2):
            rows = jnp.concatenate(
                [volume[p * 2 + half], jnp.zeros((DEPTH, WIDE - BLOCKS * BLOCK), jnp.float32)], axis=1
            )
            for r in range(FWD_FINE):
                moved = rows if r == 0 else pltpu.roll(rows, r, 1)
                stack[p, r * DEPTH : (r + 1) * DEPTH, half * WIDE : (half + 1) * WIDE] = moved.astype(jnp.bfloat16)
        both = jnp.dot(table[...], stack[p], preferred_element_type=jnp.float32)
        edges = [[] for k in range(BLOCKS)]
        for half in range(2):
            sums = both[:, half * WIDE : (half + 1) * WIDE]
            total = pltpu.roll(sums[0:ANGLES], FIRST, 1)
            for j in range(1, FWD_COARSE):
                total = total + pltpu.roll(sums[j * ANGLES : (j + 1) * ANGLES], FIRST + FWD_FINE * j, 1)
            turns = total * (1.0 / (2.0 * math.pi))
            turns = turns - jnp.floor(turns + 0.5)
            fixed = jnp.minimum(jnp.floor(turns * 65536.0 + 0.5), 32767.0)
            block = [zero] + [fixed[:, k * BLOCK : (k + 1) * BLOCK] for k in range(BLOCKS + 1)] + [zero]
            placed = []
            for k in range(BLOCKS):
                here = jnp.where(shift == 0, block[k + 1], jnp.where(shift > 0, block[k], block[k + 2]))
                placed.append(here.astype(jnp.int32))
            nothing = jnp.zeros(shape, jnp.int32)
            around = [nothing] + placed + [nothing]
            for k in range(BLOCKS):
                top = p * PAIR_ROWS + half * ANGLES
                out[k, top : top + ANGLES] = placed[k].astype(jnp.int16)
                after, before = around[k + 2], around[k]
                low = jnp.where(lane < HALO, after[:8], before[:8])
                high = jnp.where(lane < HALO, after[8:], before[8:])
                edges[k].append(jnp.where(outer, low, pltpu.roll(high, BLOCK // 2, 1)))
        for k in range(BLOCKS):
            top = p * PAIR_ROWS + OWN_ROWS
            out[k, top : top + EDGE_ROWS] = jnp.concatenate(edges[k], axis=0).astype(jnp.int16)


def project(shears, shifts, volume):
    hbm = pl.BlockSpec(memory_space=pltpu.HBM)
    return pl.pallas_call(
        project_kernel,
        name="project",
        in_specs=[hbm, hbm, hbm],
        out_specs=pl.BlockSpec(memory_space=pltpu.VMEM),
        out_shape=jax.ShapeDtypeStruct((TILES, ROWS, BLOCK), jnp.int16),
        scratch_shapes=[
            pltpu.VMEM((FWD_COARSE * ANGLES, FWD_FINE * DEPTH), jnp.bfloat16),
            pltpu.VMEM((PAIRS, FWD_FINE * DEPTH, 2 * WIDE), jnp.bfloat16),
            pltpu.VMEM((SLICES_DEV, DEPTH, BLOCKS * BLOCK), jnp.float32),
            pltpu.SMEM((ANGLES,), jnp.float32),
            pltpu.SMEM((ANGLES,), jnp.int32),
            pltpu.SemaphoreType.DMA((2 + PAIRS,)),
        ],
        compiler_params=pltpu.CompilerParams(vmem_limit_bytes=VMEM_LIMIT),
    )(shears, shifts, volume)


def frames_kernel(
    parity, owners_in, shifts_in, near_phases, far_phases, probe, measured, spread, gather,
    near_out, far_out, own, edge, own_sum, edge_sum, owners, shifts, sems,
):
    copies = [
        pltpu.make_async_copy(owners_in, owners, sems.at[0]),
        pltpu.make_async_copy(shifts_in, shifts, sems.at[1]),
    ]
    for copy in copies:
        copy.start()
    lane = iota((8, BLOCK), 1)
    outer = (lane < HALO) | (lane >= BLOCK - HALO)
    core = parity[0]

    def unpack(chip, carried):
        for which, phases in ((core, near_phases), (1 - core, far_phases)):
            start = pl.multiple_of((chip * 2 + which) * BLOCK, BLOCK)
            for p in range(SLICES_DEV // 2):
                base = pl.multiple_of(start + p * OWN_ROWS, OWN_ROWS)
                rows = phases[chip, p * PAIR_ROWS : (p + 1) * PAIR_ROWS].astype(jnp.int32).astype(jnp.float32)
                own[pl.ds(base, OWN_ROWS), :] = rows[:OWN_ROWS]
                for half in range(2):
                    packed = rows[OWN_ROWS + half * 8 : OWN_ROWS + half * 8 + 8]
                    edge[pl.ds(base + half * 16, 8), :] = packed
                    edge[pl.ds(base + half * 16 + 8, 8), :] = pltpu.roll(packed, BLOCK // 2, 1)
            own_sum[pl.ds(start, BLOCK), :] = jnp.zeros((BLOCK, BLOCK), jnp.float32)
            edge_sum[pl.ds(start, BLOCK), :] = jnp.zeros((BLOCK, BLOCK), jnp.float32)
        return carried

    lax.fori_loop(0, SLABS // 2, unpack, 0, unroll=UNPACK_UNROLL)
    for copy in copies:
        copy.wait()

    def tiled(value):
        return value.reshape(SIDE // 8, 8, BLOCK)

    def turned(value):
        top = jnp.concatenate([value[:SIDE, :SIDE], value[SIDE:, :SIDE]], axis=1)
        bottom = jnp.concatenate([value[:SIDE, SIDE:], value[SIDE:, SIDE:]], axis=1)
        return jnp.concatenate([top, bottom], axis=0)

    def group(step, carried):
        first = step * GROUP
        rows, inside, amount, waves, fields = [], [], [], [], []
        for k in range(GROUP):
            shift = shifts[first + k]
            rows.append(pl.ds(owners[first + k], SIDE, stride=ANGLES))
            bound = jnp.where(shift >= 0, shift, shift + BLOCK)
            inside.append((lane >= bound) == (shift >= 0))
            amount.append(bound)
        for k in range(GROUP):
            chosen = jnp.where(inside[k], tiled(own[rows[k], :]), tiled(edge[rows[k], :])).reshape(SIDE, BLOCK)
            turns = pltpu.roll(chosen, lax.rem(BLOCK - amount[k], BLOCK), 1) * (1.0 / 65536.0)
            object_im, object_re = sine_and_cosine(turns)
            wave_re = probe[0] * object_re - probe[1] * object_im
            wave_im = probe[0] * object_im + probe[1] * object_re
            waves.append((wave_re, wave_im))
            fields.append(jnp.concatenate([wave_re.astype(jnp.bfloat16), wave_im.astype(jnp.bfloat16)], axis=1))
        pairs = range(GROUP // 2)
        half = [
            jnp.dot(
                jnp.concatenate(fields[2 * g : 2 * g + 2], axis=0), spread[...], preferred_element_type=jnp.float32
            ).astype(jnp.bfloat16)
            for g in pairs
        ]
        far = [jnp.dot(gather[...], turned(half[g]), preferred_element_type=jnp.float32) for g in pairs]
        resid = []
        for g in pairs:
            far_re, far_im = far[g][:SIDE], far[g][SIDE:]
            amplitude = jnp.concatenate(
                [measured[first + 2 * g].astype(jnp.float32), measured[first + 2 * g + 1].astype(jnp.float32)], axis=1
            )
            factor = 1.0 - amplitude * lax.rsqrt(far_re * far_re + far_im * far_im + 0.25)
            resid.append(
                jnp.concatenate([(far_re * factor).astype(jnp.bfloat16), (far_im * factor).astype(jnp.bfloat16)], axis=0)
            )
        back = [
            jnp.dot(spread[...], resid[g], preferred_element_type=jnp.float32).astype(jnp.bfloat16) for g in pairs
        ]
        near = [jnp.dot(turned(back[g]), gather[...], preferred_element_type=jnp.float32) for g in pairs]
        grads = []
        for k in range(GROUP):
            part = near[k // 2][(k % 2) * SIDE : (k % 2 + 1) * SIDE]
            wave_re, wave_im = waves[k]
            grads.append(pltpu.roll(part[:, SIDE:] * wave_re - part[:, :SIDE] * wave_im, amount[k], 1))
        for k in range(GROUP):
            grad = tiled(grads[k])
            own_sum[rows[k], :] = own_sum[rows[k], :] + jnp.where(inside[k], grad, 0.0).reshape(SIDE, BLOCK)
            edge_sum[rows[k], :] = edge_sum[rows[k], :] + jnp.where(inside[k], 0.0, grad).reshape(SIDE, BLOCK)
        return carried

    lax.fori_loop(0, FRAMES // GROUP, group, 0)

    def pack(chip, carried):
        for which, out in ((core, near_out), (1 - core, far_out)):
            start = pl.multiple_of((chip * 2 + which) * BLOCK, BLOCK)
            for p in range(SLICES_DEV // 2):
                base = pl.multiple_of(start + p * OWN_ROWS, OWN_ROWS)
                top = p * PAIR_ROWS
                out[chip, top : top + OWN_ROWS] = own_sum[pl.ds(base, OWN_ROWS), :].astype(jnp.bfloat16)
                packed = []
                for half in range(2):
                    low = edge_sum[pl.ds(base + half * 16, 8), :]
                    high = edge_sum[pl.ds(base + half * 16 + 8, 8), :]
                    packed.append(jnp.where(outer, low, pltpu.roll(high, BLOCK // 2, 1)))
                out[chip, top + OWN_ROWS : top + PAIR_ROWS] = jnp.concatenate(packed, axis=0).astype(jnp.bfloat16)
        return carried

    lax.fori_loop(0, SLABS // 2, pack, 0, unroll=UNPACK_UNROLL)


def frame_gradients(parity, owners, shifts, near_phases, far_phases, probe, measured, spread, gather):
    smem = pl.BlockSpec(memory_space=pltpu.SMEM)
    hbm = pl.BlockSpec(memory_space=pltpu.HBM)
    vmem = pl.BlockSpec(memory_space=pltpu.VMEM)
    table = pltpu.VMEM((SLABS * SLICES_DEV * ANGLES, BLOCK), jnp.float32)
    half = jax.ShapeDtypeStruct((SLABS // 2, ROWS, BLOCK), jnp.bfloat16)
    return pl.pallas_call(
        frames_kernel,
        name="frame_gradients",
        in_specs=[smem, hbm, hbm, vmem, vmem, vmem, vmem, vmem, vmem],
        out_specs=[vmem, vmem],
        out_shape=[half, half],
        scratch_shapes=[
            table, table, table, table,
            pltpu.SMEM((FRAMES,), jnp.int32), pltpu.SMEM((FRAMES,), jnp.int32), pltpu.SemaphoreType.DMA((2,)),
        ],
        compiler_params=pltpu.CompilerParams(vmem_limit_bytes=VMEM_LIMIT),
    )(parity, owners, shifts, near_phases, far_phases, probe, measured, spread, gather)


def back_kernel(shears_in, shifts_in, tiles, out_hbm, table, stack, out, shears, shifts, sems):
    copies = [
        pltpu.make_async_copy(shears_in, shears, sems.at[0]),
        pltpu.make_async_copy(shifts_in, shifts, sems.at[1]),
    ]
    for copy in copies:
        copy.start()
    copies[0].wait()
    shape = (DEPTH, BWD_FINE * ANGLES)
    shear = pick_rows([shears[i] for i in range(ANGLES)], shape, 1, ANGLES)
    beam = iota(shape, 0).astype(jnp.float32)
    centre = BLOCK * 0.5 + (beam - (DEPTH - 1) * 0.5) * shear
    fine = (iota(shape, 1) // ANGLES).astype(jnp.float32)
    for j in range(BWD_COARSE):
        table[j * DEPTH : (j + 1) * DEPTH] = bell(fine + float(FIRST + BWD_FINE * j), centre)
    copies[1].wait()
    shape = (ANGLES, BLOCK)
    shift = pick_rows([shifts[i] for i in range(ANGLES)], shape, 0, ANGLES)
    lane = iota(shape, 1)
    zero = jnp.zeros(shape, jnp.float32)
    sends = []
    for p in range(PAIRS):
        top = p * PAIR_ROWS
        for half in range(2):
            own, margin = [], []
            for k in range(TILES):
                first = top + half * ANGLES
                own.append(tiles[k, first : first + ANGLES].astype(jnp.float32))
                packed = tiles[k, top + OWN_ROWS : top + PAIR_ROWS].astype(jnp.float32)[half * 8 : half * 8 + 8]
                margin.append(jnp.concatenate([packed, pltpu.roll(packed, BLOCK // 2, 1)], axis=0))
            whole = []
            for k in range(TILES):
                total = own[k]
                if k > 0:
                    total = total + jnp.where(lane < HALO, margin[k - 1], 0.0)
                if k < TILES - 1:
                    total = total + jnp.where(lane >= BLOCK - HALO, margin[k + 1], 0.0)
                whole.append(total.astype(jnp.bfloat16).astype(jnp.float32))
            whole = [zero] + whole + [zero, zero]
            placed = jnp.concatenate(
                [
                    jnp.where(shift == 0, whole[k + 1], jnp.where(shift > 0, whole[k + 2], whole[k]))
                    for k in range(BLOCKS + 1)
                ],
                axis=1,
            )
            for r in range(BWD_FINE):
                moved = left(placed, FIRST + r)
                stack[p, r * ANGLES : (r + 1) * ANGLES, half * WIDE : (half + 1) * WIDE] = moved.astype(jnp.bfloat16)
        both = jnp.dot(table[...], stack[p], preferred_element_type=jnp.float32)
        for half in range(2):
            sums = both[:, half * WIDE : (half + 1) * WIDE]
            total = sums[0:DEPTH]
            for j in range(1, BWD_COARSE):
                total = total + left(sums[j * DEPTH : (j + 1) * DEPTH], BWD_FINE * j)
            out[p * 2 + half] = total[:, : BLOCKS * BLOCK]
        part = pl.ds(p * 2, 2)
        sends.append(pltpu.make_async_copy(out.at[part], out_hbm.at[part], sems.at[2 + p]))
        sends[-1].start()
    for send in sends:
        send.wait()


def back_project(shears, shifts, tiles):
    hbm = pl.BlockSpec(memory_space=pltpu.HBM)
    return pl.pallas_call(
        back_kernel,
        name="back_project",
        in_specs=[hbm, hbm, pl.BlockSpec(memory_space=pltpu.VMEM)],
        out_specs=hbm,
        out_shape=jax.ShapeDtypeStruct((SLICES_DEV, DEPTH, BLOCKS * BLOCK), jnp.float32),
        scratch_shapes=[
            pltpu.VMEM((BWD_COARSE * DEPTH, BWD_FINE * ANGLES), jnp.bfloat16),
            pltpu.VMEM((PAIRS, BWD_FINE * ANGLES, 2 * WIDE), jnp.bfloat16),
            pltpu.VMEM((SLICES_DEV, DEPTH, BLOCKS * BLOCK), jnp.float32),
            pltpu.SMEM((ANGLES,), jnp.float32),
            pltpu.SMEM((ANGLES,), jnp.int32),
            pltpu.SemaphoreType.DMA((2 + PAIRS,)),
        ],
        compiler_params=pltpu.CompilerParams(vmem_limit_bytes=VMEM_LIMIT),
    )(shears, shifts, tiles)


def dft_matrices():
    index = np.arange(SIDE)
    phase = (np.outer(index, index) % SIDE) * (2.0 * np.pi / SIDE)
    cos, sin = np.cos(phase), np.sin(phase)
    spread = np.block([[cos, -sin], [sin, cos]])
    gather = np.block([[cos, sin], [-sin, cos]]) / SIDE
    return jnp.asarray(spread, jnp.bfloat16), jnp.asarray(gather, jnp.bfloat16)


def copies_of(value, count):
    return jnp.broadcast_to(value, (count, *value.shape))


def between_chips(value):
    count = lax.axis_size("slab")
    groups = [list(range(core, count, 2)) for core in range(2)]
    return lax.all_to_all(value, "slab", 0, 0, tiled=True, axis_index_groups=groups)


def between_cores(value):
    return lax.ppermute(value, "slab", [(i, i ^ 1) for i in range(lax.axis_size("slab"))])


def body(volume, shears, tile_shift, illumination, measured, frame_owner, frame_shift):
    spread, gather = dft_matrices()
    shifts = tile_shift.reshape(ANGLES)
    parity = (lax.axis_index("slab") % 2).astype(jnp.int32).reshape(1)
    partials = project(shears, shifts, volume)
    landed = lax.all_to_all(partials, "tile", 0, 0, tiled=True)
    phase = jnp.sum(landed.astype(jnp.int32), axis=0)
    phase = (((phase + 32768) & 65535) - 32768).astype(jnp.int16)
    near_phases = between_chips(copies_of(phase, SLABS // 2))
    far_phases = between_cores(near_phases)
    near_grads, far_grads = frame_gradients(
        parity, frame_owner.reshape(FRAMES), frame_shift, near_phases, far_phases, illumination, measured, spread, gather
    )
    grads = near_grads.astype(jnp.float32) + between_cores(far_grads).astype(jnp.float32)
    landed = between_chips(grads.astype(jnp.bfloat16)).astype(jnp.float32)
    grad = landed[0]
    for i in range(1, SLABS // 2):
        grad = grad + landed[i]
    tiles = lax.all_to_all(copies_of(grad.astype(jnp.bfloat16), TILES), "tile", 0, 0, tiled=True)
    return back_project(shears, shifts, tiles)


def solution(mesh):
    in_specs = (
        P("slab", "tile", None),
        P(),
        P(None, "tile"),
        P(),
        P(("slab", "tile"), None, None),
        P(("slab", "tile"), None),
        P(("slab", "tile")),
    )
    out_specs = P("slab", "tile", None)
    return jax.shard_map(body, mesh=mesh, in_specs=in_specs, out_specs=out_specs, check_vma=False)
```

```python
import math

import jax
import jax.numpy as jnp
import numpy as np
from jax import lax
from jax.experimental import pallas as pl
from jax.experimental.pallas import tpu as pltpu
from jax.sharding import PartitionSpec as P

SIDE = 128
BLOCK = 128
HALO = 32
ANGLES = 16
DEPTH = 64
SLICES_DEV = 8
BLOCKS = 8
SLABS = 16
TILES = 8
FRAMES = 32
FIRST = 38
WIDE = 9 * BLOCK
FWD_FINE, FWD_COARSE = 4, 14
BWD_FINE, BWD_COARSE = 16, 4
OWN_ROWS, EDGE_ROWS = ANGLES * SLICES_DEV, ANGLES // 2 * SLICES_DEV
PAIRS = SLICES_DEV // 2
ROWS = OWN_ROWS + EDGE_ROWS
GROUP = 16
UNPACK_UNROLL = 2
VMEM_LIMIT = 40 * 1024 * 1024
ALL_VMEM = 60 * 1024 * 1024

SIN_TERMS = (3.14159264, -5.16771008, 2.55007752, -0.598291286, 0.0776576603)
COS_TERMS = (0.999999953, -4.93479283, 4.05841135, -1.33187657, 0.219689611)


def iota(shape, dim):
    return lax.broadcasted_iota(jnp.int32, shape, dim)


def poly(terms, t):
    total = jnp.full_like(t, terms[-1])
    for term in reversed(terms[:-1]):
        total = total * t + term
    return total


def sine_and_cosine(turns):
    t = turns * turns
    half_sin = turns * poly(SIN_TERMS, t)
    half_cos = poly(COS_TERMS, t)
    return (2.0 * half_sin * half_cos, 1.0 - 2.0 * half_sin * half_sin)


def pick_rows(values, shape, dim, period):
    index = iota(shape, dim) % period
    total = jnp.zeros(shape, values[0].dtype)
    for i, value in enumerate(values):
        total = jnp.where(index == i, value, total)
    return total


def bell(offset, centre):
    spread = offset - centre
    return jnp.exp(-0.5 * spread * spread).astype(jnp.bfloat16)


def left(value, steps):
    return pltpu.roll(value, value.shape[1] - steps, 1)


def project_kernel(shears_in, shifts_in, volume_in, out, table, stack, volume, gathered, shears, shifts, sems):
    copies = [
        pltpu.make_async_copy(shears_in, shears, sems.at[0]),
        pltpu.make_async_copy(shifts_in, shifts, sems.at[1]),
    ]
    for p in range(PAIRS):
        part = pl.ds(p * 2, 2)
        copies.append(pltpu.make_async_copy(volume_in.at[part], volume.at[part], sems.at[2 + p]))
    for copy in copies:
        copy.start()
    copies[0].wait()
    shape = (ANGLES, FWD_FINE * DEPTH)
    shear = pick_rows([shears[i] for i in range(ANGLES)], shape, 0, ANGLES)
    lane = iota(shape, 1)
    beam = (lane % DEPTH).astype(jnp.float32)
    centre = BLOCK * 0.5 + (beam - (DEPTH - 1) * 0.5) * shear
    fine = (lane // DEPTH).astype(jnp.float32)
    for j in range(FWD_COARSE):
        table[j * ANGLES : (j + 1) * ANGLES] = bell(fine + float(FIRST + FWD_FINE * j), centre)
    copies[1].wait()
    shape = (ANGLES, BLOCK)
    shift = pick_rows([shifts[i] for i in range(ANGLES)], shape, 0, ANGLES)
    lane = iota((8, BLOCK), 1)
    outer = (lane < HALO) | (lane >= BLOCK - HALO)
    zero = jnp.zeros(shape, jnp.float32)
    for p in range(PAIRS):
        copies[2 + p].wait()
        for half in range(2):
            rows = jnp.concatenate(
                [volume[p * 2 + half], jnp.zeros((DEPTH, WIDE - BLOCKS * BLOCK), jnp.float32)], axis=1
            )
            for r in range(FWD_FINE):
                moved = rows if r == 0 else pltpu.roll(rows, r, 1)
                stack[p, r * DEPTH : (r + 1) * DEPTH, half * WIDE : (half + 1) * WIDE] = moved.astype(jnp.bfloat16)
        both = jnp.dot(table[...], stack[p], preferred_element_type=jnp.float32)
        for half in range(2):
            sums = both[:, half * WIDE : (half + 1) * WIDE]
            total = pltpu.roll(sums[0:ANGLES], FIRST, 1)
            for j in range(1, FWD_COARSE):
                total = total + pltpu.roll(sums[j * ANGLES : (j + 1) * ANGLES], FIRST + FWD_FINE * j, 1)
            turns = total * (1.0 / (2.0 * math.pi))
            turns = turns - jnp.floor(turns + 0.5)
            fixed = jnp.minimum(jnp.floor(turns * 65536.0 + 0.5), 32767.0)
            block = [zero] + [fixed[:, k * BLOCK : (k + 1) * BLOCK] for k in range(BLOCKS + 1)] + [zero]
            placed = []
            for k in range(BLOCKS):
                here = jnp.where(shift == 0, block[k + 1], jnp.where(shift > 0, block[k], block[k + 2]))
                placed.append(here)
            around = [zero] + placed + [zero]
            s = p * 2 + half
            for k in range(BLOCKS):
                gathered[k, pl.ds(s, ANGLES, stride=SLICES_DEV), :] = placed[k]
                after, before = around[k + 2], around[k]
                low = jnp.where(lane < HALO, after[:8], before[:8])
                high = jnp.where(lane < HALO, after[8:], before[8:])
                edge = jnp.where(outer, low, pltpu.roll(high, BLOCK // 2, 1))
                gathered[k, pl.ds(OWN_ROWS + s, ANGLES // 2, stride=SLICES_DEV), :] = edge
    for k in range(BLOCKS):
        out[k] = gathered[k].astype(jnp.int32).astype(jnp.int16)


def project(shears, shifts, volume):
    hbm = pl.BlockSpec(memory_space=pltpu.HBM)
    return pl.pallas_call(
        project_kernel,
        name="project",
        in_specs=[hbm, hbm, hbm],
        out_specs=pl.BlockSpec(memory_space=pltpu.VMEM),
        out_shape=jax.ShapeDtypeStruct((TILES, ROWS, BLOCK), jnp.int16),
        scratch_shapes=[
            pltpu.VMEM((FWD_COARSE * ANGLES, FWD_FINE * DEPTH), jnp.bfloat16),
            pltpu.VMEM((PAIRS, FWD_FINE * DEPTH, 2 * WIDE), jnp.bfloat16),
            pltpu.VMEM((SLICES_DEV, DEPTH, BLOCKS * BLOCK), jnp.float32),
            pltpu.VMEM((BLOCKS, ROWS, BLOCK), jnp.float32),
            pltpu.SMEM((ANGLES,), jnp.float32),
            pltpu.SMEM((ANGLES,), jnp.int32),
            pltpu.SemaphoreType.DMA((2 + PAIRS,)),
        ],
        compiler_params=pltpu.CompilerParams(vmem_limit_bytes=ALL_VMEM),
    )(shears, shifts, volume)


def frames_kernel(
    parity, owners_in, shifts_in, near_phases, far_phases, probe, measured, spread, gather,
    near_out, far_out, own, edge, own_sum, edge_sum, owners, shifts, sems,
):
    copies = [
        pltpu.make_async_copy(owners_in, owners, sems.at[0]),
        pltpu.make_async_copy(shifts_in, shifts, sems.at[1]),
    ]
    for copy in copies:
        copy.start()
    lane = iota((8, BLOCK), 1)
    outer = (lane < HALO) | (lane >= BLOCK - HALO)
    core = parity[0]

    def unpack(chip, carried):
        for which, phases in ((core, near_phases), (1 - core, far_phases)):
            base = pl.multiple_of((chip * 2 + which) * SLICES_DEV, SLICES_DEV)
            rows = phases[chip].astype(jnp.int32).astype(jnp.float32)
            zero = jnp.zeros((SLICES_DEV, BLOCK), jnp.float32)
            for i in range(ANGLES):
                here = pl.ds(base + i * SIDE, SLICES_DEV)
                first = OWN_ROWS + i % (ANGLES // 2) * SLICES_DEV
                packed = rows[first : first + SLICES_DEV]
                own[here, :] = rows[i * SLICES_DEV : (i + 1) * SLICES_DEV]
                edge[here, :] = packed if i < ANGLES // 2 else pltpu.roll(packed, BLOCK // 2, 1)
                own_sum[here, :] = zero
                edge_sum[here, :] = zero
        return carried

    lax.fori_loop(0, SLABS // 2, unpack, 0, unroll=UNPACK_UNROLL)
    for copy in copies:
        copy.wait()

    def tiled(value):
        return value.reshape(SIDE // 8, 8, BLOCK)

    def turned(value):
        top = jnp.concatenate([value[:SIDE, :SIDE], value[SIDE:, :SIDE]], axis=1)
        bottom = jnp.concatenate([value[:SIDE, SIDE:], value[SIDE:, SIDE:]], axis=1)
        return jnp.concatenate([top, bottom], axis=0)

    def group(step, carried):
        first = step * GROUP
        rows, inside, amount, waves, fields = [], [], [], [], []
        for k in range(GROUP):
            shift = shifts[first + k]
            rows.append(pl.ds(pl.multiple_of(owners[first + k] * SIDE, SIDE), SIDE))
            bound = jnp.where(shift >= 0, shift, shift + BLOCK)
            inside.append((lane >= bound) == (shift >= 0))
            amount.append(bound)
        for k in range(GROUP):
            chosen = jnp.where(inside[k], tiled(own[rows[k], :]), tiled(edge[rows[k], :])).reshape(SIDE, BLOCK)
            turns = pltpu.roll(chosen, lax.rem(BLOCK - amount[k], BLOCK), 1) * (1.0 / 65536.0)
            object_im, object_re = sine_and_cosine(turns)
            wave_re = probe[0] * object_re - probe[1] * object_im
            wave_im = probe[0] * object_im + probe[1] * object_re
            waves.append((wave_re, wave_im))
            fields.append(jnp.concatenate([wave_re.astype(jnp.bfloat16), wave_im.astype(jnp.bfloat16)], axis=1))
        pairs = range(GROUP // 2)
        half = [
            jnp.dot(
                jnp.concatenate(fields[2 * g : 2 * g + 2], axis=0), spread[...], preferred_element_type=jnp.float32
            ).astype(jnp.bfloat16)
            for g in pairs
        ]
        far = [jnp.dot(gather[...], turned(half[g]), preferred_element_type=jnp.float32) for g in pairs]
        resid = []
        for g in pairs:
            far_re, far_im = far[g][:SIDE], far[g][SIDE:]
            amplitude = jnp.concatenate(
                [measured[first + 2 * g].astype(jnp.float32), measured[first + 2 * g + 1].astype(jnp.float32)], axis=1
            )
            factor = 1.0 - amplitude * lax.rsqrt(far_re * far_re + far_im * far_im + 0.25)
            resid.append(
                jnp.concatenate([(far_re * factor).astype(jnp.bfloat16), (far_im * factor).astype(jnp.bfloat16)], axis=0)
            )
        back = [
            jnp.dot(spread[...], resid[g], preferred_element_type=jnp.float32).astype(jnp.bfloat16) for g in pairs
        ]
        near = [jnp.dot(turned(back[g]), gather[...], preferred_element_type=jnp.float32) for g in pairs]
        grads = []
        for k in range(GROUP):
            part = near[k // 2][(k % 2) * SIDE : (k % 2 + 1) * SIDE]
            wave_re, wave_im = waves[k]
            grads.append(pltpu.roll(part[:, SIDE:] * wave_re - part[:, :SIDE] * wave_im, amount[k], 1))
        for k in range(GROUP):
            grad = tiled(grads[k])
            own_sum[rows[k], :] = own_sum[rows[k], :] + jnp.where(inside[k], grad, 0.0).reshape(SIDE, BLOCK)
            edge_sum[rows[k], :] = edge_sum[rows[k], :] + jnp.where(inside[k], 0.0, grad).reshape(SIDE, BLOCK)
        return carried

    lax.fori_loop(0, FRAMES // GROUP, group, 0)

    def pack(chip, carried):
        for which, out in ((core, near_out), (1 - core, far_out)):
            base = pl.multiple_of((chip * 2 + which) * SLICES_DEV, SLICES_DEV)
            here = [pl.ds(base + i * SIDE, SLICES_DEV) for i in range(ANGLES)]
            rows = [own_sum[here[i], :] for i in range(ANGLES)]
            for i in range(ANGLES // 2):
                high = pltpu.roll(edge_sum[here[i + ANGLES // 2], :], BLOCK // 2, 1)
                rows.append(jnp.where(outer, edge_sum[here[i], :], high))
            out[chip] = jnp.concatenate(rows, axis=0).astype(jnp.bfloat16)
        return carried

    lax.fori_loop(0, SLABS // 2, pack, 0, unroll=UNPACK_UNROLL)


def frame_gradients(parity, owners, shifts, near_phases, far_phases, probe, measured, spread, gather):
    smem = pl.BlockSpec(memory_space=pltpu.SMEM)
    hbm = pl.BlockSpec(memory_space=pltpu.HBM)
    vmem = pl.BlockSpec(memory_space=pltpu.VMEM)
    table = pltpu.VMEM((SLABS * SLICES_DEV * ANGLES, BLOCK), jnp.float32)
    half = jax.ShapeDtypeStruct((SLABS // 2, ROWS, BLOCK), jnp.bfloat16)
    return pl.pallas_call(
        frames_kernel,
        name="frame_gradients",
        in_specs=[smem, hbm, hbm, vmem, vmem, vmem, vmem, vmem, vmem],
        out_specs=[vmem, vmem],
        out_shape=[half, half],
        scratch_shapes=[
            table, table, table, table,
            pltpu.SMEM((FRAMES,), jnp.int32), pltpu.SMEM((FRAMES,), jnp.int32), pltpu.SemaphoreType.DMA((2,)),
        ],
        compiler_params=pltpu.CompilerParams(vmem_limit_bytes=VMEM_LIMIT),
    )(parity, owners, shifts, near_phases, far_phases, probe, measured, spread, gather)


def back_kernel(shears_in, shifts_in, tiles, out_hbm, table, stack, out, gathered, shears, shifts, sems):
    copies = [
        pltpu.make_async_copy(shears_in, shears, sems.at[0]),
        pltpu.make_async_copy(shifts_in, shifts, sems.at[1]),
    ]
    for copy in copies:
        copy.start()
    copies[0].wait()
    shape = (DEPTH, BWD_FINE * ANGLES)
    shear = pick_rows([shears[i] for i in range(ANGLES)], shape, 1, ANGLES)
    beam = iota(shape, 0).astype(jnp.float32)
    centre = BLOCK * 0.5 + (beam - (DEPTH - 1) * 0.5) * shear
    fine = (iota(shape, 1) // ANGLES).astype(jnp.float32)
    for j in range(BWD_COARSE):
        table[j * DEPTH : (j + 1) * DEPTH] = bell(fine + float(FIRST + BWD_FINE * j), centre)
    copies[1].wait()
    shape = (ANGLES, BLOCK)
    shift = pick_rows([shifts[i] for i in range(ANGLES)], shape, 0, ANGLES)
    lane = iota(shape, 1)
    zero = jnp.zeros(shape, jnp.float32)
    sends = []
    for k in range(TILES):
        gathered[k] = tiles[k].astype(jnp.float32)
    for p in range(PAIRS):
        for half in range(2):
            own, margin = [], []
            for k in range(TILES):
                s = p * 2 + half
                own.append(gathered[k, pl.ds(s, ANGLES, stride=SLICES_DEV), :])
                packed = gathered[k, pl.ds(OWN_ROWS + s, ANGLES // 2, stride=SLICES_DEV), :]
                margin.append(jnp.concatenate([packed, pltpu.roll(packed, BLOCK // 2, 1)], axis=0))
            whole = []
            for k in range(TILES):
                total = own[k]
                if k > 0:
                    total = total + jnp.where(lane < HALO, margin[k - 1], 0.0)
                if k < TILES - 1:
                    total = total + jnp.where(lane >= BLOCK - HALO, margin[k + 1], 0.0)
                whole.append(total.astype(jnp.bfloat16).astype(jnp.float32))
            whole = [zero] + whole + [zero, zero]
            placed = jnp.concatenate(
                [
                    jnp.where(shift == 0, whole[k + 1], jnp.where(shift > 0, whole[k + 2], whole[k]))
                    for k in range(BLOCKS + 1)
                ],
                axis=1,
            )
            for r in range(BWD_FINE):
                moved = left(placed, FIRST + r)
                stack[p, r * ANGLES : (r + 1) * ANGLES, half * WIDE : (half + 1) * WIDE] = moved.astype(jnp.bfloat16)
        both = jnp.dot(table[...], stack[p], preferred_element_type=jnp.float32)
        for half in range(2):
            sums = both[:, half * WIDE : (half + 1) * WIDE]
            total = sums[0:DEPTH]
            for j in range(1, BWD_COARSE):
                total = total + left(sums[j * DEPTH : (j + 1) * DEPTH], BWD_FINE * j)
            out[p * 2 + half] = total[:, : BLOCKS * BLOCK]
        part = pl.ds(p * 2, 2)
        sends.append(pltpu.make_async_copy(out.at[part], out_hbm.at[part], sems.at[2 + p]))
        sends[-1].start()
    for send in sends:
        send.wait()


def back_project(shears, shifts, tiles):
    hbm = pl.BlockSpec(memory_space=pltpu.HBM)
    return pl.pallas_call(
        back_kernel,
        name="back_project",
        in_specs=[hbm, hbm, pl.BlockSpec(memory_space=pltpu.VMEM)],
        out_specs=hbm,
        out_shape=jax.ShapeDtypeStruct((SLICES_DEV, DEPTH, BLOCKS * BLOCK), jnp.float32),
        scratch_shapes=[
            pltpu.VMEM((BWD_COARSE * DEPTH, BWD_FINE * ANGLES), jnp.bfloat16),
            pltpu.VMEM((PAIRS, BWD_FINE * ANGLES, 2 * WIDE), jnp.bfloat16),
            pltpu.VMEM((SLICES_DEV, DEPTH, BLOCKS * BLOCK), jnp.float32),
            pltpu.VMEM((TILES, ROWS, BLOCK), jnp.float32),
            pltpu.SMEM((ANGLES,), jnp.float32),
            pltpu.SMEM((ANGLES,), jnp.int32),
            pltpu.SemaphoreType.DMA((2 + PAIRS,)),
        ],
        compiler_params=pltpu.CompilerParams(vmem_limit_bytes=VMEM_LIMIT),
    )(shears, shifts, tiles)


def dft_matrices():
    index = np.arange(SIDE)
    phase = (np.outer(index, index) % SIDE) * (2.0 * np.pi / SIDE)
    cos, sin = np.cos(phase), np.sin(phase)
    spread = np.block([[cos, -sin], [sin, cos]])
    gather = np.block([[cos, sin], [-sin, cos]]) / SIDE
    return jnp.asarray(spread, jnp.bfloat16), jnp.asarray(gather, jnp.bfloat16)


def copies_of(value, count):
    return jnp.broadcast_to(value, (count, *value.shape))


def between_chips(value):
    count = lax.axis_size("slab")
    groups = [list(range(core, count, 2)) for core in range(2)]
    return lax.all_to_all(value, "slab", 0, 0, tiled=True, axis_index_groups=groups)


def between_cores(value):
    return lax.ppermute(value, "slab", [(i, i ^ 1) for i in range(lax.axis_size("slab"))])


def body(volume, shears, tile_shift, illumination, measured, frame_owner, frame_shift):
    spread, gather = dft_matrices()
    shifts = tile_shift.reshape(ANGLES)
    parity = (lax.axis_index("slab") % 2).astype(jnp.int32).reshape(1)
    partials = project(shears, shifts, volume)
    landed = lax.all_to_all(partials, "tile", 0, 0, tiled=True)
    phase = jnp.sum(landed.astype(jnp.int32), axis=0)
    phase = (((phase + 32768) & 65535) - 32768).astype(jnp.int16)
    near_phases = between_chips(copies_of(phase, SLABS // 2))
    far_phases = between_cores(near_phases)
    near_grads, far_grads = frame_gradients(
        parity, frame_owner.reshape(FRAMES), frame_shift, near_phases, far_phases, illumination, measured, spread, gather
    )
    grads = near_grads.astype(jnp.float32) + between_cores(far_grads).astype(jnp.float32)
    landed = between_chips(grads.astype(jnp.bfloat16)).astype(jnp.float32)
    grad = landed[0]
    for i in range(1, SLABS // 2):
        grad = grad + landed[i]
    tiles = lax.all_to_all(copies_of(grad.astype(jnp.bfloat16), TILES), "tile", 0, 0, tiled=True)
    return back_project(shears, shifts, tiles)


def solution(mesh):
    in_specs = (
        P("slab", "tile", None),
        P(),
        P(None, "tile"),
        P(),
        P(("slab", "tile"), None, None),
        P(("slab", "tile"), None),
        P(("slab", "tile")),
    )
    out_specs = P("slab", "tile", None)
    return jax.shard_map(body, mesh=mesh, in_specs=in_specs, out_specs=out_specs, check_vma=False)
```

```python
import math

import jax
import jax.numpy as jnp
import numpy as np
from jax import lax
from jax.experimental import pallas as pl
from jax.experimental.pallas import tpu as pltpu
from jax.sharding import PartitionSpec as P

SIDE = 128
BLOCK = 128
HALO = 32
ANGLES = 16
DEPTH = 64
SLICES_DEV = 8
BLOCKS = 8
SLABS = 16
TILES = 8
FRAMES = 32
FIRST = 38
WIDE = 9 * BLOCK
FWD_FINE, FWD_COARSE = 4, 14
BWD_FINE, BWD_COARSE = 14, 4
OWN_ROWS, EDGE_ROWS = ANGLES * SLICES_DEV, ANGLES // 2 * SLICES_DEV
PAIRS = SLICES_DEV // 2
ROWS = OWN_ROWS + EDGE_ROWS
GROUP = 32
UNPACK_UNROLL = 2
VMEM_LIMIT = 40 * 1024 * 1024
ALL_VMEM = 60 * 1024 * 1024

SIN_TERMS = (3.14159264, -5.16771008, 2.55007752, -0.598291286, 0.0776576603)
COS_TERMS = (0.999999953, -4.93479283, 4.05841135, -1.33187657, 0.219689611)


def iota(shape, dim):
    return lax.broadcasted_iota(jnp.int32, shape, dim)


def poly(terms, t):
    total = jnp.full_like(t, terms[-1])
    for term in reversed(terms[:-1]):
        total = total * t + term
    return total


def sine_and_cosine(turns):
    t = turns * turns
    half_sin = turns * poly(SIN_TERMS, t)
    half_cos = poly(COS_TERMS, t)
    return (2.0 * half_sin * half_cos, 1.0 - 2.0 * half_sin * half_sin)


def pick_rows(values, shape, dim, period):
    index = iota(shape, dim) % period
    total = jnp.zeros(shape, values[0].dtype)
    for i, value in enumerate(values):
        total = jnp.where(index == i, value, total)
    return total


def bell(offset, centre):
    spread = offset - centre
    return jnp.exp(-0.5 * spread * spread).astype(jnp.bfloat16)


def left(value, steps):
    return pltpu.roll(value, value.shape[1] - steps, 1)


def project_kernel(shears_in, shifts_in, volume_in, out, table, stack, volume, gathered, shears, shifts, sems):
    copies = [
        pltpu.make_async_copy(shears_in, shears, sems.at[0]),
        pltpu.make_async_copy(shifts_in, shifts, sems.at[1]),
    ]
    for p in range(PAIRS):
        part = pl.ds(p * 2, 2)
        copies.append(pltpu.make_async_copy(volume_in.at[part], volume.at[part], sems.at[2 + p]))
    for copy in copies:
        copy.start()
    copies[0].wait()
    shape = (ANGLES, FWD_FINE * DEPTH)
    shear = pick_rows([shears[i] for i in range(ANGLES)], shape, 0, ANGLES)
    lane = iota(shape, 1)
    beam = (lane % DEPTH).astype(jnp.float32)
    centre = BLOCK * 0.5 + (beam - (DEPTH - 1) * 0.5) * shear
    fine = (lane // DEPTH).astype(jnp.float32)
    for j in range(FWD_COARSE):
        table[j * ANGLES : (j + 1) * ANGLES] = bell(fine + float(FIRST + FWD_FINE * j), centre)
    copies[1].wait()
    shape = (ANGLES, BLOCK)
    shift = pick_rows([shifts[i] for i in range(ANGLES)], shape, 0, ANGLES)
    lane = iota((8, BLOCK), 1)
    full_lane = iota(shape, 1)
    outer = (lane < HALO) | (lane >= BLOCK - HALO)
    zero = jnp.zeros(shape, jnp.float32)
    for p in range(PAIRS):
        copies[2 + p].wait()
        for half in range(2):
            rows = jnp.concatenate(
                [volume[p * 2 + half], jnp.zeros((DEPTH, WIDE - BLOCKS * BLOCK), jnp.float32)], axis=1
            ).astype(jnp.bfloat16)
            for r in range(FWD_FINE):
                moved = rows if r == 0 else jnp.concatenate([rows[:, WIDE - r :], rows[:, : WIDE - r]], axis=1)
                stack[p, r * DEPTH : (r + 1) * DEPTH, half * WIDE : (half + 1) * WIDE] = moved
        fixed = []
        for n in range(WIDE // BLOCK):
            sums = jnp.dot(table[...], stack[p, :, n * 2 * BLOCK : (n + 1) * 2 * BLOCK], preferred_element_type=jnp.float32)
            for b in range(2):
                rolled = [
                    pltpu.roll(sums[j * ANGLES : (j + 1) * ANGLES, b * BLOCK : (b + 1) * BLOCK], FIRST + FWD_FINE * j, 1)
                    for j in range(FWD_COARSE)
                ]
                if (2 * n + b) % (BLOCKS + 1) == 0:
                    before = [zero] * FWD_COARSE
                total = jnp.where(full_lane >= FIRST, rolled[0], before[0])
                for j in range(1, FWD_COARSE):
                    total = total + jnp.where(full_lane >= FIRST + FWD_FINE * j, rolled[j], before[j])
                before = rolled
                turns = total * (1.0 / (2.0 * math.pi))
                turns = turns - jnp.floor(turns + 0.5)
                fixed.append(jnp.minimum(jnp.floor(turns * 65536.0 + 0.5), 32767.0))
        for half in range(2):
            block = [zero] + fixed[half * (BLOCKS + 1) : (half + 1) * (BLOCKS + 1)] + [zero]
            placed = []
            for k in range(BLOCKS):
                here = jnp.where(shift == 0, block[k + 1], jnp.where(shift > 0, block[k], block[k + 2]))
                placed.append(here)
            around = [zero] + placed + [zero]
            s = p * 2 + half
            for k in range(BLOCKS):
                gathered[k, pl.ds(s, ANGLES, stride=SLICES_DEV), :] = placed[k]
                after, before = around[k + 2], around[k]
                low = jnp.where(lane < HALO, after[:8], before[:8])
                high = jnp.where(lane < HALO, after[8:], before[8:])
                edge = jnp.where(outer, low, pltpu.roll(high, BLOCK // 2, 1))
                gathered[k, pl.ds(OWN_ROWS + s, ANGLES // 2, stride=SLICES_DEV), :] = edge
    for k in range(BLOCKS):
        out[k] = gathered[k].astype(jnp.int32).astype(jnp.int16)


def project(shears, shifts, volume):
    hbm = pl.BlockSpec(memory_space=pltpu.HBM)
    return pl.pallas_call(
        project_kernel,
        name="project",
        in_specs=[hbm, hbm, hbm],
        out_specs=pl.BlockSpec(memory_space=pltpu.VMEM),
        out_shape=jax.ShapeDtypeStruct((TILES, ROWS, BLOCK), jnp.int16),
        scratch_shapes=[
            pltpu.VMEM((FWD_COARSE * ANGLES, FWD_FINE * DEPTH), jnp.bfloat16),
            pltpu.VMEM((PAIRS, FWD_FINE * DEPTH, 2 * WIDE), jnp.bfloat16),
            pltpu.VMEM((SLICES_DEV, DEPTH, BLOCKS * BLOCK), jnp.float32),
            pltpu.VMEM((BLOCKS, ROWS, BLOCK), jnp.float32),
            pltpu.SMEM((ANGLES,), jnp.float32),
            pltpu.SMEM((ANGLES,), jnp.int32),
            pltpu.SemaphoreType.DMA((2 + PAIRS,)),
        ],
        compiler_params=pltpu.CompilerParams(vmem_limit_bytes=ALL_VMEM),
    )(shears, shifts, volume)


def frames_kernel(
    parity, owners_in, shifts_in, near_phases, far_phases, probe, measured, spread, gather,
    near_out, far_out, own, edge, own_sum, edge_sum, owners, shifts, sems,
):
    copies = [
        pltpu.make_async_copy(owners_in, owners, sems.at[0]),
        pltpu.make_async_copy(shifts_in, shifts, sems.at[1]),
    ]
    for copy in copies:
        copy.start()
    lane = iota((8, BLOCK), 1)
    outer = (lane < HALO) | (lane >= BLOCK - HALO)
    core = parity[0]

    def unpack(chip, carried):
        for which, phases in ((core, near_phases), (1 - core, far_phases)):
            base = pl.multiple_of((chip * 2 + which) * SLICES_DEV, SLICES_DEV)
            rows = phases[chip].astype(jnp.int32).astype(jnp.float32)
            zero = jnp.zeros((SLICES_DEV, BLOCK), jnp.float32)
            for i in range(ANGLES):
                here = pl.ds(base + i * SIDE, SLICES_DEV)
                first = OWN_ROWS + i % (ANGLES // 2) * SLICES_DEV
                packed = rows[first : first + SLICES_DEV]
                own[here, :] = rows[i * SLICES_DEV : (i + 1) * SLICES_DEV]
                edge[here, :] = packed if i < ANGLES // 2 else pltpu.roll(packed, BLOCK // 2, 1)
                own_sum[here, :] = zero
                edge_sum[here, :] = zero
        return carried

    lax.fori_loop(0, SLABS // 2, unpack, 0, unroll=UNPACK_UNROLL)
    for copy in copies:
        copy.wait()

    def tiled(value):
        return value.reshape(SIDE // 8, 8, BLOCK)

    def turned(value):
        top = jnp.concatenate([value[:SIDE, :SIDE], value[SIDE:, :SIDE]], axis=1)
        bottom = jnp.concatenate([value[:SIDE, SIDE:], value[SIDE:, SIDE:]], axis=1)
        return jnp.concatenate([top, bottom], axis=0)

    def group(step, carried):
        first = step * GROUP
        rows, inside, amount, waves, fields = [], [], [], [], []
        for k in range(GROUP):
            shift = shifts[first + k]
            rows.append(pl.ds(pl.multiple_of(owners[first + k] * SIDE, SIDE), SIDE))
            bound = jnp.where(shift >= 0, shift, shift + BLOCK)
            inside.append((lane >= bound) == (shift >= 0))
            amount.append(bound)
        for k in range(GROUP):
            chosen = jnp.where(inside[k], tiled(own[rows[k], :]), tiled(edge[rows[k], :])).reshape(SIDE, BLOCK)
            turns = pltpu.roll(chosen, lax.rem(BLOCK - amount[k], BLOCK), 1) * (1.0 / 65536.0)
            object_im, object_re = sine_and_cosine(turns)
            wave_re = probe[0] * object_re - probe[1] * object_im
            wave_im = probe[0] * object_im + probe[1] * object_re
            waves.append((wave_re, wave_im))
            fields.append(jnp.concatenate([wave_re.astype(jnp.bfloat16), wave_im.astype(jnp.bfloat16)], axis=1))
        pairs = range(GROUP // 2)
        half = [
            jnp.dot(
                jnp.concatenate(fields[2 * g : 2 * g + 2], axis=0), spread[...], preferred_element_type=jnp.float32
            ).astype(jnp.bfloat16)
            for g in pairs
        ]
        far = [jnp.dot(gather[...], turned(half[g]), preferred_element_type=jnp.float32) for g in pairs]
        resid = []
        for g in pairs:
            far_re, far_im = far[g][:SIDE], far[g][SIDE:]
            amplitude = jnp.concatenate(
                [measured[first + 2 * g].astype(jnp.float32), measured[first + 2 * g + 1].astype(jnp.float32)], axis=1
            )
            factor = 1.0 - amplitude * lax.rsqrt(far_re * far_re + far_im * far_im + 0.25)
            resid.append(
                jnp.concatenate([(far_re * factor).astype(jnp.bfloat16), (far_im * factor).astype(jnp.bfloat16)], axis=0)
            )
        back = [
            jnp.dot(spread[...], resid[g], preferred_element_type=jnp.float32).astype(jnp.bfloat16) for g in pairs
        ]
        near = [jnp.dot(turned(back[g]), gather[...], preferred_element_type=jnp.float32) for g in pairs]
        grads = []
        for k in range(GROUP):
            part = near[k // 2][(k % 2) * SIDE : (k % 2 + 1) * SIDE]
            wave_re, wave_im = waves[k]
            grads.append(pltpu.roll(part[:, SIDE:] * wave_re - part[:, :SIDE] * wave_im, amount[k], 1))
        for k in range(GROUP):
            grad = tiled(grads[k])
            own_sum[rows[k], :] = own_sum[rows[k], :] + jnp.where(inside[k], grad, 0.0).reshape(SIDE, BLOCK)
            edge_sum[rows[k], :] = edge_sum[rows[k], :] + jnp.where(inside[k], 0.0, grad).reshape(SIDE, BLOCK)
        return carried

    lax.fori_loop(0, FRAMES // GROUP, group, 0)

    def pack(chip, carried):
        for which, out in ((core, near_out), (1 - core, far_out)):
            base = pl.multiple_of((chip * 2 + which) * SLICES_DEV, SLICES_DEV)
            here = [pl.ds(base + i * SIDE, SLICES_DEV) for i in range(ANGLES)]
            rows = [own_sum[here[i], :] for i in range(ANGLES)]
            for i in range(ANGLES // 2):
                high = pltpu.roll(edge_sum[here[i + ANGLES // 2], :], BLOCK // 2, 1)
                rows.append(jnp.where(outer, edge_sum[here[i], :], high))
            out[chip] = jnp.concatenate(rows, axis=0).astype(jnp.bfloat16)
        return carried

    lax.fori_loop(0, SLABS // 2, pack, 0, unroll=UNPACK_UNROLL)


def frame_gradients(parity, owners, shifts, near_phases, far_phases, probe, measured, spread, gather):
    smem = pl.BlockSpec(memory_space=pltpu.SMEM)
    hbm = pl.BlockSpec(memory_space=pltpu.HBM)
    vmem = pl.BlockSpec(memory_space=pltpu.VMEM)
    table = pltpu.VMEM((SLABS * SLICES_DEV * ANGLES, BLOCK), jnp.float32)
    half = jax.ShapeDtypeStruct((SLABS // 2, ROWS, BLOCK), jnp.bfloat16)
    return pl.pallas_call(
        frames_kernel,
        name="frame_gradients",
        in_specs=[smem, hbm, hbm, vmem, vmem, vmem, vmem, vmem, vmem],
        out_specs=[vmem, vmem],
        out_shape=[half, half],
        scratch_shapes=[
            table, table, table, table,
            pltpu.SMEM((FRAMES,), jnp.int32), pltpu.SMEM((FRAMES,), jnp.int32), pltpu.SemaphoreType.DMA((2,)),
        ],
        compiler_params=pltpu.CompilerParams(vmem_limit_bytes=VMEM_LIMIT),
    )(parity, owners, shifts, near_phases, far_phases, probe, measured, spread, gather)


def back_kernel(shears_in, shifts_in, tiles, out_hbm, table, stack, out, gathered, shears, shifts, sems):
    copies = [
        pltpu.make_async_copy(shears_in, shears, sems.at[0]),
        pltpu.make_async_copy(shifts_in, shifts, sems.at[1]),
    ]
    for copy in copies:
        copy.start()
    copies[0].wait()
    shape = (DEPTH, BWD_FINE * ANGLES)
    shear = pick_rows([shears[i] for i in range(ANGLES)], shape, 1, ANGLES)
    beam = iota(shape, 0).astype(jnp.float32)
    centre = BLOCK * 0.5 + (beam - (DEPTH - 1) * 0.5) * shear
    fine = (iota(shape, 1) // ANGLES).astype(jnp.float32)
    for j in range(BWD_COARSE):
        table[j * DEPTH : (j + 1) * DEPTH] = bell(fine + float(FIRST + BWD_FINE * j), centre)
    copies[1].wait()
    shape = (ANGLES, BLOCK)
    shift = pick_rows([shifts[i] for i in range(ANGLES)], shape, 0, ANGLES)
    lane = iota(shape, 1)
    zero = jnp.zeros(shape, jnp.float32)
    sends = []
    for k in range(TILES):
        gathered[k] = tiles[k].astype(jnp.float32)
    for p in range(PAIRS):
        for half in range(2):
            own, margin = [], []
            for k in range(TILES):
                s = p * 2 + half
                own.append(gathered[k, pl.ds(s, ANGLES, stride=SLICES_DEV), :])
                packed = gathered[k, pl.ds(OWN_ROWS + s, ANGLES // 2, stride=SLICES_DEV), :]
                margin.append(jnp.concatenate([packed, pltpu.roll(packed, BLOCK // 2, 1)], axis=0))
            whole = []
            for k in range(TILES):
                total = own[k]
                if k > 0:
                    total = total + jnp.where(lane < HALO, margin[k - 1], 0.0)
                if k < TILES - 1:
                    total = total + jnp.where(lane >= BLOCK - HALO, margin[k + 1], 0.0)
                whole.append(total.astype(jnp.bfloat16).astype(jnp.float32))
            whole = [zero] + whole + [zero, zero]
            placed = jnp.concatenate(
                [
                    jnp.where(shift == 0, whole[k + 1], jnp.where(shift > 0, whole[k + 2], whole[k]))
                    for k in range(BLOCKS + 1)
                ],
                axis=1,
            ).astype(jnp.bfloat16)
            for r in range(BWD_FINE):
                moved = jnp.concatenate([placed[:, FIRST + r :], placed[:, : FIRST + r]], axis=1)
                stack[p, r * ANGLES : (r + 1) * ANGLES, half * WIDE : (half + 1) * WIDE] = moved
        both = jnp.dot(table[...], stack[p], preferred_element_type=jnp.float32)
        for half in range(2):
            sums = both[:, half * WIDE : (half + 1) * WIDE]
            total = sums[0:DEPTH]
            for j in range(1, BWD_COARSE):
                total = total + left(sums[j * DEPTH : (j + 1) * DEPTH], BWD_FINE * j)
            out[p * 2 + half] = total[:, : BLOCKS * BLOCK]
        part = pl.ds(p * 2, 2)
        sends.append(pltpu.make_async_copy(out.at[part], out_hbm.at[part], sems.at[2 + p]))
        sends[-1].start()
    for send in sends:
        send.wait()


def back_project(shears, shifts, tiles):
    hbm = pl.BlockSpec(memory_space=pltpu.HBM)
    return pl.pallas_call(
        back_kernel,
        name="back_project",
        in_specs=[hbm, hbm, pl.BlockSpec(memory_space=pltpu.VMEM)],
        out_specs=hbm,
        out_shape=jax.ShapeDtypeStruct((SLICES_DEV, DEPTH, BLOCKS * BLOCK), jnp.float32),
        scratch_shapes=[
            pltpu.VMEM((BWD_COARSE * DEPTH, BWD_FINE * ANGLES), jnp.bfloat16),
            pltpu.VMEM((PAIRS, BWD_FINE * ANGLES, 2 * WIDE), jnp.bfloat16),
            pltpu.VMEM((SLICES_DEV, DEPTH, BLOCKS * BLOCK), jnp.float32),
            pltpu.VMEM((TILES, ROWS, BLOCK), jnp.float32),
            pltpu.SMEM((ANGLES,), jnp.float32),
            pltpu.SMEM((ANGLES,), jnp.int32),
            pltpu.SemaphoreType.DMA((2 + PAIRS,)),
        ],
        compiler_params=pltpu.CompilerParams(vmem_limit_bytes=VMEM_LIMIT),
    )(shears, shifts, tiles)


def dft_matrices():
    index = np.arange(SIDE)
    phase = (np.outer(index, index) % SIDE) * (2.0 * np.pi / SIDE)
    cos, sin = np.cos(phase), np.sin(phase)
    spread = np.block([[cos, -sin], [sin, cos]])
    gather = np.block([[cos, sin], [-sin, cos]]) / SIDE
    return jnp.asarray(spread, jnp.bfloat16), jnp.asarray(gather, jnp.bfloat16)


def copies_of(value, count):
    return jnp.broadcast_to(value, (count, *value.shape))


def between_chips(value):
    count = lax.axis_size("slab")
    groups = [list(range(core, count, 2)) for core in range(2)]
    return lax.all_to_all(value, "slab", 0, 0, tiled=True, axis_index_groups=groups)


def between_cores(value):
    return lax.ppermute(value, "slab", [(i, i ^ 1) for i in range(lax.axis_size("slab"))])


def body(volume, shears, tile_shift, illumination, measured, frame_owner, frame_shift):
    spread, gather = dft_matrices()
    shifts = tile_shift.reshape(ANGLES)
    parity = (lax.axis_index("slab") % 2).astype(jnp.int32).reshape(1)
    partials = project(shears, shifts, volume)
    landed = lax.all_to_all(partials, "tile", 0, 0, tiled=True)
    phase = jnp.sum(landed.astype(jnp.int32), axis=0)
    phase = (((phase + 32768) & 65535) - 32768).astype(jnp.int16)
    near_phases = between_chips(copies_of(phase, SLABS // 2))
    far_phases = between_cores(near_phases)
    near_grads, far_grads = frame_gradients(
        parity, frame_owner.reshape(FRAMES), frame_shift, near_phases, far_phases, illumination, measured, spread, gather
    )
    grads = near_grads.astype(jnp.float32) + between_cores(far_grads).astype(jnp.float32)
    landed = between_chips(grads.astype(jnp.bfloat16)).astype(jnp.float32)
    grad = landed[0]
    for i in range(1, SLABS // 2):
        grad = grad + landed[i]
    tiles = lax.all_to_all(copies_of(grad.astype(jnp.bfloat16), TILES), "tile", 0, 0, tiled=True)
    return back_project(shears, shifts, tiles)


def solution(mesh):
    in_specs = (
        P("slab", "tile", None),
        P(),
        P(None, "tile"),
        P(),
        P(("slab", "tile"), None, None),
        P(("slab", "tile"), None),
        P(("slab", "tile")),
    )
    out_specs = P("slab", "tile", None)
    return jax.shard_map(body, mesh=mesh, in_specs=in_specs, out_specs=out_specs, check_vma=False)
```

```python
import math

import jax
import jax.numpy as jnp
import numpy as np
from jax import lax
from jax.experimental import pallas as pl
from jax.experimental.pallas import tpu as pltpu
from jax.sharding import PartitionSpec as P

SIDE = 128
BLOCK = 128
HALO = 32
ANGLES = 16
DEPTH = 64
SLICES_DEV = 8
BLOCKS = 8
SLABS = 16
TILES = 8
FRAMES = 32
FIRST = 38
WIDE = 9 * BLOCK
FWD_FINE, FWD_COARSE = 4, 14
BWD_FINE, BWD_COARSE = 14, 4
OWN_ROWS, EDGE_ROWS = ANGLES * SLICES_DEV, ANGLES // 2 * SLICES_DEV
PAIRS = SLICES_DEV // 2
ROWS = OWN_ROWS + EDGE_ROWS
GROUP = 32
MERGED = 4
UNPACK_UNROLL = 2
VMEM_LIMIT = 40 * 1024 * 1024
ALL_VMEM = 60 * 1024 * 1024

SIN_TERMS = (3.14159264, -5.16771008, 2.55007752, -0.598291286, 0.0776576603)
COS_TERMS = (0.999999953, -4.93479283, 4.05841135, -1.33187657, 0.219689611)


def iota(shape, dim):
    return lax.broadcasted_iota(jnp.int32, shape, dim)


def poly(terms, t):
    total = jnp.full_like(t, terms[-1])
    for term in reversed(terms[:-1]):
        total = total * t + term
    return total


def sine_and_cosine(turns):
    t = turns * turns
    half_sin = turns * poly(SIN_TERMS, t)
    half_cos = poly(COS_TERMS, t)
    return (2.0 * half_sin * half_cos, 1.0 - 2.0 * half_sin * half_sin)


def pick_rows(values, shape, dim, period):
    index = iota(shape, dim) % period
    total = jnp.zeros(shape, values[0].dtype)
    for i, value in enumerate(values):
        total = jnp.where(index == i, value, total)
    return total


def bell(offset, centre):
    spread = offset - centre
    return jnp.exp(-0.5 * spread * spread).astype(jnp.bfloat16)


def left(value, steps):
    return pltpu.roll(value, value.shape[1] - steps, 1)


def project_kernel(shears_in, shifts_in, volume_in, out, table, stack, volume, gathered, shears, shifts, sems):
    copies = [
        pltpu.make_async_copy(shears_in, shears, sems.at[0]),
        pltpu.make_async_copy(shifts_in, shifts, sems.at[1]),
    ]
    for p in range(PAIRS):
        part = pl.ds(p * 2, 2)
        copies.append(pltpu.make_async_copy(volume_in.at[part], volume.at[part], sems.at[2 + p]))
    for copy in copies:
        copy.start()
    copies[0].wait()
    shape = (ANGLES, FWD_FINE * DEPTH)
    shear = pick_rows([shears[i] for i in range(ANGLES)], shape, 0, ANGLES)
    lane = iota(shape, 1)
    beam = (lane % DEPTH).astype(jnp.float32)
    centre = BLOCK * 0.5 + (beam - (DEPTH - 1) * 0.5) * shear
    fine = (lane // DEPTH).astype(jnp.float32)
    for j in range(FWD_COARSE):
        table[j * ANGLES : (j + 1) * ANGLES] = bell(fine + float(FIRST + FWD_FINE * j), centre)
    copies[1].wait()
    shape = (ANGLES, BLOCK)
    shift = pick_rows([shifts[i] for i in range(ANGLES)], shape, 0, ANGLES)
    lane = iota((8, BLOCK), 1)
    full_lane = iota(shape, 1)
    outer = (lane < HALO) | (lane >= BLOCK - HALO)
    zero = jnp.zeros(shape, jnp.float32)
    def build(p):
        copies[2 + p].wait()
        for half in range(2):
            rows = jnp.concatenate(
                [volume[p * 2 + half], jnp.zeros((DEPTH, WIDE - BLOCKS * BLOCK), jnp.float32)], axis=1
            ).astype(jnp.bfloat16)
            for r in range(FWD_FINE):
                moved = rows if r == 0 else jnp.concatenate([rows[:, WIDE - r :], rows[:, : WIDE - r]], axis=1)
                stack[p, r * DEPTH : (r + 1) * DEPTH, half * WIDE : (half + 1) * WIDE] = moved

    def finish(p):
        fixed = []
        for n in range(WIDE // BLOCK):
            sums = jnp.dot(table[...], stack[p, :, n * 2 * BLOCK : (n + 1) * 2 * BLOCK], preferred_element_type=jnp.float32)
            for b in range(2):
                rolled = [
                    pltpu.roll(sums[j * ANGLES : (j + 1) * ANGLES, b * BLOCK : (b + 1) * BLOCK], FIRST + FWD_FINE * j, 1)
                    for j in range(FWD_COARSE)
                ]
                if (2 * n + b) % (BLOCKS + 1) == 0:
                    before = [zero] * FWD_COARSE
                total = jnp.where(full_lane >= FIRST, rolled[0], before[0])
                for j in range(1, FWD_COARSE):
                    total = total + jnp.where(full_lane >= FIRST + FWD_FINE * j, rolled[j], before[j])
                before = rolled
                turns = total * (1.0 / (2.0 * math.pi))
                turns = turns - jnp.floor(turns + 0.5)
                fixed.append(jnp.minimum(jnp.floor(turns * 65536.0 + 0.5), 32767.0))
        for half in range(2):
            block = [zero] + fixed[half * (BLOCKS + 1) : (half + 1) * (BLOCKS + 1)] + [zero]
            placed = []
            for k in range(BLOCKS):
                here = jnp.where(shift == 0, block[k + 1], jnp.where(shift > 0, block[k], block[k + 2]))
                placed.append(here)
            around = [zero] + placed + [zero]
            s = p * 2 + half
            for k in range(BLOCKS):
                gathered[k, pl.ds(s, ANGLES, stride=SLICES_DEV), :] = placed[k]
                after, before = around[k + 2], around[k]
                low = jnp.where(lane < HALO, after[:8], before[:8])
                high = jnp.where(lane < HALO, after[8:], before[8:])
                edge = jnp.where(outer, low, pltpu.roll(high, BLOCK // 2, 1))
                gathered[k, pl.ds(OWN_ROWS + s, ANGLES // 2, stride=SLICES_DEV), :] = edge

    build(0)
    for p in range(PAIRS):
        if p + 1 < PAIRS:
            build(p + 1)
        finish(p)
    for k in range(BLOCKS):
        out[k] = gathered[k].astype(jnp.int32).astype(jnp.int16)


def project(shears, shifts, volume):
    hbm = pl.BlockSpec(memory_space=pltpu.HBM)
    return pl.pallas_call(
        project_kernel,
        name="project",
        in_specs=[hbm, hbm, hbm],
        out_specs=pl.BlockSpec(memory_space=pltpu.VMEM),
        out_shape=jax.ShapeDtypeStruct((TILES, ROWS, BLOCK), jnp.int16),
        scratch_shapes=[
            pltpu.VMEM((FWD_COARSE * ANGLES, FWD_FINE * DEPTH), jnp.bfloat16),
            pltpu.VMEM((PAIRS, FWD_FINE * DEPTH, 2 * WIDE), jnp.bfloat16),
            pltpu.VMEM((SLICES_DEV, DEPTH, BLOCKS * BLOCK), jnp.float32),
            pltpu.VMEM((BLOCKS, ROWS, BLOCK), jnp.float32),
            pltpu.SMEM((ANGLES,), jnp.float32),
            pltpu.SMEM((ANGLES,), jnp.int32),
            pltpu.SemaphoreType.DMA((2 + PAIRS,)),
        ],
        compiler_params=pltpu.CompilerParams(vmem_limit_bytes=ALL_VMEM),
    )(shears, shifts, volume)


def frames_kernel(
    parity, owners_in, shifts_in, near_phases, far_phases, probe, measured, spread, gather,
    near_out, far_out, own, edge, own_sum, edge_sum, owners, shifts, sems,
):
    copies = [
        pltpu.make_async_copy(owners_in, owners, sems.at[0]),
        pltpu.make_async_copy(shifts_in, shifts, sems.at[1]),
    ]
    for copy in copies:
        copy.start()
    lane = iota((8, BLOCK), 1)
    outer = (lane < HALO) | (lane >= BLOCK - HALO)
    core = parity[0]

    def unpack(chip, carried):
        for which, phases in ((core, near_phases), (1 - core, far_phases)):
            base = pl.multiple_of((chip * 2 + which) * SLICES_DEV, SLICES_DEV)
            rows = phases[chip].astype(jnp.int32).astype(jnp.float32) * (1.0 / 65536.0)
            zero = jnp.zeros((SLICES_DEV, BLOCK), jnp.float32)
            for i in range(ANGLES):
                here = pl.ds(base + i * SIDE, SLICES_DEV)
                first = OWN_ROWS + i % (ANGLES // 2) * SLICES_DEV
                packed = rows[first : first + SLICES_DEV]
                own[here, :] = rows[i * SLICES_DEV : (i + 1) * SLICES_DEV]
                edge[here, :] = packed if i < ANGLES // 2 else pltpu.roll(packed, BLOCK // 2, 1)
                own_sum[here, :] = zero
                edge_sum[here, :] = zero
        return carried

    lax.fori_loop(0, SLABS // 2, unpack, 0, unroll=UNPACK_UNROLL)
    for copy in copies:
        copy.wait()

    def tiled(value):
        return value.reshape(SIDE // 8, 8, BLOCK)

    def turned(value):
        top = jnp.concatenate([value[:SIDE, :SIDE], value[SIDE:, :SIDE]], axis=1)
        bottom = jnp.concatenate([value[:SIDE, SIDE:], value[SIDE:, SIDE:]], axis=1)
        return jnp.concatenate([top, bottom], axis=0)

    def across(values, matrix, per_pair):
        results = []
        for first in range(0, len(values), MERGED * per_pair):
            rows = jnp.concatenate(values[first : first + MERGED * per_pair], axis=0)
            product = jnp.dot(rows, matrix[...], preferred_element_type=jnp.float32)
            results += [product[g * 2 * SIDE : (g + 1) * 2 * SIDE] for g in range(MERGED)]
        return results

    def group(step, carried):
        first = step * GROUP
        rows, inside, amount, waves, fields = [], [], [], [], []
        for k in range(GROUP):
            shift = shifts[first + k]
            rows.append(pl.ds(pl.multiple_of(owners[first + k] * SIDE, SIDE), SIDE))
            bound = jnp.where(shift >= 0, shift, shift + BLOCK)
            inside.append((lane >= bound) == (shift >= 0))
            amount.append(bound)
        for k in range(GROUP):
            chosen = jnp.where(inside[k], tiled(own[rows[k], :]), tiled(edge[rows[k], :])).reshape(SIDE, BLOCK)
            turns = pltpu.roll(chosen, lax.rem(BLOCK - amount[k], BLOCK), 1)
            object_im, object_re = sine_and_cosine(turns)
            wave_re = probe[0] * object_re - probe[1] * object_im
            wave_im = probe[0] * object_im + probe[1] * object_re
            waves.append((wave_re, wave_im))
            fields.append(jnp.concatenate([wave_re.astype(jnp.bfloat16), wave_im.astype(jnp.bfloat16)], axis=1))
        pairs = range(GROUP // 2)
        half = across(fields, spread, 2)
        far = [jnp.dot(gather[...], turned(half[g].astype(jnp.bfloat16)), preferred_element_type=jnp.float32) for g in pairs]
        resid = []
        for g in pairs:
            far_re, far_im = far[g][:SIDE], far[g][SIDE:]
            amplitude = jnp.concatenate(
                [measured[first + 2 * g].astype(jnp.float32), measured[first + 2 * g + 1].astype(jnp.float32)], axis=1
            )
            factor = 1.0 - amplitude * lax.rsqrt(far_re * far_re + far_im * far_im + 0.25)
            resid.append(
                jnp.concatenate([(far_re * factor).astype(jnp.bfloat16), (far_im * factor).astype(jnp.bfloat16)], axis=0)
            )
        back = [
            jnp.dot(spread[...], resid[g], preferred_element_type=jnp.float32) for g in pairs
        ]
        near = across([turned(back[g].astype(jnp.bfloat16)) for g in pairs], gather, 1)
        grads = []
        for k in range(GROUP):
            part = near[k // 2][(k % 2) * SIDE : (k % 2 + 1) * SIDE]
            wave_re, wave_im = waves[k]
            grads.append(pltpu.roll(part[:, SIDE:] * wave_re - part[:, :SIDE] * wave_im, amount[k], 1))
        for k in range(GROUP):
            grad = tiled(grads[k])
            own_sum[rows[k], :] = own_sum[rows[k], :] + jnp.where(inside[k], grad, 0.0).reshape(SIDE, BLOCK)
            edge_sum[rows[k], :] = edge_sum[rows[k], :] + jnp.where(inside[k], 0.0, grad).reshape(SIDE, BLOCK)
        return carried

    lax.fori_loop(0, FRAMES // GROUP, group, 0)

    def pack(chip, carried):
        for which, out in ((core, near_out), (1 - core, far_out)):
            base = pl.multiple_of((chip * 2 + which) * SLICES_DEV, SLICES_DEV)
            here = [pl.ds(base + i * SIDE, SLICES_DEV) for i in range(ANGLES)]
            rows = [own_sum[here[i], :] for i in range(ANGLES)]
            for i in range(ANGLES // 2):
                high = pltpu.roll(edge_sum[here[i + ANGLES // 2], :], BLOCK // 2, 1)
                rows.append(jnp.where(outer, edge_sum[here[i], :], high))
            out[chip] = jnp.concatenate(rows, axis=0).astype(jnp.bfloat16)
        return carried

    lax.fori_loop(0, SLABS // 2, pack, 0, unroll=UNPACK_UNROLL)


def frame_gradients(parity, owners, shifts, near_phases, far_phases, probe, measured, spread, gather):
    smem = pl.BlockSpec(memory_space=pltpu.SMEM)
    hbm = pl.BlockSpec(memory_space=pltpu.HBM)
    vmem = pl.BlockSpec(memory_space=pltpu.VMEM)
    table = pltpu.VMEM((SLABS * SLICES_DEV * ANGLES, BLOCK), jnp.float32)
    half = jax.ShapeDtypeStruct((SLABS // 2, ROWS, BLOCK), jnp.bfloat16)
    return pl.pallas_call(
        frames_kernel,
        name="frame_gradients",
        in_specs=[smem, hbm, hbm, vmem, vmem, vmem, vmem, vmem, vmem],
        out_specs=[vmem, vmem],
        out_shape=[half, half],
        scratch_shapes=[
            table, table, table, table,
            pltpu.SMEM((FRAMES,), jnp.int32), pltpu.SMEM((FRAMES,), jnp.int32), pltpu.SemaphoreType.DMA((2,)),
        ],
        compiler_params=pltpu.CompilerParams(vmem_limit_bytes=VMEM_LIMIT),
    )(parity, owners, shifts, near_phases, far_phases, probe, measured, spread, gather)


def back_kernel(shears_in, shifts_in, tiles, out_hbm, table, stack, out, gathered, shears, shifts, sems):
    copies = [
        pltpu.make_async_copy(shears_in, shears, sems.at[0]),
        pltpu.make_async_copy(shifts_in, shifts, sems.at[1]),
    ]
    for copy in copies:
        copy.start()
    copies[0].wait()
    shape = (DEPTH, BWD_FINE * ANGLES)
    shear = pick_rows([shears[i] for i in range(ANGLES)], shape, 1, ANGLES)
    beam = iota(shape, 0).astype(jnp.float32)
    centre = BLOCK * 0.5 + (beam - (DEPTH - 1) * 0.5) * shear
    fine = (iota(shape, 1) // ANGLES).astype(jnp.float32)
    for j in range(BWD_COARSE):
        table[j * DEPTH : (j + 1) * DEPTH] = bell(fine + float(FIRST + BWD_FINE * j), centre)
    copies[1].wait()
    shape = (ANGLES, BLOCK)
    shift = pick_rows([shifts[i] for i in range(ANGLES)], shape, 0, ANGLES)
    lane = iota(shape, 1)
    zero = jnp.zeros(shape, jnp.float32)
    sends = []
    for k in range(TILES):
        gathered[k] = tiles[k].astype(jnp.float32)
    def build(p):
        for half in range(2):
            own, margin = [], []
            for k in range(TILES):
                s = p * 2 + half
                own.append(gathered[k, pl.ds(s, ANGLES, stride=SLICES_DEV), :])
                packed = gathered[k, pl.ds(OWN_ROWS + s, ANGLES // 2, stride=SLICES_DEV), :]
                margin.append(jnp.concatenate([packed, pltpu.roll(packed, BLOCK // 2, 1)], axis=0))
            whole = []
            for k in range(TILES):
                total = own[k]
                if k > 0:
                    total = total + jnp.where(lane < HALO, margin[k - 1], 0.0)
                if k < TILES - 1:
                    total = total + jnp.where(lane >= BLOCK - HALO, margin[k + 1], 0.0)
                whole.append(total.astype(jnp.bfloat16).astype(jnp.float32))
            whole = [zero] + whole + [zero, zero]
            placed = jnp.concatenate(
                [
                    jnp.where(shift == 0, whole[k + 1], jnp.where(shift > 0, whole[k + 2], whole[k]))
                    for k in range(BLOCKS + 1)
                ],
                axis=1,
            ).astype(jnp.bfloat16)
            for r in range(BWD_FINE):
                moved = jnp.concatenate([placed[:, FIRST + r :], placed[:, : FIRST + r]], axis=1)
                stack[p, r * ANGLES : (r + 1) * ANGLES, half * WIDE : (half + 1) * WIDE] = moved

    def finish(p):
        both = jnp.dot(table[...], stack[p], preferred_element_type=jnp.float32)
        for half in range(2):
            sums = both[:, half * WIDE : (half + 1) * WIDE]
            total = sums[0:DEPTH]
            for j in range(1, BWD_COARSE):
                total = total + left(sums[j * DEPTH : (j + 1) * DEPTH], BWD_FINE * j)
            out[p * 2 + half] = total[:, : BLOCKS * BLOCK]
        part = pl.ds(p * 2, 2)
        sends.append(pltpu.make_async_copy(out.at[part], out_hbm.at[part], sems.at[2 + p]))
        sends[-1].start()

    for p in range(PAIRS):
        build(p)
    for p in range(PAIRS):
        finish(p)
    for send in sends:
        send.wait()


def back_project(shears, shifts, tiles):
    hbm = pl.BlockSpec(memory_space=pltpu.HBM)
    return pl.pallas_call(
        back_kernel,
        name="back_project",
        in_specs=[hbm, hbm, pl.BlockSpec(memory_space=pltpu.VMEM)],
        out_specs=hbm,
        out_shape=jax.ShapeDtypeStruct((SLICES_DEV, DEPTH, BLOCKS * BLOCK), jnp.float32),
        scratch_shapes=[
            pltpu.VMEM((BWD_COARSE * DEPTH, BWD_FINE * ANGLES), jnp.bfloat16),
            pltpu.VMEM((PAIRS, BWD_FINE * ANGLES, 2 * WIDE), jnp.bfloat16),
            pltpu.VMEM((SLICES_DEV, DEPTH, BLOCKS * BLOCK), jnp.float32),
            pltpu.VMEM((TILES, ROWS, BLOCK), jnp.float32),
            pltpu.SMEM((ANGLES,), jnp.float32),
            pltpu.SMEM((ANGLES,), jnp.int32),
            pltpu.SemaphoreType.DMA((2 + PAIRS,)),
        ],
        compiler_params=pltpu.CompilerParams(vmem_limit_bytes=VMEM_LIMIT),
    )(shears, shifts, tiles)


def dft_matrices():
    index = np.arange(SIDE)
    phase = (np.outer(index, index) % SIDE) * (2.0 * np.pi / SIDE)
    cos, sin = np.cos(phase), np.sin(phase)
    spread = np.block([[cos, -sin], [sin, cos]])
    gather = np.block([[cos, sin], [-sin, cos]]) / SIDE
    return jnp.asarray(spread, jnp.bfloat16), jnp.asarray(gather, jnp.bfloat16)


def copies_of(value, count):
    return jnp.broadcast_to(value, (count, *value.shape))


def between_chips(value):
    count = lax.axis_size("slab")
    groups = [list(range(core, count, 2)) for core in range(2)]
    return lax.all_to_all(value, "slab", 0, 0, tiled=True, axis_index_groups=groups)


def between_cores(value):
    return lax.ppermute(value, "slab", [(i, i ^ 1) for i in range(lax.axis_size("slab"))])


def body(volume, shears, tile_shift, illumination, measured, frame_owner, frame_shift):
    spread, gather = dft_matrices()
    shifts = tile_shift.reshape(ANGLES)
    parity = (lax.axis_index("slab") % 2).astype(jnp.int32).reshape(1)
    partials = project(shears, shifts, volume)
    landed = lax.all_to_all(partials, "tile", 0, 0, tiled=True)
    phase = jnp.sum(landed.astype(jnp.int32), axis=0)
    phase = (((phase + 32768) & 65535) - 32768).astype(jnp.int16)
    near_phases = between_chips(copies_of(phase, SLABS // 2))
    far_phases = between_cores(near_phases)
    near_grads, far_grads = frame_gradients(
        parity, frame_owner.reshape(FRAMES), frame_shift, near_phases, far_phases, illumination, measured, spread, gather
    )
    grads = near_grads.astype(jnp.float32) + between_cores(far_grads).astype(jnp.float32)
    landed = between_chips(grads.astype(jnp.bfloat16)).astype(jnp.float32)
    grad = landed[0]
    for i in range(1, SLABS // 2):
        grad = grad + landed[i]
    tiles = lax.all_to_all(copies_of(grad.astype(jnp.bfloat16), TILES), "tile", 0, 0, tiled=True)
    return back_project(shears, shifts, tiles)


def solution(mesh):
    in_specs = (
        P("slab", "tile", None),
        P(),
        P(None, "tile"),
        P(),
        P(("slab", "tile"), None, None),
        P(("slab", "tile"), None),
        P(("slab", "tile")),
    )
    out_specs = P("slab", "tile", None)
    return jax.shard_map(body, mesh=mesh, in_specs=in_specs, out_specs=out_specs, check_vma=False)
```

```python
import math

import jax
import jax.numpy as jnp
import numpy as np
from jax import lax
from jax.experimental import pallas as pl
from jax.experimental.pallas import tpu as pltpu
from jax.sharding import PartitionSpec as P

SIDE = 128
BLOCK = 128
HALO = 32
ANGLES = 16
DEPTH = 64
SLICES_DEV = 8
BLOCKS = 8
SLABS = 16
TILES = 8
FRAMES = 32
FIRST = 38
WIDE = 9 * BLOCK
FWD_FINE, FWD_COARSE = 4, 14
BWD_FINE, BWD_COARSE = 14, 4
OWN_ROWS, EDGE_ROWS = ANGLES * SLICES_DEV, ANGLES // 2 * SLICES_DEV
PAIRS = SLICES_DEV // 2
ROWS = OWN_ROWS + EDGE_ROWS
GROUP = 32
MERGED = 4
UNPACK_UNROLL = 2
VMEM_LIMIT = 40 * 1024 * 1024
ALL_VMEM = 60 * 1024 * 1024

SIN_TERMS = (3.14159264, -5.16771008, 2.55007752, -0.598291286, 0.0776576603)
COS_TERMS = (0.999999953, -4.93479283, 4.05841135, -1.33187657, 0.219689611)


def iota(shape, dim):
    return lax.broadcasted_iota(jnp.int32, shape, dim)


def poly(terms, t):
    total = jnp.full_like(t, terms[-1])
    for term in reversed(terms[:-1]):
        total = total * t + term
    return total


def sine_and_cosine(turns):
    t = turns * turns
    half_sin = turns * poly(SIN_TERMS, t)
    half_cos = poly(COS_TERMS, t)
    return (2.0 * half_sin * half_cos, 1.0 - 2.0 * half_sin * half_sin)


def pick_rows(values, shape, dim, period):
    index = iota(shape, dim) % period
    total = jnp.zeros(shape, values[0].dtype)
    for i, value in enumerate(values):
        total = jnp.where(index == i, value, total)
    return total


def bell(offset, centre):
    spread = offset - centre
    return jnp.exp(-0.5 * spread * spread).astype(jnp.bfloat16)


def left(value, steps):
    return pltpu.roll(value, value.shape[1] - steps, 1)


def project_kernel(shears_in, shifts_in, volume_in, out, table, stack, volume, gathered, shears, shifts, sems):
    copies = [
        pltpu.make_async_copy(shears_in, shears, sems.at[0]),
        pltpu.make_async_copy(shifts_in, shifts, sems.at[1]),
    ]
    for p in range(PAIRS):
        part = pl.ds(p * 2, 2)
        copies.append(pltpu.make_async_copy(volume_in.at[part], volume.at[part], sems.at[2 + p]))
    for copy in copies:
        copy.start()
    copies[0].wait()
    shape = (ANGLES, FWD_FINE * DEPTH)
    shear = pick_rows([shears[i] for i in range(ANGLES)], shape, 0, ANGLES)
    lane = iota(shape, 1)
    beam = (lane % DEPTH).astype(jnp.float32)
    centre = BLOCK * 0.5 + (beam - (DEPTH - 1) * 0.5) * shear
    fine = (lane // DEPTH).astype(jnp.float32)
    for j in range(FWD_COARSE):
        table[j * ANGLES : (j + 1) * ANGLES] = bell(fine + float(FIRST + FWD_FINE * j), centre)
    copies[1].wait()
    shape = (ANGLES, BLOCK)
    shift = pick_rows([shifts[i] for i in range(ANGLES)], shape, 0, ANGLES)
    lane = iota((8, BLOCK), 1)
    full_lane = iota(shape, 1)
    outer = (lane < HALO) | (lane >= BLOCK - HALO)
    zero = jnp.zeros(shape, jnp.float32)
    def build(p):
        copies[2 + p].wait()
        for half in range(2):
            rows = jnp.concatenate(
                [volume[p * 2 + half], jnp.zeros((DEPTH, WIDE - BLOCKS * BLOCK), jnp.float32)], axis=1
            ).astype(jnp.bfloat16)
            for r in range(FWD_FINE):
                moved = rows if r == 0 else jnp.concatenate([rows[:, WIDE - r :], rows[:, : WIDE - r]], axis=1)
                stack[p, r * DEPTH : (r + 1) * DEPTH, half * WIDE : (half + 1) * WIDE] = moved

    def finish(p):
        fixed = []
        for n in range(WIDE // BLOCK):
            sums = jnp.dot(table[...], stack[p, :, n * 2 * BLOCK : (n + 1) * 2 * BLOCK], preferred_element_type=jnp.float32)
            for b in range(2):
                rolled = [
                    pltpu.roll(sums[j * ANGLES : (j + 1) * ANGLES, b * BLOCK : (b + 1) * BLOCK], FIRST + FWD_FINE * j, 1)
                    for j in range(FWD_COARSE)
                ]
                if (2 * n + b) % (BLOCKS + 1) == 0:
                    before = [zero] * FWD_COARSE
                total = jnp.where(full_lane >= FIRST, rolled[0], before[0])
                for j in range(1, FWD_COARSE):
                    total = total + jnp.where(full_lane >= FIRST + FWD_FINE * j, rolled[j], before[j])
                before = rolled
                turns = total * (1.0 / (2.0 * math.pi))
                turns = turns - jnp.floor(turns + 0.5)
                fixed.append(jnp.minimum(jnp.floor(turns * 65536.0 + 0.5), 32767.0))
        for half in range(2):
            block = [zero] + fixed[half * (BLOCKS + 1) : (half + 1) * (BLOCKS + 1)] + [zero]
            placed = []
            for k in range(BLOCKS):
                here = jnp.where(shift == 0, block[k + 1], jnp.where(shift > 0, block[k], block[k + 2]))
                placed.append(here)
            around = [zero] + placed + [zero]
            s = p * 2 + half
            for k in range(BLOCKS):
                gathered[k, pl.ds(s, ANGLES, stride=SLICES_DEV), :] = placed[k]
                after, before = around[k + 2], around[k]
                low = jnp.where(lane < HALO, after[:8], before[:8])
                high = jnp.where(lane < HALO, after[8:], before[8:])
                edge = jnp.where(outer, low, pltpu.roll(high, BLOCK // 2, 1))
                gathered[k, pl.ds(OWN_ROWS + s, ANGLES // 2, stride=SLICES_DEV), :] = edge

    build(0)
    for p in range(PAIRS):
        if p + 1 < PAIRS:
            build(p + 1)
        finish(p)
    for k in range(BLOCKS):
        out[k] = gathered[k].astype(jnp.int32).astype(jnp.int16)


def project(shears, shifts, volume):
    hbm = pl.BlockSpec(memory_space=pltpu.HBM)
    return pl.pallas_call(
        project_kernel,
        name="project",
        in_specs=[hbm, hbm, hbm],
        out_specs=pl.BlockSpec(memory_space=pltpu.VMEM),
        out_shape=jax.ShapeDtypeStruct((TILES, ROWS, BLOCK), jnp.int16),
        scratch_shapes=[
            pltpu.VMEM((FWD_COARSE * ANGLES, FWD_FINE * DEPTH), jnp.bfloat16),
            pltpu.VMEM((PAIRS, FWD_FINE * DEPTH, 2 * WIDE), jnp.bfloat16),
            pltpu.VMEM((SLICES_DEV, DEPTH, BLOCKS * BLOCK), jnp.float32),
            pltpu.VMEM((BLOCKS, ROWS, BLOCK), jnp.float32),
            pltpu.SMEM((ANGLES,), jnp.float32),
            pltpu.SMEM((ANGLES,), jnp.int32),
            pltpu.SemaphoreType.DMA((2 + PAIRS,)),
        ],
        compiler_params=pltpu.CompilerParams(vmem_limit_bytes=ALL_VMEM),
    )(shears, shifts, volume)


def frames_kernel(
    parity, owners_in, shifts_in, near_phases, far_phases, probe, measured, spread, gather,
    near_out, far_out, own, edge, own_sum, edge_sum, owners, shifts, sems,
):
    copies = [
        pltpu.make_async_copy(owners_in, owners, sems.at[0]),
        pltpu.make_async_copy(shifts_in, shifts, sems.at[1]),
    ]
    for copy in copies:
        copy.start()
    lane = iota((8, BLOCK), 1)
    outer = (lane < HALO) | (lane >= BLOCK - HALO)
    core = parity[0]

    def unpack(chip, carried):
        for which, phases in ((core, near_phases), (1 - core, far_phases)):
            base = pl.multiple_of((chip * 2 + which) * SLICES_DEV, SLICES_DEV)
            rows = phases[chip].astype(jnp.int32).astype(jnp.float32) * (1.0 / 65536.0)
            zero = jnp.zeros((SLICES_DEV, BLOCK), jnp.float32)
            for i in range(ANGLES):
                here = pl.ds(base + i * SIDE, SLICES_DEV)
                first = OWN_ROWS + i % (ANGLES // 2) * SLICES_DEV
                packed = rows[first : first + SLICES_DEV]
                own[here, :] = rows[i * SLICES_DEV : (i + 1) * SLICES_DEV]
                edge[here, :] = packed if i < ANGLES // 2 else pltpu.roll(packed, BLOCK // 2, 1)
                own_sum[here, :] = zero
                edge_sum[here, :] = zero
        return carried

    lax.fori_loop(0, SLABS // 2, unpack, 0, unroll=UNPACK_UNROLL)
    for copy in copies:
        copy.wait()

    def tiled(value):
        return value.reshape(SIDE // 8, 8, BLOCK)

    def turned(value):
        top = jnp.concatenate([value[:SIDE, :SIDE], value[SIDE:, :SIDE]], axis=1)
        bottom = jnp.concatenate([value[:SIDE, SIDE:], value[SIDE:, SIDE:]], axis=1)
        return jnp.concatenate([top, bottom], axis=0)

    def across(values, matrix, per_pair):
        results = []
        for first in range(0, len(values), MERGED * per_pair):
            rows = jnp.concatenate(values[first : first + MERGED * per_pair], axis=0)
            product = jnp.dot(rows, matrix[...], preferred_element_type=jnp.float32)
            results += [product[g * 2 * SIDE : (g + 1) * 2 * SIDE] for g in range(MERGED)]
        return results

    def group(step, carried):
        first = step * GROUP
        rows, inside, amount, waves, fields = [], [], [], [], []
        for k in range(GROUP):
            shift = shifts[first + k]
            rows.append(pl.ds(pl.multiple_of(owners[first + k] * SIDE, SIDE), SIDE))
            bound = jnp.where(shift >= 0, shift, shift + BLOCK)
            inside.append((lane >= bound) == (shift >= 0))
            amount.append(bound)
        for k in range(GROUP):
            chosen = jnp.where(inside[k], tiled(own[rows[k], :]), tiled(edge[rows[k], :])).reshape(SIDE, BLOCK)
            turns = pltpu.roll(chosen, lax.rem(BLOCK - amount[k], BLOCK), 1)
            object_im, object_re = sine_and_cosine(turns)
            wave_re = probe[0] * object_re - probe[1] * object_im
            wave_im = probe[0] * object_im + probe[1] * object_re
            waves.append((wave_re, wave_im))
            fields.append(jnp.concatenate([wave_re.astype(jnp.bfloat16), wave_im.astype(jnp.bfloat16)], axis=1))
        pairs = range(GROUP // 2)
        half = across(fields, spread, 2)
        far = [jnp.dot(gather[...], turned(half[g].astype(jnp.bfloat16)), preferred_element_type=jnp.float32) for g in pairs]
        resid = []
        for g in pairs:
            far_re, far_im = far[g][:SIDE], far[g][SIDE:]
            amplitude = jnp.concatenate(
                [measured[first + 2 * g].astype(jnp.float32), measured[first + 2 * g + 1].astype(jnp.float32)], axis=1
            )
            factor = amplitude * lax.rsqrt(far_re * far_re + far_im * far_im + 0.25)
            resid.append(
                jnp.concatenate([(far_re * factor).astype(jnp.bfloat16), (far_im * factor).astype(jnp.bfloat16)], axis=0)
            )
        back = [
            jnp.dot(spread[...], resid[g], preferred_element_type=jnp.float32) for g in pairs
        ]
        near = across([turned(back[g].astype(jnp.bfloat16)) for g in pairs], gather, 1)
        grads = []
        for k in range(GROUP):
            part = near[k // 2][(k % 2) * SIDE : (k % 2 + 1) * SIDE]
            wave_re, wave_im = waves[k]
            grads.append(pltpu.roll(part[:, :SIDE] * wave_im - part[:, SIDE:] * wave_re, amount[k], 1))
        for k in range(GROUP):
            grad = tiled(grads[k])
            own_sum[rows[k], :] = own_sum[rows[k], :] + jnp.where(inside[k], grad, 0.0).reshape(SIDE, BLOCK)
            edge_sum[rows[k], :] = edge_sum[rows[k], :] + jnp.where(inside[k], 0.0, grad).reshape(SIDE, BLOCK)
        return carried

    lax.fori_loop(0, FRAMES // GROUP, group, 0)

    def pack(chip, carried):
        for which, out in ((core, near_out), (1 - core, far_out)):
            base = pl.multiple_of((chip * 2 + which) * SLICES_DEV, SLICES_DEV)
            here = [pl.ds(base + i * SIDE, SLICES_DEV) for i in range(ANGLES)]
            rows = [own_sum[here[i], :] for i in range(ANGLES)]
            for i in range(ANGLES // 2):
                high = pltpu.roll(edge_sum[here[i + ANGLES // 2], :], BLOCK // 2, 1)
                rows.append(jnp.where(outer, edge_sum[here[i], :], high))
            out[chip] = jnp.concatenate(rows, axis=0).astype(jnp.bfloat16)
        return carried

    lax.fori_loop(0, SLABS // 2, pack, 0, unroll=UNPACK_UNROLL)


def frame_gradients(parity, owners, shifts, near_phases, far_phases, probe, measured, spread, gather):
    smem = pl.BlockSpec(memory_space=pltpu.SMEM)
    hbm = pl.BlockSpec(memory_space=pltpu.HBM)
    vmem = pl.BlockSpec(memory_space=pltpu.VMEM)
    table = pltpu.VMEM((SLABS * SLICES_DEV * ANGLES, BLOCK), jnp.float32)
    half = jax.ShapeDtypeStruct((SLABS // 2, ROWS, BLOCK), jnp.bfloat16)
    return pl.pallas_call(
        frames_kernel,
        name="frame_gradients",
        in_specs=[smem, hbm, hbm, vmem, vmem, vmem, vmem, vmem, vmem],
        out_specs=[vmem, vmem],
        out_shape=[half, half],
        scratch_shapes=[
            table, table, table, table,
            pltpu.SMEM((FRAMES,), jnp.int32), pltpu.SMEM((FRAMES,), jnp.int32), pltpu.SemaphoreType.DMA((2,)),
        ],
        compiler_params=pltpu.CompilerParams(vmem_limit_bytes=VMEM_LIMIT),
    )(parity, owners, shifts, near_phases, far_phases, probe, measured, spread, gather)


def back_kernel(shears_in, shifts_in, tiles, out_hbm, table, stack, out, gathered, shears, shifts, sems):
    copies = [
        pltpu.make_async_copy(shears_in, shears, sems.at[0]),
        pltpu.make_async_copy(shifts_in, shifts, sems.at[1]),
    ]
    for copy in copies:
        copy.start()
    copies[0].wait()
    shape = (DEPTH, BWD_FINE * ANGLES)
    shear = pick_rows([shears[i] for i in range(ANGLES)], shape, 1, ANGLES)
    beam = iota(shape, 0).astype(jnp.float32)
    centre = BLOCK * 0.5 + (beam - (DEPTH - 1) * 0.5) * shear
    fine = (iota(shape, 1) // ANGLES).astype(jnp.float32)
    for j in range(BWD_COARSE):
        table[j * DEPTH : (j + 1) * DEPTH] = bell(fine + float(FIRST + BWD_FINE * j), centre)
    copies[1].wait()
    shape = (ANGLES, BLOCK)
    shift = pick_rows([shifts[i] for i in range(ANGLES)], shape, 0, ANGLES)
    lane = iota(shape, 1)
    zero = jnp.zeros(shape, jnp.float32)
    sends = []
    for k in range(TILES):
        gathered[k] = tiles[k].astype(jnp.float32)
    def build(p):
        for half in range(2):
            own, margin = [], []
            for k in range(TILES):
                s = p * 2 + half
                own.append(gathered[k, pl.ds(s, ANGLES, stride=SLICES_DEV), :])
                packed = gathered[k, pl.ds(OWN_ROWS + s, ANGLES // 2, stride=SLICES_DEV), :]
                margin.append(jnp.concatenate([packed, pltpu.roll(packed, BLOCK // 2, 1)], axis=0))
            whole = []
            for k in range(TILES):
                total = own[k]
                if k > 0:
                    total = total + jnp.where(lane < HALO, margin[k - 1], 0.0)
                if k < TILES - 1:
                    total = total + jnp.where(lane >= BLOCK - HALO, margin[k + 1], 0.0)
                whole.append(total.astype(jnp.bfloat16).astype(jnp.float32))
            whole = [zero] + whole + [zero, zero]
            placed = jnp.concatenate(
                [
                    jnp.where(shift == 0, whole[k + 1], jnp.where(shift > 0, whole[k + 2], whole[k]))
                    for k in range(BLOCKS + 1)
                ],
                axis=1,
            ).astype(jnp.bfloat16)
            for r in range(BWD_FINE):
                moved = jnp.concatenate([placed[:, FIRST + r :], placed[:, : FIRST + r]], axis=1)
                stack[p, r * ANGLES : (r + 1) * ANGLES, half * WIDE : (half + 1) * WIDE] = moved

    def finish(p):
        both = jnp.dot(table[...], stack[p], preferred_element_type=jnp.float32)
        for half in range(2):
            sums = both[:, half * WIDE : (half + 1) * WIDE]
            total = sums[0:DEPTH]
            for j in range(1, BWD_COARSE):
                total = total + left(sums[j * DEPTH : (j + 1) * DEPTH], BWD_FINE * j)
            out[p * 2 + half] = total[:, : BLOCKS * BLOCK]
        part = pl.ds(p * 2, 2)
        sends.append(pltpu.make_async_copy(out.at[part], out_hbm.at[part], sems.at[2 + p]))
        sends[-1].start()

    for p in range(PAIRS):
        build(p)
    for p in range(PAIRS):
        finish(p)
    for send in sends:
        send.wait()


def back_project(shears, shifts, tiles):
    hbm = pl.BlockSpec(memory_space=pltpu.HBM)
    return pl.pallas_call(
        back_kernel,
        name="back_project",
        in_specs=[hbm, hbm, pl.BlockSpec(memory_space=pltpu.VMEM)],
        out_specs=hbm,
        out_shape=jax.ShapeDtypeStruct((SLICES_DEV, DEPTH, BLOCKS * BLOCK), jnp.float32),
        scratch_shapes=[
            pltpu.VMEM((BWD_COARSE * DEPTH, BWD_FINE * ANGLES), jnp.bfloat16),
            pltpu.VMEM((PAIRS, BWD_FINE * ANGLES, 2 * WIDE), jnp.bfloat16),
            pltpu.VMEM((SLICES_DEV, DEPTH, BLOCKS * BLOCK), jnp.float32),
            pltpu.VMEM((TILES, ROWS, BLOCK), jnp.float32),
            pltpu.SMEM((ANGLES,), jnp.float32),
            pltpu.SMEM((ANGLES,), jnp.int32),
            pltpu.SemaphoreType.DMA((2 + PAIRS,)),
        ],
        compiler_params=pltpu.CompilerParams(vmem_limit_bytes=VMEM_LIMIT),
    )(shears, shifts, tiles)


def dft_matrices():
    index = np.arange(SIDE)
    phase = (np.outer(index, index) % SIDE) * (2.0 * np.pi / SIDE)
    cos, sin = np.cos(phase), np.sin(phase)
    spread = np.block([[cos, -sin], [sin, cos]])
    gather = np.block([[cos, sin], [-sin, cos]]) / SIDE
    return jnp.asarray(spread, jnp.bfloat16), jnp.asarray(gather, jnp.bfloat16)


def copies_of(value, count):
    return jnp.broadcast_to(value, (count, *value.shape))


def between_chips(value):
    count = lax.axis_size("slab")
    groups = [list(range(core, count, 2)) for core in range(2)]
    return lax.all_to_all(value, "slab", 0, 0, tiled=True, axis_index_groups=groups)


def between_cores(value):
    return lax.ppermute(value, "slab", [(i, i ^ 1) for i in range(lax.axis_size("slab"))])


def body(volume, shears, tile_shift, illumination, measured, frame_owner, frame_shift):
    spread, gather = dft_matrices()
    shifts = tile_shift.reshape(ANGLES)
    parity = (lax.axis_index("slab") % 2).astype(jnp.int32).reshape(1)
    partials = project(shears, shifts, volume)
    landed = lax.all_to_all(partials, "tile", 0, 0, tiled=True)
    phase = jnp.sum(landed.astype(jnp.int32), axis=0)
    phase = (((phase + 32768) & 65535) - 32768).astype(jnp.int16)
    near_phases = between_chips(copies_of(phase, SLABS // 2))
    far_phases = between_cores(near_phases)
    near_grads, far_grads = frame_gradients(
        parity, frame_owner.reshape(FRAMES), frame_shift, near_phases, far_phases, illumination, measured, spread, gather
    )
    grads = near_grads.astype(jnp.float32) + between_cores(far_grads).astype(jnp.float32)
    landed = between_chips(grads.astype(jnp.bfloat16)).astype(jnp.float32)
    grad = landed[0]
    for i in range(1, SLABS // 2):
        grad = grad + landed[i]
    tiles = lax.all_to_all(copies_of(grad.astype(jnp.bfloat16), TILES), "tile", 0, 0, tiled=True)
    return back_project(shears, shifts, tiles)


def solution(mesh):
    in_specs = (
        P("slab", "tile", None),
        P(),
        P(None, "tile"),
        P(),
        P(("slab", "tile"), None, None),
        P(("slab", "tile"), None),
        P(("slab", "tile")),
    )
    out_specs = P("slab", "tile", None)
    return jax.shard_map(body, mesh=mesh, in_specs=in_specs, out_specs=out_specs, check_vma=False)
```

```python
import math

import jax
import jax.numpy as jnp
import numpy as np
from jax import lax
from jax.experimental import pallas as pl
from jax.experimental.pallas import tpu as pltpu
from jax.sharding import PartitionSpec as P

SIDE = 128
BLOCK = 128
HALO = 32
ANGLES = 16
DEPTH = 64
SLICES_DEV = 8
BLOCKS = 8
SLABS = 16
TILES = 8
FRAMES = 32
FIRST = 38
WIDE = 9 * BLOCK
FWD_FINE, FWD_COARSE = 4, 14
BWD_FINE, BWD_COARSE = 14, 4
OWN_ROWS, EDGE_ROWS = ANGLES * SLICES_DEV, ANGLES // 2 * SLICES_DEV
PAIRS = SLICES_DEV // 2
ROWS = OWN_ROWS + EDGE_ROWS
GROUP = 32
MERGED = 4
UNPACK_UNROLL = 2
VMEM_LIMIT = 40 * 1024 * 1024
ALL_VMEM = 60 * 1024 * 1024

SIN_TERMS = (3.14159264, -5.16771008, 2.55007752, -0.598291286, 0.0776576603)
COS_TERMS = (0.999999953, -4.93479283, 4.05841135, -1.33187657, 0.219689611)


def iota(shape, dim):
    return lax.broadcasted_iota(jnp.int32, shape, dim)


def poly(terms, t):
    total = jnp.full_like(t, terms[-1])
    for term in reversed(terms[:-1]):
        total = total * t + term
    return total


def sine_and_cosine(turns):
    t = turns * turns
    half_sin = turns * poly(SIN_TERMS, t)
    half_cos = poly(COS_TERMS, t)
    return (2.0 * half_sin * half_cos, 1.0 - 2.0 * half_sin * half_sin)


def pick_rows(values, shape, dim, period):
    index = iota(shape, dim) % period
    total = jnp.zeros(shape, values[0].dtype)
    for i, value in enumerate(values):
        total = jnp.where(index == i, value, total)
    return total


def bell(offset, centre):
    spread = offset - centre
    return jnp.exp(-0.5 * spread * spread).astype(jnp.bfloat16)


def left(value, steps):
    return pltpu.roll(value, value.shape[1] - steps, 1)


def project_kernel(shears_in, shifts_in, volume_in, out, table, stack, volume, gathered, shears, shifts, sems):
    copies = [
        pltpu.make_async_copy(shears_in, shears, sems.at[0]),
        pltpu.make_async_copy(shifts_in, shifts, sems.at[1]),
    ]
    for p in range(PAIRS):
        part = pl.ds(p * 2, 2)
        copies.append(pltpu.make_async_copy(volume_in.at[part], volume.at[part], sems.at[2 + p]))
    for copy in copies:
        copy.start()
    copies[0].wait()
    shape = (ANGLES, FWD_FINE * DEPTH)
    shear = pick_rows([shears[i] for i in range(ANGLES)], shape, 0, ANGLES)
    lane = iota(shape, 1)
    beam = (lane % DEPTH).astype(jnp.float32)
    centre = BLOCK * 0.5 + (beam - (DEPTH - 1) * 0.5) * shear
    fine = (lane // DEPTH).astype(jnp.float32)
    for j in range(FWD_COARSE):
        table[j * ANGLES : (j + 1) * ANGLES] = bell(fine + float(FIRST + FWD_FINE * j), centre)
    copies[1].wait()
    shape = (ANGLES, BLOCK)
    shift = pick_rows([shifts[i] for i in range(ANGLES)], shape, 0, ANGLES)
    lane = iota((8, BLOCK), 1)
    full_lane = iota(shape, 1)
    outer = (lane < HALO) | (lane >= BLOCK - HALO)
    zero = jnp.zeros(shape, jnp.float32)
    def build(p):
        copies[2 + p].wait()
        for half in range(2):
            rows = jnp.concatenate(
                [volume[p * 2 + half], jnp.zeros((DEPTH, WIDE - BLOCKS * BLOCK), jnp.float32)], axis=1
            ).astype(jnp.bfloat16)
            for r in range(FWD_FINE):
                moved = rows if r == 0 else jnp.concatenate([rows[:, WIDE - r :], rows[:, : WIDE - r]], axis=1)
                stack[p, r * DEPTH : (r + 1) * DEPTH, half * WIDE : (half + 1) * WIDE] = moved

    def finish(p):
        fixed = []
        for n in range(WIDE // BLOCK):
            sums = jnp.dot(table[...], stack[p, :, n * 2 * BLOCK : (n + 1) * 2 * BLOCK], preferred_element_type=jnp.float32)
            for b in range(2):
                rolled = [
                    pltpu.roll(sums[j * ANGLES : (j + 1) * ANGLES, b * BLOCK : (b + 1) * BLOCK], FIRST + FWD_FINE * j, 1)
                    for j in range(FWD_COARSE)
                ]
                if (2 * n + b) % (BLOCKS + 1) == 0:
                    before = [zero] * FWD_COARSE
                total = jnp.where(full_lane >= FIRST, rolled[0], before[0])
                for j in range(1, FWD_COARSE):
                    total = total + jnp.where(full_lane >= FIRST + FWD_FINE * j, rolled[j], before[j])
                before = rolled
                turns = total * (1.0 / (2.0 * math.pi))
                turns = turns - jnp.floor(turns + 0.5)
                fixed.append(jnp.minimum(jnp.floor(turns * 65536.0 + 0.5), 32767.0))
        for half in range(2):
            block = [zero] + fixed[half * (BLOCKS + 1) : (half + 1) * (BLOCKS + 1)] + [zero]
            placed = []
            for k in range(BLOCKS):
                here = jnp.where(shift == 0, block[k + 1], jnp.where(shift > 0, block[k], block[k + 2]))
                placed.append(here)
            around = [zero] + placed + [zero]
            s = p * 2 + half
            for k in range(BLOCKS):
                gathered[k, pl.ds(s, ANGLES, stride=SLICES_DEV), :] = placed[k]
                after, before = around[k + 2], around[k]
                low = jnp.where(lane < HALO, after[:8], before[:8])
                high = jnp.where(lane < HALO, after[8:], before[8:])
                edge = jnp.where(outer, low, pltpu.roll(high, BLOCK // 2, 1))
                gathered[k, pl.ds(OWN_ROWS + s, ANGLES // 2, stride=SLICES_DEV), :] = edge

    build(0)
    for p in range(PAIRS):
        if p + 1 < PAIRS:
            build(p + 1)
        finish(p)
    for k in range(BLOCKS):
        out[k] = gathered[k].astype(jnp.int32).astype(jnp.int16)


def project(shears, shifts, volume):
    hbm = pl.BlockSpec(memory_space=pltpu.HBM)
    return pl.pallas_call(
        project_kernel,
        name="project",
        in_specs=[hbm, hbm, hbm],
        out_specs=pl.BlockSpec(memory_space=pltpu.VMEM),
        out_shape=jax.ShapeDtypeStruct((TILES, ROWS, BLOCK), jnp.int16),
        scratch_shapes=[
            pltpu.VMEM((FWD_COARSE * ANGLES, FWD_FINE * DEPTH), jnp.bfloat16),
            pltpu.VMEM((PAIRS, FWD_FINE * DEPTH, 2 * WIDE), jnp.bfloat16),
            pltpu.VMEM((SLICES_DEV, DEPTH, BLOCKS * BLOCK), jnp.float32),
            pltpu.VMEM((BLOCKS, ROWS, BLOCK), jnp.float32),
            pltpu.SMEM((ANGLES,), jnp.float32),
            pltpu.SMEM((ANGLES,), jnp.int32),
            pltpu.SemaphoreType.DMA((2 + PAIRS,)),
        ],
        compiler_params=pltpu.CompilerParams(vmem_limit_bytes=ALL_VMEM),
    )(shears, shifts, volume)


def frames_kernel(
    parity, owners_in, shifts_in, near_phases, far_phases, probe, measured, spread, gather,
    near_out, far_out, own, edge, own_sum, edge_sum, owners, shifts, sems,
):
    copies = [
        pltpu.make_async_copy(owners_in, owners, sems.at[0]),
        pltpu.make_async_copy(shifts_in, shifts, sems.at[1]),
    ]
    for copy in copies:
        copy.start()
    lane = iota((8, BLOCK), 1)
    outer = (lane < HALO) | (lane >= BLOCK - HALO)
    core = parity[0]

    def unpack(chip, carried):
        for which, phases in ((core, near_phases), (1 - core, far_phases)):
            base = pl.multiple_of((chip * 2 + which) * SLICES_DEV, SLICES_DEV)
            rows = phases[chip].astype(jnp.int32).astype(jnp.float32) * (1.0 / 65536.0)
            zero = jnp.zeros((SLICES_DEV, BLOCK), jnp.float32)
            for i in range(ANGLES):
                here = pl.ds(base + i * SIDE, SLICES_DEV)
                first = OWN_ROWS + i % (ANGLES // 2) * SLICES_DEV
                packed = rows[first : first + SLICES_DEV]
                own[here, :] = rows[i * SLICES_DEV : (i + 1) * SLICES_DEV]
                edge[here, :] = packed if i < ANGLES // 2 else pltpu.roll(packed, BLOCK // 2, 1)
                own_sum[here, :] = zero
                edge_sum[here, :] = zero
        return carried

    lax.fori_loop(0, SLABS // 2, unpack, 0, unroll=UNPACK_UNROLL)
    for copy in copies:
        copy.wait()

    def tiled(value):
        return value.reshape(SIDE // 8, 8, BLOCK)

    def turned(value):
        top = jnp.concatenate([value[:SIDE, :SIDE], value[SIDE:, :SIDE]], axis=1)
        bottom = jnp.concatenate([value[:SIDE, SIDE:], value[SIDE:, SIDE:]], axis=1)
        return jnp.concatenate([top, bottom], axis=0)

    def across(values, matrix, per_pair):
        results = []
        for first in range(0, len(values), MERGED * per_pair):
            rows = jnp.concatenate(values[first : first + MERGED * per_pair], axis=0)
            product = jnp.dot(rows, matrix[...], preferred_element_type=jnp.float32)
            results += [product[g * 2 * SIDE : (g + 1) * 2 * SIDE] for g in range(MERGED)]
        return results

    def group(step, carried):
        first = step * GROUP
        rows, inside, amount, waves, fields = [], [], [], [], []
        for k in range(GROUP):
            shift = shifts[first + k]
            rows.append(pl.ds(pl.multiple_of(owners[first + k] * SIDE, SIDE), SIDE))
            bound = jnp.where(shift >= 0, shift, shift + BLOCK)
            inside.append((lane >= bound) == (shift >= 0))
            amount.append(bound)
        for k in range(GROUP):
            chosen = jnp.where(inside[k], tiled(own[rows[k], :]), tiled(edge[rows[k], :])).reshape(SIDE, BLOCK)
            turns = pltpu.roll(chosen, lax.rem(BLOCK - amount[k], BLOCK), 1)
            object_im, object_re = sine_and_cosine(turns)
            wave_re = probe[0] * object_re - probe[1] * object_im
            wave_im = probe[0] * object_im + probe[1] * object_re
            waves.append((wave_re, wave_im))
            fields.append(jnp.concatenate([wave_re.astype(jnp.bfloat16), wave_im.astype(jnp.bfloat16)], axis=1))
        pairs = range(GROUP // 2)
        half = across(fields, spread, 2)
        far = [jnp.dot(gather[...], turned(half[g].astype(jnp.bfloat16)), preferred_element_type=jnp.float32) for g in pairs]
        resid = []
        for g in pairs:
            far_re, far_im = far[g][:SIDE], far[g][SIDE:]
            amplitude = jnp.concatenate(
                [measured[first + 2 * g].astype(jnp.float32), measured[first + 2 * g + 1].astype(jnp.float32)], axis=1
            )
            ratio = amplitude * lax.rsqrt(far_re * far_re + far_im * far_im + 0.25)
            factor = 0.5 * jnp.mean(ratio, axis=(0, 1), keepdims=True) - ratio
            resid.append(
                jnp.concatenate([(far_re * factor).astype(jnp.bfloat16), (far_im * factor).astype(jnp.bfloat16)], axis=0)
            )
        back = [
            jnp.dot(spread[...], resid[g], preferred_element_type=jnp.float32) for g in pairs
        ]
        near = across([turned(back[g].astype(jnp.bfloat16)) for g in pairs], gather, 1)
        grads = []
        for k in range(GROUP):
            part = near[k // 2][(k % 2) * SIDE : (k % 2 + 1) * SIDE]
            wave_re, wave_im = waves[k]
            grads.append(pltpu.roll(part[:, SIDE:] * wave_re - part[:, :SIDE] * wave_im, amount[k], 1))
        for k in range(GROUP):
            grad = tiled(grads[k])
            own_sum[rows[k], :] = own_sum[rows[k], :] + jnp.where(inside[k], grad, 0.0).reshape(SIDE, BLOCK)
            edge_sum[rows[k], :] = edge_sum[rows[k], :] + jnp.where(inside[k], 0.0, grad).reshape(SIDE, BLOCK)
        return carried

    lax.fori_loop(0, FRAMES // GROUP, group, 0)

    def pack(chip, carried):
        for which, out in ((core, near_out), (1 - core, far_out)):
            base = pl.multiple_of((chip * 2 + which) * SLICES_DEV, SLICES_DEV)
            here = [pl.ds(base + i * SIDE, SLICES_DEV) for i in range(ANGLES)]
            rows = [own_sum[here[i], :] for i in range(ANGLES)]
            for i in range(ANGLES // 2):
                high = pltpu.roll(edge_sum[here[i + ANGLES // 2], :], BLOCK // 2, 1)
                rows.append(jnp.where(outer, edge_sum[here[i], :], high))
            out[chip] = jnp.concatenate(rows, axis=0).astype(jnp.bfloat16)
        return carried

    lax.fori_loop(0, SLABS // 2, pack, 0, unroll=UNPACK_UNROLL)


def frame_gradients(parity, owners, shifts, near_phases, far_phases, probe, measured, spread, gather):
    smem = pl.BlockSpec(memory_space=pltpu.SMEM)
    hbm = pl.BlockSpec(memory_space=pltpu.HBM)
    vmem = pl.BlockSpec(memory_space=pltpu.VMEM)
    table = pltpu.VMEM((SLABS * SLICES_DEV * ANGLES, BLOCK), jnp.float32)
    half = jax.ShapeDtypeStruct((SLABS // 2, ROWS, BLOCK), jnp.bfloat16)
    return pl.pallas_call(
        frames_kernel,
        name="frame_gradients",
        in_specs=[smem, hbm, hbm, vmem, vmem, vmem, vmem, vmem, vmem],
        out_specs=[vmem, vmem],
        out_shape=[half, half],
        scratch_shapes=[
            table, table, table, table,
            pltpu.SMEM((FRAMES,), jnp.int32), pltpu.SMEM((FRAMES,), jnp.int32), pltpu.SemaphoreType.DMA((2,)),
        ],
        compiler_params=pltpu.CompilerParams(vmem_limit_bytes=VMEM_LIMIT),
    )(parity, owners, shifts, near_phases, far_phases, probe, measured, spread, gather)


def back_kernel(shears_in, shifts_in, tiles, out_hbm, table, stack, out, gathered, shears, shifts, sems):
    copies = [
        pltpu.make_async_copy(shears_in, shears, sems.at[0]),
        pltpu.make_async_copy(shifts_in, shifts, sems.at[1]),
    ]
    for copy in copies:
        copy.start()
    copies[0].wait()
    shape = (DEPTH, BWD_FINE * ANGLES)
    shear = pick_rows([shears[i] for i in range(ANGLES)], shape, 1, ANGLES)
    beam = iota(shape, 0).astype(jnp.float32)
    centre = BLOCK * 0.5 + (beam - (DEPTH - 1) * 0.5) * shear
    fine = (iota(shape, 1) // ANGLES).astype(jnp.float32)
    for j in range(BWD_COARSE):
        table[j * DEPTH : (j + 1) * DEPTH] = bell(fine + float(FIRST + BWD_FINE * j), centre)
    copies[1].wait()
    shape = (ANGLES, BLOCK)
    shift = pick_rows([shifts[i] for i in range(ANGLES)], shape, 0, ANGLES)
    lane = iota(shape, 1)
    zero = jnp.zeros(shape, jnp.float32)
    sends = []
    for k in range(TILES):
        gathered[k] = tiles[k].astype(jnp.float32)
    def build(p):
        for half in range(2):
            own, margin = [], []
            for k in range(TILES):
                s = p * 2 + half
                own.append(gathered[k, pl.ds(s, ANGLES, stride=SLICES_DEV), :])
                packed = gathered[k, pl.ds(OWN_ROWS + s, ANGLES // 2, stride=SLICES_DEV), :]
                margin.append(jnp.concatenate([packed, pltpu.roll(packed, BLOCK // 2, 1)], axis=0))
            whole = []
            for k in range(TILES):
                total = own[k]
                if k > 0:
                    total = total + jnp.where(lane < HALO, margin[k - 1], 0.0)
                if k < TILES - 1:
                    total = total + jnp.where(lane >= BLOCK - HALO, margin[k + 1], 0.0)
                whole.append(total.astype(jnp.bfloat16).astype(jnp.float32))
            whole = [zero] + whole + [zero, zero]
            placed = jnp.concatenate(
                [
                    jnp.where(shift == 0, whole[k + 1], jnp.where(shift > 0, whole[k + 2], whole[k]))
                    for k in range(BLOCKS + 1)
                ],
                axis=1,
            ).astype(jnp.bfloat16)
            for r in range(BWD_FINE):
                moved = jnp.concatenate([placed[:, FIRST + r :], placed[:, : FIRST + r]], axis=1)
                stack[p, r * ANGLES : (r + 1) * ANGLES, half * WIDE : (half + 1) * WIDE] = moved

    def finish(p):
        both = jnp.dot(table[...], stack[p], preferred_element_type=jnp.float32)
        for half in range(2):
            sums = both[:, half * WIDE : (half + 1) * WIDE]
            total = sums[0:DEPTH]
            for j in range(1, BWD_COARSE):
                total = total + left(sums[j * DEPTH : (j + 1) * DEPTH], BWD_FINE * j)
            out[p * 2 + half] = total[:, : BLOCKS * BLOCK]
        part = pl.ds(p * 2, 2)
        sends.append(pltpu.make_async_copy(out.at[part], out_hbm.at[part], sems.at[2 + p]))
        sends[-1].start()

    for p in range(PAIRS):
        build(p)
    for p in range(PAIRS):
        finish(p)
    for send in sends:
        send.wait()


def back_project(shears, shifts, tiles):
    hbm = pl.BlockSpec(memory_space=pltpu.HBM)
    return pl.pallas_call(
        back_kernel,
        name="back_project",
        in_specs=[hbm, hbm, pl.BlockSpec(memory_space=pltpu.VMEM)],
        out_specs=hbm,
        out_shape=jax.ShapeDtypeStruct((SLICES_DEV, DEPTH, BLOCKS * BLOCK), jnp.float32),
        scratch_shapes=[
            pltpu.VMEM((BWD_COARSE * DEPTH, BWD_FINE * ANGLES), jnp.bfloat16),
            pltpu.VMEM((PAIRS, BWD_FINE * ANGLES, 2 * WIDE), jnp.bfloat16),
            pltpu.VMEM((SLICES_DEV, DEPTH, BLOCKS * BLOCK), jnp.float32),
            pltpu.VMEM((TILES, ROWS, BLOCK), jnp.float32),
            pltpu.SMEM((ANGLES,), jnp.float32),
            pltpu.SMEM((ANGLES,), jnp.int32),
            pltpu.SemaphoreType.DMA((2 + PAIRS,)),
        ],
        compiler_params=pltpu.CompilerParams(vmem_limit_bytes=VMEM_LIMIT),
    )(shears, shifts, tiles)


def dft_matrices():
    index = np.arange(SIDE)
    phase = (np.outer(index, index) % SIDE) * (2.0 * np.pi / SIDE)
    cos, sin = np.cos(phase), np.sin(phase)
    spread = np.block([[cos, -sin], [sin, cos]])
    gather = np.block([[cos, sin], [-sin, cos]]) / SIDE
    return jnp.asarray(spread, jnp.bfloat16), jnp.asarray(gather, jnp.bfloat16)


def copies_of(value, count):
    return jnp.broadcast_to(value, (count, *value.shape))


def between_chips(value):
    count = lax.axis_size("slab")
    groups = [list(range(core, count, 2)) for core in range(2)]
    return lax.all_to_all(value, "slab", 0, 0, tiled=True, axis_index_groups=groups)


def between_cores(value):
    return lax.ppermute(value, "slab", [(i, i ^ 1) for i in range(lax.axis_size("slab"))])


def body(volume, shears, tile_shift, illumination, measured, frame_owner, frame_shift):
    spread, gather = dft_matrices()
    shifts = tile_shift.reshape(ANGLES)
    parity = (lax.axis_index("slab") % 2).astype(jnp.int32).reshape(1)
    partials = project(shears, shifts, volume)
    landed = lax.all_to_all(partials, "tile", 0, 0, tiled=True)
    phase = jnp.sum(landed.astype(jnp.int32), axis=0)
    phase = (((phase + 32768) & 65535) - 32768).astype(jnp.int16)
    near_phases = between_chips(copies_of(phase, SLABS // 2))
    far_phases = between_cores(near_phases)
    near_grads, far_grads = frame_gradients(
        parity, frame_owner.reshape(FRAMES), frame_shift, near_phases, far_phases, illumination, measured, spread, gather
    )
    grads = near_grads.astype(jnp.float32) + between_cores(far_grads).astype(jnp.float32)
    landed = between_chips(grads.astype(jnp.bfloat16)).astype(jnp.float32)
    grad = landed[0]
    for i in range(1, SLABS // 2):
        grad = grad + landed[i]
    tiles = lax.all_to_all(copies_of(grad.astype(jnp.bfloat16), TILES), "tile", 0, 0, tiled=True)
    return back_project(shears, shifts, tiles)


def solution(mesh):
    in_specs = (
        P("slab", "tile", None),
        P(),
        P(None, "tile"),
        P(),
        P(("slab", "tile"), None, None),
        P(("slab", "tile"), None),
        P(("slab", "tile")),
    )
    out_specs = P("slab", "tile", None)
    return jax.shard_map(body, mesh=mesh, in_specs=in_specs, out_specs=out_specs, check_vma=False)
```

```python
import math

import jax
import jax.numpy as jnp
import numpy as np
from jax import lax
from jax.experimental import pallas as pl
from jax.experimental.pallas import tpu as pltpu
from jax.sharding import PartitionSpec as P

SIDE = 128
BLOCK = 128
HALO = 32
ANGLES = 16
DEPTH = 64
SLICES_DEV = 8
BLOCKS = 8
SLABS = 16
TILES = 8
FRAMES = 32
FIRST = 38
WIDE = 9 * BLOCK
FWD_FINE, FWD_COARSE = 4, 14
BWD_FINE, BWD_COARSE = 14, 4
OWN_ROWS, EDGE_ROWS = ANGLES * SLICES_DEV, ANGLES // 2 * SLICES_DEV
PAIRS = SLICES_DEV // 2
ROWS = OWN_ROWS + EDGE_ROWS
GROUP = 32
MERGED = 4
UNPACK_UNROLL = 2
VMEM_LIMIT = 40 * 1024 * 1024
ALL_VMEM = 60 * 1024 * 1024

SIN_TERMS = (3.14159264, -5.16771008, 2.55007752, -0.598291286, 0.0776576603)
COS_TERMS = (0.999999953, -4.93479283, 4.05841135, -1.33187657, 0.219689611)


def iota(shape, dim):
    return lax.broadcasted_iota(jnp.int32, shape, dim)


def poly(terms, t):
    total = jnp.full_like(t, terms[-1])
    for term in reversed(terms[:-1]):
        total = total * t + term
    return total


def sine_and_cosine(turns):
    t = turns * turns
    half_sin = turns * poly(SIN_TERMS, t)
    half_cos = poly(COS_TERMS, t)
    return (2.0 * half_sin * half_cos, 1.0 - 2.0 * half_sin * half_sin)


def pick_rows(values, shape, dim, period):
    index = iota(shape, dim) % period
    total = jnp.zeros(shape, values[0].dtype)
    for i, value in enumerate(values):
        total = jnp.where(index == i, value, total)
    return total


def bell(offset, centre):
    spread = offset - centre
    return jnp.exp(-0.5 * spread * spread).astype(jnp.bfloat16)


def left(value, steps):
    return pltpu.roll(value, value.shape[1] - steps, 1)


def project_kernel(shears_in, shifts_in, volume_in, out, table, stack, volume, gathered, shears, shifts, sems):
    copies = [
        pltpu.make_async_copy(shears_in, shears, sems.at[0]),
        pltpu.make_async_copy(shifts_in, shifts, sems.at[1]),
    ]
    for p in range(PAIRS):
        part = pl.ds(p * 2, 2)
        copies.append(pltpu.make_async_copy(volume_in.at[part], volume.at[part], sems.at[2 + p]))
    for copy in copies:
        copy.start()
    copies[0].wait()
    shape = (ANGLES, FWD_FINE * DEPTH)
    shear = pick_rows([shears[i] for i in range(ANGLES)], shape, 0, ANGLES)
    lane = iota(shape, 1)
    beam = (lane % DEPTH).astype(jnp.float32)
    centre = BLOCK * 0.5 + (beam - (DEPTH - 1) * 0.5) * shear
    fine = (lane // DEPTH).astype(jnp.float32)
    for j in range(FWD_COARSE):
        table[j * ANGLES : (j + 1) * ANGLES] = bell(fine + float(FIRST + FWD_FINE * j), centre)
    copies[1].wait()
    shape = (ANGLES, BLOCK)
    shift = pick_rows([shifts[i] for i in range(ANGLES)], shape, 0, ANGLES)
    lane = iota((8, BLOCK), 1)
    full_lane = iota(shape, 1)
    outer = (lane < HALO) | (lane >= BLOCK - HALO)
    zero = jnp.zeros(shape, jnp.float32)
    def build(p):
        copies[2 + p].wait()
        for half in range(2):
            rows = jnp.concatenate(
                [volume[p * 2 + half], jnp.zeros((DEPTH, WIDE - BLOCKS * BLOCK), jnp.float32)], axis=1
            ).astype(jnp.bfloat16)
            for r in range(FWD_FINE):
                moved = rows if r == 0 else jnp.concatenate([rows[:, WIDE - r :], rows[:, : WIDE - r]], axis=1)
                stack[p, r * DEPTH : (r + 1) * DEPTH, half * WIDE : (half + 1) * WIDE] = moved

    def finish(p):
        fixed = []
        for n in range(WIDE // BLOCK):
            sums = jnp.dot(table[...], stack[p, :, n * 2 * BLOCK : (n + 1) * 2 * BLOCK], preferred_element_type=jnp.float32)
            for b in range(2):
                rolled = [
                    pltpu.roll(sums[j * ANGLES : (j + 1) * ANGLES, b * BLOCK : (b + 1) * BLOCK], FIRST + FWD_FINE * j, 1)
                    for j in range(FWD_COARSE)
                ]
                if (2 * n + b) % (BLOCKS + 1) == 0:
                    before = [zero] * FWD_COARSE
                total = jnp.where(full_lane >= FIRST, rolled[0], before[0])
                for j in range(1, FWD_COARSE):
                    total = total + jnp.where(full_lane >= FIRST + FWD_FINE * j, rolled[j], before[j])
                before = rolled
                turns = total * (1.0 / (2.0 * math.pi))
                turns = turns - jnp.floor(turns + 0.5)
                fixed.append(jnp.minimum(jnp.floor(turns * 65536.0 + 0.5), 32767.0))
        for half in range(2):
            block = [zero] + fixed[half * (BLOCKS + 1) : (half + 1) * (BLOCKS + 1)] + [zero]
            placed = []
            for k in range(BLOCKS):
                here = jnp.where(shift == 0, block[k + 1], jnp.where(shift > 0, block[k], block[k + 2]))
                placed.append(here)
            around = [zero] + placed + [zero]
            s = p * 2 + half
            for k in range(BLOCKS):
                gathered[k, pl.ds(s, ANGLES, stride=SLICES_DEV), :] = placed[k]
                after, before = around[k + 2], around[k]
                low = jnp.where(lane < HALO, after[:8], before[:8])
                high = jnp.where(lane < HALO, after[8:], before[8:])
                edge = jnp.where(outer, low, pltpu.roll(high, BLOCK // 2, 1))
                gathered[k, pl.ds(OWN_ROWS + s, ANGLES // 2, stride=SLICES_DEV), :] = edge

    build(0)
    for p in range(PAIRS):
        if p + 1 < PAIRS:
            build(p + 1)
        finish(p)
    for k in range(BLOCKS):
        out[k] = gathered[k].astype(jnp.int32).astype(jnp.int16)


def project(shears, shifts, volume):
    hbm = pl.BlockSpec(memory_space=pltpu.HBM)
    return pl.pallas_call(
        project_kernel,
        name="project",
        in_specs=[hbm, hbm, hbm],
        out_specs=pl.BlockSpec(memory_space=pltpu.VMEM),
        out_shape=jax.ShapeDtypeStruct((TILES, ROWS, BLOCK), jnp.int16),
        scratch_shapes=[
            pltpu.VMEM((FWD_COARSE * ANGLES, FWD_FINE * DEPTH), jnp.bfloat16),
            pltpu.VMEM((PAIRS, FWD_FINE * DEPTH, 2 * WIDE), jnp.bfloat16),
            pltpu.VMEM((SLICES_DEV, DEPTH, BLOCKS * BLOCK), jnp.float32),
            pltpu.VMEM((BLOCKS, ROWS, BLOCK), jnp.float32),
            pltpu.SMEM((ANGLES,), jnp.float32),
            pltpu.SMEM((ANGLES,), jnp.int32),
            pltpu.SemaphoreType.DMA((2 + PAIRS,)),
        ],
        compiler_params=pltpu.CompilerParams(vmem_limit_bytes=ALL_VMEM),
    )(shears, shifts, volume)


def frames_kernel(
    parity, owners_in, shifts_in, near_phases, far_phases, probe, measured, spread, gather,
    near_out, far_out, own, edge, own_sum, edge_sum, owners, shifts, sems,
):
    copies = [
        pltpu.make_async_copy(owners_in, owners, sems.at[0]),
        pltpu.make_async_copy(shifts_in, shifts, sems.at[1]),
    ]
    for copy in copies:
        copy.start()
    lane = iota((8, BLOCK), 1)
    outer = (lane < HALO) | (lane >= BLOCK - HALO)
    core = parity[0]

    def unpack(chip, carried):
        for which, phases in ((core, near_phases), (1 - core, far_phases)):
            base = pl.multiple_of((chip * 2 + which) * SLICES_DEV, SLICES_DEV)
            rows = phases[chip].astype(jnp.int32).astype(jnp.float32) * (1.0 / 65536.0)
            zero = jnp.zeros((SLICES_DEV, BLOCK), jnp.float32)
            for i in range(ANGLES):
                here = pl.ds(base + i * SIDE, SLICES_DEV)
                first = OWN_ROWS + i % (ANGLES // 2) * SLICES_DEV
                packed = rows[first : first + SLICES_DEV]
                own[here, :] = rows[i * SLICES_DEV : (i + 1) * SLICES_DEV]
                edge[here, :] = packed if i < ANGLES // 2 else pltpu.roll(packed, BLOCK // 2, 1)
                own_sum[here, :] = zero
                edge_sum[here, :] = zero
        return carried

    lax.fori_loop(0, SLABS // 2, unpack, 0, unroll=UNPACK_UNROLL)
    for copy in copies:
        copy.wait()

    power = probe[0] * probe[0] + probe[1] * probe[1]
    sample = measured[0, 0:16].astype(jnp.float32)
    for k in range(4, FRAMES, 4):
        sample = sample + measured[k, k * 4 % SIDE : k * 4 % SIDE + 16].astype(jnp.float32)
    share = lax.rsqrt(jnp.mean(power, axis=(0, 1), keepdims=True) + 0.25)
    share = share * jnp.mean(sample, axis=(0, 1), keepdims=True) * (0.75 / (FRAMES // 4))

    def tiled(value):
        return value.reshape(SIDE // 8, 8, BLOCK)

    def turned(value):
        top = jnp.concatenate([value[:SIDE, :SIDE], value[SIDE:, :SIDE]], axis=1)
        bottom = jnp.concatenate([value[:SIDE, SIDE:], value[SIDE:, SIDE:]], axis=1)
        return jnp.concatenate([top, bottom], axis=0)

    def across(values, matrix, per_pair):
        results = []
        for first in range(0, len(values), MERGED * per_pair):
            rows = jnp.concatenate(values[first : first + MERGED * per_pair], axis=0)
            product = jnp.dot(rows, matrix[...], preferred_element_type=jnp.float32)
            results += [product[g * 2 * SIDE : (g + 1) * 2 * SIDE] for g in range(MERGED)]
        return results

    def group(step, carried):
        first = step * GROUP
        rows, inside, amount, waves, fields = [], [], [], [], []
        for k in range(GROUP):
            shift = shifts[first + k]
            rows.append(pl.ds(pl.multiple_of(owners[first + k] * SIDE, SIDE), SIDE))
            bound = jnp.where(shift >= 0, shift, shift + BLOCK)
            inside.append((lane >= bound) == (shift >= 0))
            amount.append(bound)
        for k in range(GROUP):
            chosen = jnp.where(inside[k], tiled(own[rows[k], :]), tiled(edge[rows[k], :])).reshape(SIDE, BLOCK)
            turns = pltpu.roll(chosen, lax.rem(BLOCK - amount[k], BLOCK), 1)
            object_im, object_re = sine_and_cosine(turns)
            wave_re = probe[0] * object_re - probe[1] * object_im
            wave_im = probe[0] * object_im + probe[1] * object_re
            waves.append((wave_re, wave_im))
            fields.append(jnp.concatenate([wave_re.astype(jnp.bfloat16), wave_im.astype(jnp.bfloat16)], axis=1))
        pairs = range(GROUP // 2)
        half = across(fields, spread, 2)
        far = [jnp.dot(gather[...], turned(half[g].astype(jnp.bfloat16)), preferred_element_type=jnp.float32) for g in pairs]
        resid = []
        for g in pairs:
            far_re, far_im = far[g][:SIDE], far[g][SIDE:]
            amplitude = jnp.concatenate(
                [measured[first + 2 * g].astype(jnp.float32), measured[first + 2 * g + 1].astype(jnp.float32)], axis=1
            )
            ratio = amplitude * lax.rsqrt(far_re * far_re + far_im * far_im + 0.25)
            factor = share - ratio
            resid.append(
                jnp.concatenate([(far_re * factor).astype(jnp.bfloat16), (far_im * factor).astype(jnp.bfloat16)], axis=0)
            )
        back = [
            jnp.dot(spread[...], resid[g], preferred_element_type=jnp.float32) for g in pairs
        ]
        near = across([turned(back[g].astype(jnp.bfloat16)) for g in pairs], gather, 1)
        grads = []
        for k in range(GROUP):
            part = near[k // 2][(k % 2) * SIDE : (k % 2 + 1) * SIDE]
            wave_re, wave_im = waves[k]
            grads.append(pltpu.roll(part[:, SIDE:] * wave_re - part[:, :SIDE] * wave_im, amount[k], 1))
        for k in range(GROUP):
            grad = tiled(grads[k])
            own_sum[rows[k], :] = own_sum[rows[k], :] + jnp.where(inside[k], grad, 0.0).reshape(SIDE, BLOCK)
            edge_sum[rows[k], :] = edge_sum[rows[k], :] + jnp.where(inside[k], 0.0, grad).reshape(SIDE, BLOCK)
        return carried

    lax.fori_loop(0, FRAMES // GROUP, group, 0)

    def pack(chip, carried):
        for which, out in ((core, near_out), (1 - core, far_out)):
            base = pl.multiple_of((chip * 2 + which) * SLICES_DEV, SLICES_DEV)
            here = [pl.ds(base + i * SIDE, SLICES_DEV) for i in range(ANGLES)]
            rows = [own_sum[here[i], :] for i in range(ANGLES)]
            for i in range(ANGLES // 2):
                high = pltpu.roll(edge_sum[here[i + ANGLES // 2], :], BLOCK // 2, 1)
                rows.append(jnp.where(outer, edge_sum[here[i], :], high))
            out[chip] = jnp.concatenate(rows, axis=0).astype(jnp.bfloat16)
        return carried

    lax.fori_loop(0, SLABS // 2, pack, 0, unroll=UNPACK_UNROLL)


def frame_gradients(parity, owners, shifts, near_phases, far_phases, probe, measured, spread, gather):
    smem = pl.BlockSpec(memory_space=pltpu.SMEM)
    hbm = pl.BlockSpec(memory_space=pltpu.HBM)
    vmem = pl.BlockSpec(memory_space=pltpu.VMEM)
    table = pltpu.VMEM((SLABS * SLICES_DEV * ANGLES, BLOCK), jnp.float32)
    half = jax.ShapeDtypeStruct((SLABS // 2, ROWS, BLOCK), jnp.bfloat16)
    return pl.pallas_call(
        frames_kernel,
        name="frame_gradients",
        in_specs=[smem, hbm, hbm, vmem, vmem, vmem, vmem, vmem, vmem],
        out_specs=[vmem, vmem],
        out_shape=[half, half],
        scratch_shapes=[
            table, table, table, table,
            pltpu.SMEM((FRAMES,), jnp.int32), pltpu.SMEM((FRAMES,), jnp.int32), pltpu.SemaphoreType.DMA((2,)),
        ],
        compiler_params=pltpu.CompilerParams(vmem_limit_bytes=VMEM_LIMIT),
    )(parity, owners, shifts, near_phases, far_phases, probe, measured, spread, gather)


def back_kernel(shears_in, shifts_in, tiles, out_hbm, table, stack, out, gathered, shears, shifts, sems):
    copies = [
        pltpu.make_async_copy(shears_in, shears, sems.at[0]),
        pltpu.make_async_copy(shifts_in, shifts, sems.at[1]),
    ]
    for copy in copies:
        copy.start()
    copies[0].wait()
    shape = (DEPTH, BWD_FINE * ANGLES)
    shear = pick_rows([shears[i] for i in range(ANGLES)], shape, 1, ANGLES)
    beam = iota(shape, 0).astype(jnp.float32)
    centre = BLOCK * 0.5 + (beam - (DEPTH - 1) * 0.5) * shear
    fine = (iota(shape, 1) // ANGLES).astype(jnp.float32)
    for j in range(BWD_COARSE):
        table[j * DEPTH : (j + 1) * DEPTH] = bell(fine + float(FIRST + BWD_FINE * j), centre)
    copies[1].wait()
    shape = (ANGLES, BLOCK)
    shift = pick_rows([shifts[i] for i in range(ANGLES)], shape, 0, ANGLES)
    lane = iota(shape, 1)
    zero = jnp.zeros(shape, jnp.float32)
    sends = []
    for k in range(TILES):
        gathered[k] = tiles[k].astype(jnp.float32)
    def build(p):
        for half in range(2):
            own, margin = [], []
            for k in range(TILES):
                s = p * 2 + half
                own.append(gathered[k, pl.ds(s, ANGLES, stride=SLICES_DEV), :])
                packed = gathered[k, pl.ds(OWN_ROWS + s, ANGLES // 2, stride=SLICES_DEV), :]
                margin.append(jnp.concatenate([packed, pltpu.roll(packed, BLOCK // 2, 1)], axis=0))
            whole = []
            for k in range(TILES):
                total = own[k]
                if k > 0:
                    total = total + jnp.where(lane < HALO, margin[k - 1], 0.0)
                if k < TILES - 1:
                    total = total + jnp.where(lane >= BLOCK - HALO, margin[k + 1], 0.0)
                whole.append(total.astype(jnp.bfloat16).astype(jnp.float32))
            whole = [zero] + whole + [zero, zero]
            placed = jnp.concatenate(
                [
                    jnp.where(shift == 0, whole[k + 1], jnp.where(shift > 0, whole[k + 2], whole[k]))
                    for k in range(BLOCKS + 1)
                ],
                axis=1,
            ).astype(jnp.bfloat16)
            for r in range(BWD_FINE):
                moved = jnp.concatenate([placed[:, FIRST + r :], placed[:, : FIRST + r]], axis=1)
                stack[p, r * ANGLES : (r + 1) * ANGLES, half * WIDE : (half + 1) * WIDE] = moved

    def finish(p):
        both = jnp.dot(table[...], stack[p], preferred_element_type=jnp.float32)
        for half in range(2):
            sums = both[:, half * WIDE : (half + 1) * WIDE]
            total = sums[0:DEPTH]
            for j in range(1, BWD_COARSE):
                total = total + left(sums[j * DEPTH : (j + 1) * DEPTH], BWD_FINE * j)
            out[p * 2 + half] = total[:, : BLOCKS * BLOCK]
        part = pl.ds(p * 2, 2)
        sends.append(pltpu.make_async_copy(out.at[part], out_hbm.at[part], sems.at[2 + p]))
        sends[-1].start()

    for p in range(PAIRS):
        build(p)
    for p in range(PAIRS):
        finish(p)
    for send in sends:
        send.wait()


def back_project(shears, shifts, tiles):
    hbm = pl.BlockSpec(memory_space=pltpu.HBM)
    return pl.pallas_call(
        back_kernel,
        name="back_project",
        in_specs=[hbm, hbm, pl.BlockSpec(memory_space=pltpu.VMEM)],
        out_specs=hbm,
        out_shape=jax.ShapeDtypeStruct((SLICES_DEV, DEPTH, BLOCKS * BLOCK), jnp.float32),
        scratch_shapes=[
            pltpu.VMEM((BWD_COARSE * DEPTH, BWD_FINE * ANGLES), jnp.bfloat16),
            pltpu.VMEM((PAIRS, BWD_FINE * ANGLES, 2 * WIDE), jnp.bfloat16),
            pltpu.VMEM((SLICES_DEV, DEPTH, BLOCKS * BLOCK), jnp.float32),
            pltpu.VMEM((TILES, ROWS, BLOCK), jnp.float32),
            pltpu.SMEM((ANGLES,), jnp.float32),
            pltpu.SMEM((ANGLES,), jnp.int32),
            pltpu.SemaphoreType.DMA((2 + PAIRS,)),
        ],
        compiler_params=pltpu.CompilerParams(vmem_limit_bytes=VMEM_LIMIT),
    )(shears, shifts, tiles)


def dft_matrices():
    index = np.arange(SIDE)
    phase = (np.outer(index, index) % SIDE) * (2.0 * np.pi / SIDE)
    cos, sin = np.cos(phase), np.sin(phase)
    spread = np.block([[cos, -sin], [sin, cos]])
    gather = np.block([[cos, sin], [-sin, cos]]) / SIDE
    return jnp.asarray(spread, jnp.bfloat16), jnp.asarray(gather, jnp.bfloat16)


def copies_of(value, count):
    return jnp.broadcast_to(value, (count, *value.shape))


def between_chips(value):
    count = lax.axis_size("slab")
    groups = [list(range(core, count, 2)) for core in range(2)]
    return lax.all_to_all(value, "slab", 0, 0, tiled=True, axis_index_groups=groups)


def between_cores(value):
    return lax.ppermute(value, "slab", [(i, i ^ 1) for i in range(lax.axis_size("slab"))])


def body(volume, shears, tile_shift, illumination, measured, frame_owner, frame_shift):
    spread, gather = dft_matrices()
    shifts = tile_shift.reshape(ANGLES)
    parity = (lax.axis_index("slab") % 2).astype(jnp.int32).reshape(1)
    partials = project(shears, shifts, volume)
    landed = lax.all_to_all(partials, "tile", 0, 0, tiled=True)
    phase = jnp.sum(landed.astype(jnp.int32), axis=0)
    phase = (((phase + 32768) & 65535) - 32768).astype(jnp.int16)
    near_phases = between_chips(copies_of(phase, SLABS // 2))
    far_phases = between_cores(near_phases)
    near_grads, far_grads = frame_gradients(
        parity, frame_owner.reshape(FRAMES), frame_shift, near_phases, far_phases, illumination, measured, spread, gather
    )
    grads = near_grads.astype(jnp.float32) + between_cores(far_grads).astype(jnp.float32)
    landed = between_chips(grads.astype(jnp.bfloat16)).astype(jnp.float32)
    grad = landed[0]
    for i in range(1, SLABS // 2):
        grad = grad + landed[i]
    tiles = lax.all_to_all(copies_of(grad.astype(jnp.bfloat16), TILES), "tile", 0, 0, tiled=True)
    return back_project(shears, shifts, tiles)


def solution(mesh):
    in_specs = (
        P("slab", "tile", None),
        P(),
        P(None, "tile"),
        P(),
        P(("slab", "tile"), None, None),
        P(("slab", "tile"), None),
        P(("slab", "tile")),
    )
    out_specs = P("slab", "tile", None)
    return jax.shard_map(body, mesh=mesh, in_specs=in_specs, out_specs=out_specs, check_vma=False)
```

```python
import math

import jax
import jax.numpy as jnp
import numpy as np
from jax import lax
from jax.experimental import pallas as pl
from jax.experimental.pallas import tpu as pltpu
from jax.sharding import PartitionSpec as P

SIDE = 128
BLOCK = 128
HALO = 32
ANGLES = 16
DEPTH = 64
SLICES_DEV = 8
BLOCKS = 8
SLABS = 16
TILES = 8
FRAMES = 32
FIRST = 38
WIDE = 9 * BLOCK
FWD_FINE, FWD_COARSE = 4, 14
BWD_FINE, BWD_COARSE = 14, 4
OWN_ROWS, EDGE_ROWS = ANGLES * SLICES_DEV, ANGLES // 2 * SLICES_DEV
PAIRS = SLICES_DEV // 2
ROWS = OWN_ROWS + EDGE_ROWS
GROUP = 32
MERGED = 4
UNPACK_UNROLL = 2
VMEM_LIMIT = 40 * 1024 * 1024
ALL_VMEM = 60 * 1024 * 1024

SIN_TERMS = (3.14159264, -5.16771008, 2.55007752, -0.598291286, 0.0776576603)
COS_TERMS = (0.999999953, -4.93479283, 4.05841135, -1.33187657, 0.219689611)


def iota(shape, dim):
    return lax.broadcasted_iota(jnp.int32, shape, dim)


def poly(terms, t):
    total = jnp.full_like(t, terms[-1])
    for term in reversed(terms[:-1]):
        total = total * t + term
    return total


def sine_and_cosine(turns):
    t = turns * turns
    half_sin = turns * poly(SIN_TERMS, t)
    half_cos = poly(COS_TERMS, t)
    return (2.0 * half_sin * half_cos, 1.0 - 2.0 * half_sin * half_sin)


def pick_rows(values, shape, dim, period):
    index = iota(shape, dim) % period
    total = jnp.zeros(shape, values[0].dtype)
    for i, value in enumerate(values):
        total = jnp.where(index == i, value, total)
    return total


def bell(offset, centre):
    spread = offset - centre
    return jnp.exp(-0.5 * spread * spread).astype(jnp.bfloat16)


def left(value, steps):
    return pltpu.roll(value, value.shape[1] - steps, 1)


def project_kernel(shears_in, shifts_in, volume_in, out, table, stack, volume, gathered, shears, shifts, sems):
    copies = [
        pltpu.make_async_copy(shears_in, shears, sems.at[0]),
        pltpu.make_async_copy(shifts_in, shifts, sems.at[1]),
    ]
    for p in range(PAIRS):
        part = pl.ds(p * 2, 2)
        copies.append(pltpu.make_async_copy(volume_in.at[part], volume.at[part], sems.at[2 + p]))
    for copy in copies:
        copy.start()
    copies[0].wait()
    shape = (ANGLES, FWD_FINE * DEPTH)
    shear = pick_rows([shears[i] for i in range(ANGLES)], shape, 0, ANGLES)
    lane = iota(shape, 1)
    beam = (lane % DEPTH).astype(jnp.float32)
    centre = BLOCK * 0.5 + (beam - (DEPTH - 1) * 0.5) * shear
    fine = (lane // DEPTH).astype(jnp.float32)
    for j in range(FWD_COARSE):
        table[j * ANGLES : (j + 1) * ANGLES] = bell(fine + float(FIRST + FWD_FINE * j), centre)
    copies[1].wait()
    shape = (ANGLES, BLOCK)
    shift = pick_rows([shifts[i] for i in range(ANGLES)], shape, 0, ANGLES)
    lane = iota((8, BLOCK), 1)
    full_lane = iota(shape, 1)
    outer = (lane < HALO) | (lane >= BLOCK - HALO)
    zero = jnp.zeros(shape, jnp.float32)
    def build(p):
        copies[2 + p].wait()
        for half in range(2):
            rows = jnp.concatenate(
                [volume[p * 2 + half], jnp.zeros((DEPTH, WIDE - BLOCKS * BLOCK), jnp.float32)], axis=1
            ).astype(jnp.bfloat16)
            for r in range(FWD_FINE):
                moved = rows if r == 0 else jnp.concatenate([rows[:, WIDE - r :], rows[:, : WIDE - r]], axis=1)
                stack[p, r * DEPTH : (r + 1) * DEPTH, half * WIDE : (half + 1) * WIDE] = moved

    def finish(p):
        fixed = []
        for n in range(WIDE // BLOCK):
            sums = jnp.dot(table[...], stack[p, :, n * 2 * BLOCK : (n + 1) * 2 * BLOCK], preferred_element_type=jnp.float32)
            for b in range(2):
                rolled = [
                    pltpu.roll(sums[j * ANGLES : (j + 1) * ANGLES, b * BLOCK : (b + 1) * BLOCK], FIRST + FWD_FINE * j, 1)
                    for j in range(FWD_COARSE)
                ]
                if (2 * n + b) % (BLOCKS + 1) == 0:
                    before = [zero] * FWD_COARSE
                total = jnp.where(full_lane >= FIRST, rolled[0], before[0])
                for j in range(1, FWD_COARSE):
                    total = total + jnp.where(full_lane >= FIRST + FWD_FINE * j, rolled[j], before[j])
                before = rolled
                turns = total * (1.0 / (2.0 * math.pi))
                turns = turns - jnp.floor(turns + 0.5)
                fixed.append(jnp.minimum(jnp.floor(turns * 65536.0 + 0.5), 32767.0))
        for half in range(2):
            block = [zero] + fixed[half * (BLOCKS + 1) : (half + 1) * (BLOCKS + 1)] + [zero]
            placed = []
            for k in range(BLOCKS):
                here = jnp.where(shift == 0, block[k + 1], jnp.where(shift > 0, block[k], block[k + 2]))
                placed.append(here)
            around = [zero] + placed + [zero]
            s = p * 2 + half
            for k in range(BLOCKS):
                gathered[k, pl.ds(s, ANGLES, stride=SLICES_DEV), :] = placed[k]
                after, before = around[k + 2], around[k]
                low = jnp.where(lane < HALO, after[:8], before[:8])
                high = jnp.where(lane < HALO, after[8:], before[8:])
                edge = jnp.where(outer, low, pltpu.roll(high, BLOCK // 2, 1))
                gathered[k, pl.ds(OWN_ROWS + s, ANGLES // 2, stride=SLICES_DEV), :] = edge

    build(0)
    for p in range(PAIRS):
        if p + 1 < PAIRS:
            build(p + 1)
        finish(p)
    for k in range(BLOCKS):
        out[k] = gathered[k, :ROWS].astype(jnp.int32).astype(jnp.int16)


def project(shears, shifts, volume):
    hbm = pl.BlockSpec(memory_space=pltpu.HBM)
    return pl.pallas_call(
        project_kernel,
        name="project",
        in_specs=[hbm, hbm, hbm],
        out_specs=pl.BlockSpec(memory_space=pltpu.VMEM),
        out_shape=jax.ShapeDtypeStruct((TILES, ROWS, BLOCK), jnp.int16),
        scratch_shapes=[
            pltpu.VMEM((FWD_COARSE * ANGLES, FWD_FINE * DEPTH), jnp.bfloat16),
            pltpu.VMEM((PAIRS, FWD_FINE * DEPTH, 2 * WIDE), jnp.bfloat16),
            pltpu.VMEM((SLICES_DEV, DEPTH, BLOCKS * BLOCK), jnp.float32),
            pltpu.VMEM((BLOCKS, ROWS + SLICES_DEV, BLOCK), jnp.float32),
            pltpu.SMEM((ANGLES,), jnp.float32),
            pltpu.SMEM((ANGLES,), jnp.int32),
            pltpu.SemaphoreType.DMA((2 + PAIRS,)),
        ],
        compiler_params=pltpu.CompilerParams(vmem_limit_bytes=ALL_VMEM),
    )(shears, shifts, volume)


def frames_kernel(
    parity, owners_in, shifts_in, near_phases, far_phases, probe, measured, spread, gather,
    near_out, far_out, own, edge, own_sum, edge_sum, owners, shifts, sems,
):
    copies = [
        pltpu.make_async_copy(owners_in, owners, sems.at[0]),
        pltpu.make_async_copy(shifts_in, shifts, sems.at[1]),
    ]
    for copy in copies:
        copy.start()
    lane = iota((8, BLOCK), 1)
    outer = (lane < HALO) | (lane >= BLOCK - HALO)
    core = parity[0]

    def unpack(chip, carried):
        for which, phases in ((core, near_phases), (1 - core, far_phases)):
            base = pl.multiple_of((chip * 2 + which) * SLICES_DEV, SLICES_DEV)
            rows = phases[chip].astype(jnp.int32).astype(jnp.float32) * (1.0 / 65536.0)
            zero = jnp.zeros((SLICES_DEV, BLOCK), jnp.float32)
            for i in range(ANGLES):
                here = pl.ds(base + i * SIDE, SLICES_DEV)
                first = OWN_ROWS + i % (ANGLES // 2) * SLICES_DEV
                packed = rows[first : first + SLICES_DEV]
                own[here, :] = rows[i * SLICES_DEV : (i + 1) * SLICES_DEV]
                edge[here, :] = packed if i < ANGLES // 2 else pltpu.roll(packed, BLOCK // 2, 1)
                own_sum[here, :] = zero
                edge_sum[here, :] = zero
        return carried

    lax.fori_loop(0, SLABS // 2, unpack, 0, unroll=UNPACK_UNROLL)
    for copy in copies:
        copy.wait()

    power = probe[0] * probe[0] + probe[1] * probe[1]
    sample = measured[0, 0:16].astype(jnp.float32)
    for k in range(4, FRAMES, 4):
        sample = sample + measured[k, k * 4 % SIDE : k * 4 % SIDE + 16].astype(jnp.float32)
    share = lax.rsqrt(jnp.mean(power, axis=(0, 1), keepdims=True) + 0.25)
    share = share * jnp.mean(sample, axis=(0, 1), keepdims=True) * (0.75 / (FRAMES // 4))

    def tiled(value):
        return value.reshape(SIDE // 8, 8, BLOCK)

    def turned(value):
        top = jnp.concatenate([value[:SIDE, :SIDE], value[SIDE:, :SIDE]], axis=1)
        bottom = jnp.concatenate([value[:SIDE, SIDE:], value[SIDE:, SIDE:]], axis=1)
        return jnp.concatenate([top, bottom], axis=0)

    def across(values, matrix, per_pair):
        results = []
        for first in range(0, len(values), MERGED * per_pair):
            rows = jnp.concatenate(values[first : first + MERGED * per_pair], axis=0)
            product = jnp.dot(rows, matrix[...], preferred_element_type=jnp.float32)
            results += [product[g * 2 * SIDE : (g + 1) * 2 * SIDE] for g in range(MERGED)]
        return results

    def group(step, carried):
        first = step * GROUP
        rows, inside, amount, waves, fields = [], [], [], [], []
        for k in range(GROUP):
            shift = shifts[first + k]
            rows.append(pl.ds(pl.multiple_of(owners[first + k] * SIDE, SIDE), SIDE))
            bound = jnp.where(shift >= 0, shift, shift + BLOCK)
            inside.append((lane >= bound) == (shift >= 0))
            amount.append(bound)
        for k in range(GROUP):
            chosen = jnp.where(inside[k], tiled(own[rows[k], :]), tiled(edge[rows[k], :])).reshape(SIDE, BLOCK)
            turns = pltpu.roll(chosen, lax.rem(BLOCK - amount[k], BLOCK), 1)
            object_im, object_re = sine_and_cosine(turns)
            wave_re = probe[0] * object_re - probe[1] * object_im
            wave_im = probe[0] * object_im + probe[1] * object_re
            waves.append((wave_re, wave_im))
            fields.append(jnp.concatenate([wave_re.astype(jnp.bfloat16), wave_im.astype(jnp.bfloat16)], axis=1))
        pairs = range(GROUP // 2)
        half = across(fields, spread, 2)
        far = [jnp.dot(gather[...], turned(half[g].astype(jnp.bfloat16)), preferred_element_type=jnp.float32) for g in pairs]
        resid = []
        for g in pairs:
            far_re, far_im = far[g][:SIDE], far[g][SIDE:]
            amplitude = jnp.concatenate(
                [measured[first + 2 * g].astype(jnp.float32), measured[first + 2 * g + 1].astype(jnp.float32)], axis=1
            )
            ratio = amplitude * lax.rsqrt(far_re * far_re + far_im * far_im + 0.25)
            factor = share - ratio
            resid.append(
                jnp.concatenate([(far_re * factor).astype(jnp.bfloat16), (far_im * factor).astype(jnp.bfloat16)], axis=0)
            )
        back = [
            jnp.dot(spread[...], resid[g], preferred_element_type=jnp.float32) for g in pairs
        ]
        near = across([turned(back[g].astype(jnp.bfloat16)) for g in pairs], gather, 1)
        grads = []
        for k in range(GROUP):
            part = near[k // 2][(k % 2) * SIDE : (k % 2 + 1) * SIDE]
            wave_re, wave_im = waves[k]
            grads.append(pltpu.roll(part[:, SIDE:] * wave_re - part[:, :SIDE] * wave_im, amount[k], 1))
        for k in range(GROUP):
            grad = tiled(grads[k])
            own_sum[rows[k], :] = own_sum[rows[k], :] + jnp.where(inside[k], grad, 0.0).reshape(SIDE, BLOCK)
            edge_sum[rows[k], :] = edge_sum[rows[k], :] + jnp.where(inside[k], 0.0, grad).reshape(SIDE, BLOCK)
        return carried

    lax.fori_loop(0, FRAMES // GROUP, group, 0)

    def pack(chip, carried):
        for which, out in ((core, near_out), (1 - core, far_out)):
            base = pl.multiple_of((chip * 2 + which) * SLICES_DEV, SLICES_DEV)
            here = [pl.ds(base + i * SIDE, SLICES_DEV) for i in range(ANGLES)]
            rows = [own_sum[here[i], :] for i in range(ANGLES)]
            for i in range(ANGLES // 2):
                high = pltpu.roll(edge_sum[here[i + ANGLES // 2], :], BLOCK // 2, 1)
                rows.append(jnp.where(outer, edge_sum[here[i], :], high))
            out[chip] = jnp.concatenate(rows, axis=0).astype(jnp.bfloat16)
        return carried

    lax.fori_loop(0, SLABS // 2, pack, 0, unroll=UNPACK_UNROLL)


def frame_gradients(parity, owners, shifts, near_phases, far_phases, probe, measured, spread, gather):
    smem = pl.BlockSpec(memory_space=pltpu.SMEM)
    hbm = pl.BlockSpec(memory_space=pltpu.HBM)
    vmem = pl.BlockSpec(memory_space=pltpu.VMEM)
    table = pltpu.VMEM((SLABS * SLICES_DEV * ANGLES, BLOCK), jnp.float32)
    half = jax.ShapeDtypeStruct((SLABS // 2, ROWS, BLOCK), jnp.bfloat16)
    return pl.pallas_call(
        frames_kernel,
        name="frame_gradients",
        in_specs=[smem, hbm, hbm, vmem, vmem, vmem, vmem, vmem, vmem],
        out_specs=[vmem, vmem],
        out_shape=[half, half],
        scratch_shapes=[
            table, table, table, table,
            pltpu.SMEM((FRAMES,), jnp.int32), pltpu.SMEM((FRAMES,), jnp.int32), pltpu.SemaphoreType.DMA((2,)),
        ],
        compiler_params=pltpu.CompilerParams(vmem_limit_bytes=VMEM_LIMIT),
    )(parity, owners, shifts, near_phases, far_phases, probe, measured, spread, gather)


def back_kernel(shears_in, shifts_in, tiles, out_hbm, table, stack, out, gathered, shears, shifts, sems):
    copies = [
        pltpu.make_async_copy(shears_in, shears, sems.at[0]),
        pltpu.make_async_copy(shifts_in, shifts, sems.at[1]),
    ]
    for copy in copies:
        copy.start()
    copies[0].wait()
    shape = (DEPTH, BWD_FINE * ANGLES)
    shear = pick_rows([shears[i] for i in range(ANGLES)], shape, 1, ANGLES)
    beam = iota(shape, 0).astype(jnp.float32)
    centre = BLOCK * 0.5 + (beam - (DEPTH - 1) * 0.5) * shear
    fine = (iota(shape, 1) // ANGLES).astype(jnp.float32)
    for j in range(BWD_COARSE):
        table[j * DEPTH : (j + 1) * DEPTH] = bell(fine + float(FIRST + BWD_FINE * j), centre)
    copies[1].wait()
    shape = (ANGLES, BLOCK)
    shift = pick_rows([shifts[i] for i in range(ANGLES)], shape, 0, ANGLES)
    lane = iota(shape, 1)
    zero = jnp.zeros(shape, jnp.float32)
    sends = []
    for k in range(TILES):
        gathered[k, :ROWS] = tiles[k].astype(jnp.float32)
    def build(p):
        for half in range(2):
            own, margin = [], []
            for k in range(TILES):
                s = p * 2 + half
                own.append(gathered[k, pl.ds(s, ANGLES, stride=SLICES_DEV), :])
                packed = gathered[k, pl.ds(OWN_ROWS + s, ANGLES // 2, stride=SLICES_DEV), :]
                margin.append(jnp.concatenate([packed, pltpu.roll(packed, BLOCK // 2, 1)], axis=0))
            whole = []
            for k in range(TILES):
                total = own[k]
                if k > 0:
                    total = total + jnp.where(lane < HALO, margin[k - 1], 0.0)
                if k < TILES - 1:
                    total = total + jnp.where(lane >= BLOCK - HALO, margin[k + 1], 0.0)
                whole.append(total.astype(jnp.bfloat16).astype(jnp.float32))
            whole = [zero] + whole + [zero, zero]
            placed = jnp.concatenate(
                [
                    jnp.where(shift == 0, whole[k + 1], jnp.where(shift > 0, whole[k + 2], whole[k]))
                    for k in range(BLOCKS + 1)
                ],
                axis=1,
            ).astype(jnp.bfloat16)
            for r in range(BWD_FINE):
                moved = jnp.concatenate([placed[:, FIRST + r :], placed[:, : FIRST + r]], axis=1)
                stack[p, r * ANGLES : (r + 1) * ANGLES, half * WIDE : (half + 1) * WIDE] = moved

    def finish(p):
        both = jnp.dot(table[...], stack[p], preferred_element_type=jnp.float32)
        for half in range(2):
            sums = both[:, half * WIDE : (half + 1) * WIDE]
            total = sums[0:DEPTH]
            for j in range(1, BWD_COARSE):
                total = total + left(sums[j * DEPTH : (j + 1) * DEPTH], BWD_FINE * j)
            out[p * 2 + half] = total[:, : BLOCKS * BLOCK]
        part = pl.ds(p * 2, 2)
        sends.append(pltpu.make_async_copy(out.at[part], out_hbm.at[part], sems.at[2 + p]))
        sends[-1].start()

    for p in range(PAIRS):
        build(p)
    for p in range(PAIRS):
        finish(p)
    for send in sends:
        send.wait()


def back_project(shears, shifts, tiles):
    hbm = pl.BlockSpec(memory_space=pltpu.HBM)
    return pl.pallas_call(
        back_kernel,
        name="back_project",
        in_specs=[hbm, hbm, pl.BlockSpec(memory_space=pltpu.VMEM)],
        out_specs=hbm,
        out_shape=jax.ShapeDtypeStruct((SLICES_DEV, DEPTH, BLOCKS * BLOCK), jnp.float32),
        scratch_shapes=[
            pltpu.VMEM((BWD_COARSE * DEPTH, BWD_FINE * ANGLES), jnp.bfloat16),
            pltpu.VMEM((PAIRS, BWD_FINE * ANGLES, 2 * WIDE), jnp.bfloat16),
            pltpu.VMEM((SLICES_DEV, DEPTH, BLOCKS * BLOCK), jnp.float32),
            pltpu.VMEM((TILES, ROWS + SLICES_DEV, BLOCK), jnp.float32),
            pltpu.SMEM((ANGLES,), jnp.float32),
            pltpu.SMEM((ANGLES,), jnp.int32),
            pltpu.SemaphoreType.DMA((2 + PAIRS,)),
        ],
        compiler_params=pltpu.CompilerParams(vmem_limit_bytes=VMEM_LIMIT),
    )(shears, shifts, tiles)


def dft_matrices():
    index = np.arange(SIDE)
    phase = (np.outer(index, index) % SIDE) * (2.0 * np.pi / SIDE)
    cos, sin = np.cos(phase), np.sin(phase)
    spread = np.block([[cos, -sin], [sin, cos]])
    gather = np.block([[cos, sin], [-sin, cos]]) / SIDE
    return jnp.asarray(spread, jnp.bfloat16), jnp.asarray(gather, jnp.bfloat16)


def copies_of(value, count):
    return jnp.broadcast_to(value, (count, *value.shape))


def between_chips(value):
    count = lax.axis_size("slab")
    groups = [list(range(core, count, 2)) for core in range(2)]
    return lax.all_to_all(value, "slab", 0, 0, tiled=True, axis_index_groups=groups)


def between_cores(value):
    return lax.ppermute(value, "slab", [(i, i ^ 1) for i in range(lax.axis_size("slab"))])


def body(volume, shears, tile_shift, illumination, measured, frame_owner, frame_shift):
    spread, gather = dft_matrices()
    shifts = tile_shift.reshape(ANGLES)
    parity = (lax.axis_index("slab") % 2).astype(jnp.int32).reshape(1)
    partials = project(shears, shifts, volume)
    landed = lax.all_to_all(partials, "tile", 0, 0, tiled=True)
    phase = jnp.sum(landed.astype(jnp.int32), axis=0)
    phase = (((phase + 32768) & 65535) - 32768).astype(jnp.int16)
    near_phases = between_chips(copies_of(phase, SLABS // 2))
    far_phases = between_cores(near_phases)
    near_grads, far_grads = frame_gradients(
        parity, frame_owner.reshape(FRAMES), frame_shift, near_phases, far_phases, illumination, measured, spread, gather
    )
    grads = near_grads.astype(jnp.float32) + between_cores(far_grads).astype(jnp.float32)
    landed = between_chips(grads.astype(jnp.bfloat16)).astype(jnp.float32)
    grad = landed[0]
    for i in range(1, SLABS // 2):
        grad = grad + landed[i]
    tiles = lax.all_to_all(copies_of(grad.astype(jnp.bfloat16), TILES), "tile", 0, 0, tiled=True)
    return back_project(shears, shifts, tiles)


def solution(mesh):
    in_specs = (
        P("slab", "tile", None),
        P(),
        P(None, "tile"),
        P(),
        P(("slab", "tile"), None, None),
        P(("slab", "tile"), None),
        P(("slab", "tile")),
    )
    out_specs = P("slab", "tile", None)
    return jax.shard_map(body, mesh=mesh, in_specs=in_specs, out_specs=out_specs, check_vma=False)
```

```python
import math

import jax
import jax.numpy as jnp
import numpy as np
from jax import lax
from jax.experimental import pallas as pl
from jax.experimental.pallas import tpu as pltpu
from jax.sharding import PartitionSpec as P

SIDE = 128
BLOCK = 128
HALO = 32
ANGLES = 16
DEPTH = 64
SLICES_DEV = 8
BLOCKS = 8
SLABS = 16
TILES = 8
FRAMES = 32
FIRST = 38
WIDE = 9 * BLOCK
FWD_FINE, FWD_COARSE = 4, 14
BWD_FINE, BWD_COARSE = 14, 4
OWN_ROWS, EDGE_ROWS = ANGLES * SLICES_DEV, ANGLES // 2 * SLICES_DEV
PAIRS = SLICES_DEV // 2
ROWS = OWN_ROWS + EDGE_ROWS
GROUP = 32
MERGED = 4
UNPACK_UNROLL = 2
VMEM_LIMIT = 40 * 1024 * 1024
ALL_VMEM = 60 * 1024 * 1024

SIN_TERMS = (3.14159264, -5.16771008, 2.55007752, -0.598291286, 0.0776576603)
COS_TERMS = (0.999999953, -4.93479283, 4.05841135, -1.33187657, 0.219689611)


def iota(shape, dim):
    return lax.broadcasted_iota(jnp.int32, shape, dim)


def poly(terms, t):
    total = jnp.full_like(t, terms[-1])
    for term in reversed(terms[:-1]):
        total = total * t + term
    return total


def sine_and_cosine(turns):
    t = turns * turns
    half_sin = turns * poly(SIN_TERMS, t)
    half_cos = poly(COS_TERMS, t)
    return (2.0 * half_sin * half_cos, 1.0 - 2.0 * half_sin * half_sin)


def pick_rows(values, shape, dim, period):
    index = iota(shape, dim) % period
    total = jnp.zeros(shape, values[0].dtype)
    for i, value in enumerate(values):
        total = jnp.where(index == i, value, total)
    return total


def bell(offset, centre):
    spread = offset - centre
    return jnp.exp(-0.5 * spread * spread).astype(jnp.bfloat16)


def left(value, steps):
    return pltpu.roll(value, value.shape[1] - steps, 1)


def project_kernel(shears_in, shifts_in, volume_in, out, table, stack, volume, gathered, shears, shifts, sems):
    copies = [
        pltpu.make_async_copy(shears_in, shears, sems.at[0]),
        pltpu.make_async_copy(shifts_in, shifts, sems.at[1]),
    ]
    for p in range(PAIRS):
        part = pl.ds(p * 2, 2)
        copies.append(pltpu.make_async_copy(volume_in.at[part], volume.at[part], sems.at[2 + p]))
    for copy in copies:
        copy.start()
    copies[0].wait()
    shape = (ANGLES, FWD_FINE * DEPTH)
    shear = pick_rows([shears[i] for i in range(ANGLES)], shape, 0, ANGLES)
    lane = iota(shape, 1)
    beam = (lane % DEPTH).astype(jnp.float32)
    centre = BLOCK * 0.5 + (beam - (DEPTH - 1) * 0.5) * shear
    fine = (lane // DEPTH).astype(jnp.float32)
    for j in range(FWD_COARSE):
        table[j * ANGLES : (j + 1) * ANGLES] = bell(fine + float(FIRST + FWD_FINE * j), centre)
    copies[1].wait()
    shape = (ANGLES, BLOCK)
    shift = pick_rows([shifts[i] for i in range(ANGLES)], shape, 0, ANGLES)
    lane = iota((8, BLOCK), 1)
    full_lane = iota(shape, 1)
    outer = (lane < HALO) | (lane >= BLOCK - HALO)
    zero = jnp.zeros(shape, jnp.float32)
    def build(p):
        copies[2 + p].wait()
        for half in range(2):
            rows = jnp.concatenate(
                [volume[p * 2 + half], jnp.zeros((DEPTH, WIDE - BLOCKS * BLOCK), jnp.float32)], axis=1
            ).astype(jnp.bfloat16)
            for r in range(FWD_FINE):
                moved = rows if r == 0 else jnp.concatenate([rows[:, WIDE - r :], rows[:, : WIDE - r]], axis=1)
                stack[p, r * DEPTH : (r + 1) * DEPTH, half * WIDE : (half + 1) * WIDE] = moved

    def finish(p):
        fixed = []
        for n in range(WIDE // BLOCK):
            sums = jnp.dot(table[...], stack[p, :, n * 2 * BLOCK : (n + 1) * 2 * BLOCK], preferred_element_type=jnp.float32)
            for b in range(2):
                rolled = [
                    pltpu.roll(sums[j * ANGLES : (j + 1) * ANGLES, b * BLOCK : (b + 1) * BLOCK], FIRST + FWD_FINE * j, 1)
                    for j in range(FWD_COARSE)
                ]
                if (2 * n + b) % (BLOCKS + 1) == 0:
                    before = [zero] * FWD_COARSE
                total = jnp.where(full_lane >= FIRST, rolled[0], before[0])
                for j in range(1, FWD_COARSE):
                    total = total + jnp.where(full_lane >= FIRST + FWD_FINE * j, rolled[j], before[j])
                before = rolled
                turns = total * (1.0 / (2.0 * math.pi))
                turns = turns - jnp.floor(turns + 0.5)
                fixed.append(jnp.minimum(jnp.floor(turns * 65536.0 + 0.5), 32767.0))
        for half in range(2):
            block = [zero] + fixed[half * (BLOCKS + 1) : (half + 1) * (BLOCKS + 1)] + [zero]
            placed = []
            for k in range(BLOCKS):
                here = jnp.where(shift == 0, block[k + 1], jnp.where(shift > 0, block[k], block[k + 2]))
                placed.append(here)
            around = [zero] + placed + [zero]
            s = p * 2 + half
            for k in range(BLOCKS):
                gathered[k, pl.ds(s, ANGLES, stride=SLICES_DEV), :] = placed[k]
                after, before = around[k + 2], around[k]
                low = jnp.where(lane < HALO, after[:8], before[:8])
                high = jnp.where(lane < HALO, after[8:], before[8:])
                edge = jnp.where(outer, low, pltpu.roll(high, BLOCK // 2, 1))
                gathered[k, pl.ds(OWN_ROWS + s, ANGLES // 2, stride=SLICES_DEV), :] = edge

    build(0)
    for p in range(PAIRS):
        if p + 1 < PAIRS:
            build(p + 1)
        finish(p)
    for k in range(BLOCKS):
        out[k] = gathered[k, :ROWS].astype(jnp.int32).astype(jnp.int16)


def project(shears, shifts, volume):
    hbm = pl.BlockSpec(memory_space=pltpu.HBM)
    return pl.pallas_call(
        project_kernel,
        name="project",
        in_specs=[hbm, hbm, hbm],
        out_specs=pl.BlockSpec(memory_space=pltpu.VMEM),
        out_shape=jax.ShapeDtypeStruct((TILES, ROWS, BLOCK), jnp.int16),
        scratch_shapes=[
            pltpu.VMEM((FWD_COARSE * ANGLES, FWD_FINE * DEPTH), jnp.bfloat16),
            pltpu.VMEM((PAIRS, FWD_FINE * DEPTH, 2 * WIDE), jnp.bfloat16),
            pltpu.VMEM((SLICES_DEV, DEPTH, BLOCKS * BLOCK), jnp.float32),
            pltpu.VMEM((BLOCKS, ROWS + SLICES_DEV, BLOCK), jnp.float32),
            pltpu.SMEM((ANGLES,), jnp.float32),
            pltpu.SMEM((ANGLES,), jnp.int32),
            pltpu.SemaphoreType.DMA((2 + PAIRS,)),
        ],
        compiler_params=pltpu.CompilerParams(vmem_limit_bytes=ALL_VMEM),
    )(shears, shifts, volume)


def frames_kernel(
    parity, owners_in, shifts_in, near_phases, far_phases, probe, measured, spread, gather,
    near_out, far_out, own, edge, own_sum, edge_sum, owners, shifts, sems,
):
    copies = [
        pltpu.make_async_copy(owners_in, owners, sems.at[0]),
        pltpu.make_async_copy(shifts_in, shifts, sems.at[1]),
    ]
    for copy in copies:
        copy.start()
    lane = iota((8, BLOCK), 1)
    outer = (lane < HALO) | (lane >= BLOCK - HALO)
    core = parity[0]

    def unpack(chip, carried):
        for which, phases in ((core, near_phases), (1 - core, far_phases)):
            base = pl.multiple_of((chip * 2 + which) * SLICES_DEV, SLICES_DEV)
            rows = phases[chip].astype(jnp.int32).astype(jnp.float32) * (1.0 / 65536.0)
            zero = jnp.zeros((SLICES_DEV, BLOCK), jnp.float32)
            for i in range(ANGLES):
                here = pl.ds(base + i * SIDE, SLICES_DEV)
                first = OWN_ROWS + i % (ANGLES // 2) * SLICES_DEV
                packed = rows[first : first + SLICES_DEV]
                own[here, :] = rows[i * SLICES_DEV : (i + 1) * SLICES_DEV]
                edge[here, :] = packed if i < ANGLES // 2 else pltpu.roll(packed, BLOCK // 2, 1)
                own_sum[here, :] = zero
                edge_sum[here, :] = zero
        return carried

    lax.fori_loop(0, SLABS // 2, unpack, 0, unroll=UNPACK_UNROLL)
    for copy in copies:
        copy.wait()

    power = probe[0] * probe[0] + probe[1] * probe[1]
    sample = measured[0, 0:16].astype(jnp.float32)
    for k in range(4, FRAMES, 4):
        sample = sample + measured[k, k * 4 % SIDE : k * 4 % SIDE + 16].astype(jnp.float32)
    share = lax.rsqrt(jnp.mean(power, axis=(0, 1), keepdims=True) + 0.25)
    share = share * jnp.mean(sample, axis=(0, 1), keepdims=True) * (0.75 / (FRAMES // 4))

    def tiled(value):
        return value.reshape(SIDE // 8, 8, BLOCK)

    def turned(value):
        top = jnp.concatenate([value[:SIDE, :SIDE], value[SIDE:, :SIDE]], axis=1)
        bottom = jnp.concatenate([value[:SIDE, SIDE:], value[SIDE:, SIDE:]], axis=1)
        return jnp.concatenate([top, bottom], axis=0)

    def across(values, matrix, per_pair):
        results = []
        for first in range(0, len(values), MERGED * per_pair):
            rows = jnp.concatenate(values[first : first + MERGED * per_pair], axis=0)
            product = jnp.dot(rows, matrix[...], preferred_element_type=jnp.float32)
            results += [product[g * 2 * SIDE : (g + 1) * 2 * SIDE] for g in range(MERGED)]
        return results

    def group(step, carried):
        first = step * GROUP
        rows, inside, amount, waves, fields = [], [], [], [], []
        for k in range(GROUP):
            shift = shifts[first + k]
            rows.append(pl.ds(pl.multiple_of(owners[first + k] * SIDE, SIDE), SIDE))
            bound = jnp.where(shift >= 0, shift, shift + BLOCK)
            inside.append((lane >= bound) == (shift >= 0))
            amount.append(bound)
        for k in range(GROUP):
            chosen = jnp.where(inside[k], tiled(own[rows[k], :]), tiled(edge[rows[k], :])).reshape(SIDE, BLOCK)
            turns = pltpu.roll(chosen, lax.rem(BLOCK - amount[k], BLOCK), 1)
            object_im, object_re = sine_and_cosine(turns)
            wave_re = probe[0] * object_re - probe[1] * object_im
            wave_im = probe[0] * object_im + probe[1] * object_re
            waves.append((wave_re, wave_im))
            fields.append(jnp.concatenate([wave_re.astype(jnp.bfloat16), wave_im.astype(jnp.bfloat16)], axis=1))
        pairs = range(GROUP // 2)
        half = across(fields, spread, 2)
        far = [jnp.dot(gather[...], turned(half[g].astype(jnp.bfloat16)), preferred_element_type=jnp.float32) for g in pairs]
        resid = []
        for g in pairs:
            far_re, far_im = far[g][:SIDE], far[g][SIDE:]
            amplitude = jnp.concatenate(
                [measured[first + 2 * g].astype(jnp.float32), measured[first + 2 * g + 1].astype(jnp.float32)], axis=1
            )
            ratio = amplitude * lax.rsqrt(far_re * far_re + far_im * far_im + 0.25)
            factor = share - ratio
            resid.append(
                jnp.concatenate([(far_re * factor).astype(jnp.bfloat16), (far_im * factor).astype(jnp.bfloat16)], axis=0)
            )
        back = [
            jnp.dot(spread[...], resid[g], preferred_element_type=jnp.float32) for g in pairs
        ]
        near = across([turned(back[g].astype(jnp.bfloat16)) for g in pairs], gather, 1)
        grads = []
        for k in range(GROUP):
            part = near[k // 2][(k % 2) * SIDE : (k % 2 + 1) * SIDE]
            wave_re, wave_im = waves[k]
            grads.append(pltpu.roll(part[:, SIDE:] * wave_re - part[:, :SIDE] * wave_im, amount[k], 1))
        for k in range(GROUP):
            grad = tiled(grads[k])
            own_sum[rows[k], :] = own_sum[rows[k], :] + jnp.where(inside[k], grad, 0.0).reshape(SIDE, BLOCK)
            edge_sum[rows[k], :] = edge_sum[rows[k], :] + jnp.where(inside[k], 0.0, grad).reshape(SIDE, BLOCK)
        return carried

    lax.fori_loop(0, FRAMES // GROUP, group, 0)

    def pack(chip, carried):
        for which, out in ((core, near_out), (1 - core, far_out)):
            base = pl.multiple_of((chip * 2 + which) * SLICES_DEV, SLICES_DEV)
            here = [pl.ds(base + i * SIDE, SLICES_DEV) for i in range(ANGLES)]
            rows = [own_sum[here[i], :] for i in range(ANGLES)]
            for i in range(ANGLES // 2):
                high = pltpu.roll(edge_sum[here[i + ANGLES // 2], :], BLOCK // 2, 1)
                rows.append(jnp.where(outer, edge_sum[here[i], :], high))
            out[chip] = jnp.concatenate(rows, axis=0).astype(jnp.bfloat16)
        return carried

    lax.fori_loop(0, SLABS // 2, pack, 0, unroll=UNPACK_UNROLL)


def frame_gradients(parity, owners, shifts, near_phases, far_phases, probe, measured, spread, gather):
    smem = pl.BlockSpec(memory_space=pltpu.SMEM)
    hbm = pl.BlockSpec(memory_space=pltpu.HBM)
    vmem = pl.BlockSpec(memory_space=pltpu.VMEM)
    table = pltpu.VMEM((SLABS * SLICES_DEV * ANGLES, BLOCK), jnp.float32)
    half = jax.ShapeDtypeStruct((SLABS // 2, ROWS, BLOCK), jnp.bfloat16)
    return pl.pallas_call(
        frames_kernel,
        name="frame_gradients",
        in_specs=[smem, hbm, hbm, vmem, vmem, vmem, vmem, vmem, vmem],
        out_specs=[vmem, vmem],
        out_shape=[half, half],
        scratch_shapes=[
            table, table, table, table,
            pltpu.SMEM((FRAMES,), jnp.int32), pltpu.SMEM((FRAMES,), jnp.int32), pltpu.SemaphoreType.DMA((2,)),
        ],
        compiler_params=pltpu.CompilerParams(vmem_limit_bytes=VMEM_LIMIT),
    )(parity, owners, shifts, near_phases, far_phases, probe, measured, spread, gather)


def back_kernel(shears_in, shifts_in, tiles, out_hbm, table, stack, out, gathered, shears, shifts, sems):
    copies = [
        pltpu.make_async_copy(shears_in, shears, sems.at[0]),
        pltpu.make_async_copy(shifts_in, shifts, sems.at[1]),
    ]
    for copy in copies:
        copy.start()
    copies[0].wait()
    shape = (DEPTH, BWD_FINE * ANGLES)
    shear = pick_rows([shears[i] for i in range(ANGLES)], shape, 1, ANGLES)
    beam = iota(shape, 0).astype(jnp.float32)
    centre = BLOCK * 0.5 + (beam - (DEPTH - 1) * 0.5) * shear
    fine = (iota(shape, 1) // ANGLES).astype(jnp.float32)
    for j in range(BWD_COARSE):
        table[j * DEPTH : (j + 1) * DEPTH] = bell(fine + float(FIRST + BWD_FINE * j), centre)
    copies[1].wait()
    shape = (ANGLES, BLOCK)
    shift = pick_rows([shifts[i] for i in range(ANGLES)], shape, 0, ANGLES)
    lane = iota(shape, 1)
    zero = jnp.zeros(shape, jnp.float32)
    outer = (lane < HALO) | (lane >= BLOCK - HALO)
    from_left = iota((ANGLES // 2, BLOCK), 1) % (BLOCK // 2) < HALO
    empty = jnp.zeros((ANGLES // 2, BLOCK), jnp.float32)
    sends = []
    for k in range(TILES):
        gathered[k, :ROWS] = tiles[k].astype(jnp.float32)
    def build(p):
        for half in range(2):
            own, margin = [], [empty]
            for k in range(TILES):
                s = p * 2 + half
                own.append(gathered[k, pl.ds(s, ANGLES, stride=SLICES_DEV), :])
                margin.append(gathered[k, pl.ds(OWN_ROWS + s, ANGLES // 2, stride=SLICES_DEV), :])
            margin.append(empty)
            whole = []
            for k in range(TILES):
                packed = jnp.where(from_left, margin[k], margin[k + 2])
                added = jnp.concatenate([packed, pltpu.roll(packed, BLOCK // 2, 1)], axis=0)
                total = own[k] + jnp.where(outer, added, 0.0)
                whole.append(total.astype(jnp.bfloat16).astype(jnp.float32))
            whole = [zero] + whole + [zero, zero]
            placed = jnp.concatenate(
                [
                    jnp.where(shift == 0, whole[k + 1], jnp.where(shift > 0, whole[k + 2], whole[k]))
                    for k in range(BLOCKS + 1)
                ],
                axis=1,
            ).astype(jnp.bfloat16)
            for r in range(BWD_FINE):
                moved = jnp.concatenate([placed[:, FIRST + r :], placed[:, : FIRST + r]], axis=1)
                stack[p, r * ANGLES : (r + 1) * ANGLES, half * WIDE : (half + 1) * WIDE] = moved

    def finish(p):
        both = jnp.dot(table[...], stack[p], preferred_element_type=jnp.float32)
        for half in range(2):
            sums = both[:, half * WIDE : (half + 1) * WIDE]
            total = sums[0:DEPTH]
            for j in range(1, BWD_COARSE):
                total = total + left(sums[j * DEPTH : (j + 1) * DEPTH], BWD_FINE * j)
            out[p * 2 + half] = total[:, : BLOCKS * BLOCK]
        part = pl.ds(p * 2, 2)
        sends.append(pltpu.make_async_copy(out.at[part], out_hbm.at[part], sems.at[2 + p]))
        sends[-1].start()

    for p in range(PAIRS):
        build(p)
    for p in range(PAIRS):
        finish(p)
    for send in sends:
        send.wait()


def back_project(shears, shifts, tiles):
    hbm = pl.BlockSpec(memory_space=pltpu.HBM)
    return pl.pallas_call(
        back_kernel,
        name="back_project",
        in_specs=[hbm, hbm, pl.BlockSpec(memory_space=pltpu.VMEM)],
        out_specs=hbm,
        out_shape=jax.ShapeDtypeStruct((SLICES_DEV, DEPTH, BLOCKS * BLOCK), jnp.float32),
        scratch_shapes=[
            pltpu.VMEM((BWD_COARSE * DEPTH, BWD_FINE * ANGLES), jnp.bfloat16),
            pltpu.VMEM((PAIRS, BWD_FINE * ANGLES, 2 * WIDE), jnp.bfloat16),
            pltpu.VMEM((SLICES_DEV, DEPTH, BLOCKS * BLOCK), jnp.float32),
            pltpu.VMEM((TILES, ROWS + SLICES_DEV, BLOCK), jnp.float32),
            pltpu.SMEM((ANGLES,), jnp.float32),
            pltpu.SMEM((ANGLES,), jnp.int32),
            pltpu.SemaphoreType.DMA((2 + PAIRS,)),
        ],
        compiler_params=pltpu.CompilerParams(vmem_limit_bytes=VMEM_LIMIT),
    )(shears, shifts, tiles)


def dft_matrices():
    index = np.arange(SIDE)
    phase = (np.outer(index, index) % SIDE) * (2.0 * np.pi / SIDE)
    cos, sin = np.cos(phase), np.sin(phase)
    spread = np.block([[cos, -sin], [sin, cos]])
    gather = np.block([[cos, sin], [-sin, cos]]) / SIDE
    return jnp.asarray(spread, jnp.bfloat16), jnp.asarray(gather, jnp.bfloat16)


def copies_of(value, count):
    return jnp.broadcast_to(value, (count, *value.shape))


def between_chips(value):
    count = lax.axis_size("slab")
    groups = [list(range(core, count, 2)) for core in range(2)]
    return lax.all_to_all(value, "slab", 0, 0, tiled=True, axis_index_groups=groups)


def between_cores(value):
    return lax.ppermute(value, "slab", [(i, i ^ 1) for i in range(lax.axis_size("slab"))])


def body(volume, shears, tile_shift, illumination, measured, frame_owner, frame_shift):
    spread, gather = dft_matrices()
    shifts = tile_shift.reshape(ANGLES)
    parity = (lax.axis_index("slab") % 2).astype(jnp.int32).reshape(1)
    partials = project(shears, shifts, volume)
    landed = lax.all_to_all(partials, "tile", 0, 0, tiled=True)
    phase = jnp.sum(landed.astype(jnp.int32), axis=0)
    phase = (((phase + 32768) & 65535) - 32768).astype(jnp.int16)
    near_phases = between_chips(copies_of(phase, SLABS // 2))
    far_phases = between_cores(near_phases)
    near_grads, far_grads = frame_gradients(
        parity, frame_owner.reshape(FRAMES), frame_shift, near_phases, far_phases, illumination, measured, spread, gather
    )
    grads = near_grads.astype(jnp.float32) + between_cores(far_grads).astype(jnp.float32)
    landed = between_chips(grads.astype(jnp.bfloat16)).astype(jnp.float32)
    grad = landed[0]
    for i in range(1, SLABS // 2):
        grad = grad + landed[i]
    tiles = lax.all_to_all(copies_of(grad.astype(jnp.bfloat16), TILES), "tile", 0, 0, tiled=True)
    return back_project(shears, shifts, tiles)


def solution(mesh):
    in_specs = (
        P("slab", "tile", None),
        P(),
        P(None, "tile"),
        P(),
        P(("slab", "tile"), None, None),
        P(("slab", "tile"), None),
        P(("slab", "tile")),
    )
    out_specs = P("slab", "tile", None)
    return jax.shard_map(body, mesh=mesh, in_specs=in_specs, out_specs=out_specs, check_vma=False)
```

```python
import math

import jax
import jax.numpy as jnp
import numpy as np
from jax import lax
from jax.experimental import pallas as pl
from jax.experimental.pallas import tpu as pltpu
from jax.sharding import PartitionSpec as P

SIDE = 128
BLOCK = 128
HALO = 32
ANGLES = 16
DEPTH = 64
SLICES_DEV = 8
BLOCKS = 8
SLABS = 16
TILES = 8
FRAMES = 32
FIRST = 38
WIDE = 9 * BLOCK
FWD_FINE, FWD_COARSE = 4, 14
BWD_FINE, BWD_COARSE = 14, 4
OWN_ROWS, EDGE_ROWS = ANGLES * SLICES_DEV, ANGLES // 2 * SLICES_DEV
PAIRS = SLICES_DEV // 2
ROWS = OWN_ROWS + EDGE_ROWS
GROUP = 32
MERGED = 8
UNPACK_UNROLL = 2
VMEM_LIMIT = 40 * 1024 * 1024
ALL_VMEM = 60 * 1024 * 1024

SIN_TERMS = (3.14159264, -5.16771008, 2.55007752, -0.598291286, 0.0776576603)
COS_TERMS = (0.999999953, -4.93479283, 4.05841135, -1.33187657, 0.219689611)


def iota(shape, dim):
    return lax.broadcasted_iota(jnp.int32, shape, dim)


def poly(terms, t):
    total = jnp.full_like(t, terms[-1])
    for term in reversed(terms[:-1]):
        total = total * t + term
    return total


def sine_and_cosine(turns):
    t = turns * turns
    half_sin = turns * poly(SIN_TERMS, t)
    half_cos = poly(COS_TERMS, t)
    return (2.0 * half_sin * half_cos, 1.0 - 2.0 * half_sin * half_sin)


def pick_rows(values, shape, dim, period):
    index = iota(shape, dim) % period
    total = jnp.zeros(shape, values[0].dtype)
    for i, value in enumerate(values):
        total = jnp.where(index == i, value, total)
    return total


def bell(offset, centre):
    spread = offset - centre
    return jnp.exp(-0.5 * spread * spread).astype(jnp.bfloat16)


def left(value, steps):
    return pltpu.roll(value, value.shape[1] - steps, 1)


def project_kernel(shears_in, shifts_in, volume_in, out, table, stack, volume, gathered, shears, shifts, sems):
    copies = [
        pltpu.make_async_copy(shears_in, shears, sems.at[0]),
        pltpu.make_async_copy(shifts_in, shifts, sems.at[1]),
    ]
    for p in range(PAIRS):
        part = pl.ds(p * 2, 2)
        copies.append(pltpu.make_async_copy(volume_in.at[part], volume.at[part], sems.at[2 + p]))
    for copy in copies:
        copy.start()
    copies[0].wait()
    shape = (ANGLES, FWD_FINE * DEPTH)
    shear = pick_rows([shears[i] for i in range(ANGLES)], shape, 0, ANGLES)
    lane = iota(shape, 1)
    beam = (lane % DEPTH).astype(jnp.float32)
    centre = BLOCK * 0.5 + (beam - (DEPTH - 1) * 0.5) * shear
    fine = (lane // DEPTH).astype(jnp.float32)
    for j in range(FWD_COARSE):
        table[j * ANGLES : (j + 1) * ANGLES] = bell(fine + float(FIRST + FWD_FINE * j), centre)
    copies[1].wait()
    shape = (ANGLES, BLOCK)
    shift = pick_rows([shifts[i] for i in range(ANGLES)], shape, 0, ANGLES)
    lane = iota((8, BLOCK), 1)
    full_lane = iota(shape, 1)
    outer = (lane < HALO) | (lane >= BLOCK - HALO)
    zero = jnp.zeros(shape, jnp.float32)
    def build(p):
        copies[2 + p].wait()
        for half in range(2):
            rows = jnp.concatenate(
                [volume[p * 2 + half], jnp.zeros((DEPTH, WIDE - BLOCKS * BLOCK), jnp.float32)], axis=1
            ).astype(jnp.bfloat16)
            for r in range(FWD_FINE):
                moved = rows if r == 0 else jnp.concatenate([rows[:, WIDE - r :], rows[:, : WIDE - r]], axis=1)
                stack[p, r * DEPTH : (r + 1) * DEPTH, half * WIDE : (half + 1) * WIDE] = moved

    def finish(p):
        fixed = []
        for n in range(WIDE // BLOCK):
            sums = jnp.dot(table[...], stack[p, :, n * 2 * BLOCK : (n + 1) * 2 * BLOCK], preferred_element_type=jnp.float32)
            for b in range(2):
                rolled = [
                    pltpu.roll(sums[j * ANGLES : (j + 1) * ANGLES, b * BLOCK : (b + 1) * BLOCK], FIRST + FWD_FINE * j, 1)
                    for j in range(FWD_COARSE)
                ]
                if (2 * n + b) % (BLOCKS + 1) == 0:
                    before = [zero] * FWD_COARSE
                total = jnp.where(full_lane >= FIRST, rolled[0], before[0])
                for j in range(1, FWD_COARSE):
                    total = total + jnp.where(full_lane >= FIRST + FWD_FINE * j, rolled[j], before[j])
                before = rolled
                turns = total * (1.0 / (2.0 * math.pi))
                turns = turns - jnp.floor(turns + 0.5)
                fixed.append(jnp.minimum(jnp.floor(turns * 65536.0 + 0.5), 32767.0))
        for half in range(2):
            block = [zero] + fixed[half * (BLOCKS + 1) : (half + 1) * (BLOCKS + 1)] + [zero]
            placed = []
            for k in range(BLOCKS):
                here = jnp.where(shift == 0, block[k + 1], jnp.where(shift > 0, block[k], block[k + 2]))
                placed.append(here)
            packed = [jnp.where(outer, here[:8], pltpu.roll(here[8:], BLOCK // 2, 1)) for here in placed]
            packed = [zero[:8]] + packed + [zero[:8]]
            s = p * 2 + half
            for k in range(BLOCKS):
                gathered[k, pl.ds(s, ANGLES, stride=SLICES_DEV), :] = placed[k]
                edge = jnp.where(lane % (BLOCK // 2) < HALO, packed[k + 2], packed[k])
                gathered[k, pl.ds(OWN_ROWS + s, ANGLES // 2, stride=SLICES_DEV), :] = edge

    build(0)
    for p in range(PAIRS):
        if p + 1 < PAIRS:
            build(p + 1)
        finish(p)
    for k in range(BLOCKS):
        out[k] = gathered[k, :ROWS].astype(jnp.int32).astype(jnp.int16)


def project(shears, shifts, volume):
    hbm = pl.BlockSpec(memory_space=pltpu.HBM)
    return pl.pallas_call(
        project_kernel,
        name="project",
        in_specs=[hbm, hbm, hbm],
        out_specs=pl.BlockSpec(memory_space=pltpu.VMEM),
        out_shape=jax.ShapeDtypeStruct((TILES, ROWS, BLOCK), jnp.int16),
        scratch_shapes=[
            pltpu.VMEM((FWD_COARSE * ANGLES, FWD_FINE * DEPTH), jnp.bfloat16),
            pltpu.VMEM((PAIRS, FWD_FINE * DEPTH, 2 * WIDE), jnp.bfloat16),
            pltpu.VMEM((SLICES_DEV, DEPTH, BLOCKS * BLOCK), jnp.float32),
            pltpu.VMEM((BLOCKS, ROWS + SLICES_DEV, BLOCK), jnp.float32),
            pltpu.SMEM((ANGLES,), jnp.float32),
            pltpu.SMEM((ANGLES,), jnp.int32),
            pltpu.SemaphoreType.DMA((2 + PAIRS,)),
        ],
        compiler_params=pltpu.CompilerParams(vmem_limit_bytes=ALL_VMEM),
    )(shears, shifts, volume)


def frames_kernel(
    parity, owners_in, shifts_in, near_phases, far_phases, probe, measured, spread, gather,
    near_out, far_out, own, edge, own_sum, edge_sum, owners, shifts, sems,
):
    copies = [
        pltpu.make_async_copy(owners_in, owners, sems.at[0]),
        pltpu.make_async_copy(shifts_in, shifts, sems.at[1]),
    ]
    for copy in copies:
        copy.start()
    lane = iota((8, BLOCK), 1)
    outer = (lane < HALO) | (lane >= BLOCK - HALO)
    core = parity[0]

    def unpack(chip, carried):
        for which, phases in ((core, near_phases), (1 - core, far_phases)):
            base = pl.multiple_of((chip * 2 + which) * SLICES_DEV, SLICES_DEV)
            rows = phases[chip].astype(jnp.int32).astype(jnp.float32) * (1.0 / 65536.0)
            zero = jnp.zeros((SLICES_DEV, BLOCK), jnp.float32)
            for i in range(ANGLES):
                here = pl.ds(base + i * SIDE, SLICES_DEV)
                first = OWN_ROWS + i % (ANGLES // 2) * SLICES_DEV
                packed = rows[first : first + SLICES_DEV]
                own[here, :] = rows[i * SLICES_DEV : (i + 1) * SLICES_DEV]
                edge[here, :] = packed if i < ANGLES // 2 else pltpu.roll(packed, BLOCK // 2, 1)
                own_sum[here, :] = zero
                edge_sum[here, :] = zero
        return carried

    lax.fori_loop(0, SLABS // 2, unpack, 0, unroll=UNPACK_UNROLL)
    for copy in copies:
        copy.wait()

    power = probe[0] * probe[0] + probe[1] * probe[1]
    sample = measured[0, 0:16].astype(jnp.float32)
    for k in range(4, FRAMES, 4):
        sample = sample + measured[k, k * 4 % SIDE : k * 4 % SIDE + 16].astype(jnp.float32)
    share = lax.rsqrt(jnp.mean(power, axis=(0, 1), keepdims=True) + 0.25)
    share = share * jnp.mean(sample, axis=(0, 1), keepdims=True) * (0.75 / (FRAMES // 4))

    def tiled(value):
        return value.reshape(SIDE // 8, 8, BLOCK)

    def turned(value):
        top = jnp.concatenate([value[:SIDE, :SIDE], value[SIDE:, :SIDE]], axis=1)
        bottom = jnp.concatenate([value[:SIDE, SIDE:], value[SIDE:, SIDE:]], axis=1)
        return jnp.concatenate([top, bottom], axis=0)

    def across(values, matrix, per_pair):
        results = []
        for first in range(0, len(values), MERGED * per_pair):
            rows = jnp.concatenate(values[first : first + MERGED * per_pair], axis=0)
            product = jnp.dot(rows, matrix[...], preferred_element_type=jnp.float32)
            results += [product[g * 2 * SIDE : (g + 1) * 2 * SIDE] for g in range(MERGED)]
        return results

    def group(step, carried):
        first = step * GROUP
        rows, inside, amount, waves, fields = [], [], [], [], []
        for k in range(GROUP):
            shift = shifts[first + k]
            rows.append(pl.ds(pl.multiple_of(owners[first + k] * SIDE, SIDE), SIDE))
            bound = jnp.where(shift >= 0, shift, shift + BLOCK)
            inside.append((lane >= bound) == (shift >= 0))
            amount.append(bound)
        for k in range(GROUP):
            chosen = jnp.where(inside[k], tiled(own[rows[k], :]), tiled(edge[rows[k], :])).reshape(SIDE, BLOCK)
            turns = pltpu.roll(chosen, lax.rem(BLOCK - amount[k], BLOCK), 1)
            object_im, object_re = sine_and_cosine(turns)
            wave_re = probe[0] * object_re - probe[1] * object_im
            wave_im = probe[0] * object_im + probe[1] * object_re
            waves.append((wave_re, wave_im))
            fields.append(jnp.concatenate([wave_re.astype(jnp.bfloat16), wave_im.astype(jnp.bfloat16)], axis=1))
        pairs = range(GROUP // 2)
        half = across(fields, spread, 2)
        far = [jnp.dot(gather[...], turned(half[g].astype(jnp.bfloat16)), preferred_element_type=jnp.float32) for g in pairs]
        resid = []
        for g in pairs:
            far_re, far_im = far[g][:SIDE], far[g][SIDE:]
            amplitude = jnp.concatenate(
                [measured[first + 2 * g].astype(jnp.float32), measured[first + 2 * g + 1].astype(jnp.float32)], axis=1
            )
            ratio = amplitude * lax.rsqrt(far_re * far_re + far_im * far_im + 0.25)
            factor = share - ratio
            resid.append(
                jnp.concatenate([(far_re * factor).astype(jnp.bfloat16), (far_im * factor).astype(jnp.bfloat16)], axis=0)
            )
        back = [
            jnp.dot(spread[...], resid[g], preferred_element_type=jnp.float32) for g in pairs
        ]
        near = across([turned(back[g].astype(jnp.bfloat16)) for g in pairs], gather, 1)
        grads = []
        for k in range(GROUP):
            part = near[k // 2][(k % 2) * SIDE : (k % 2 + 1) * SIDE]
            wave_re, wave_im = waves[k]
            grads.append(pltpu.roll(part[:, SIDE:] * wave_re - part[:, :SIDE] * wave_im, amount[k], 1))
        for k in range(GROUP):
            grad = tiled(grads[k])
            own_sum[rows[k], :] = own_sum[rows[k], :] + jnp.where(inside[k], grad, 0.0).reshape(SIDE, BLOCK)
            edge_sum[rows[k], :] = edge_sum[rows[k], :] + jnp.where(inside[k], 0.0, grad).reshape(SIDE, BLOCK)
        return carried

    lax.fori_loop(0, FRAMES // GROUP, group, 0)

    def pack(chip, carried):
        for which, out in ((core, near_out), (1 - core, far_out)):
            base = pl.multiple_of((chip * 2 + which) * SLICES_DEV, SLICES_DEV)
            here = [pl.ds(base + i * SIDE, SLICES_DEV) for i in range(ANGLES)]
            rows = [own_sum[here[i], :] for i in range(ANGLES)]
            for i in range(ANGLES // 2):
                high = pltpu.roll(edge_sum[here[i + ANGLES // 2], :], BLOCK // 2, 1)
                rows.append(jnp.where(outer, edge_sum[here[i], :], high))
            out[chip] = jnp.concatenate(rows, axis=0).astype(jnp.bfloat16)
        return carried

    lax.fori_loop(0, SLABS // 2, pack, 0, unroll=UNPACK_UNROLL)


def frame_gradients(parity, owners, shifts, near_phases, far_phases, probe, measured, spread, gather):
    smem = pl.BlockSpec(memory_space=pltpu.SMEM)
    hbm = pl.BlockSpec(memory_space=pltpu.HBM)
    vmem = pl.BlockSpec(memory_space=pltpu.VMEM)
    table = pltpu.VMEM((SLABS * SLICES_DEV * ANGLES, BLOCK), jnp.float32)
    half = jax.ShapeDtypeStruct((SLABS // 2, ROWS, BLOCK), jnp.bfloat16)
    return pl.pallas_call(
        frames_kernel,
        name="frame_gradients",
        in_specs=[smem, hbm, hbm, vmem, vmem, vmem, vmem, vmem, vmem],
        out_specs=[vmem, vmem],
        out_shape=[half, half],
        scratch_shapes=[
            table, table, table, table,
            pltpu.SMEM((FRAMES,), jnp.int32), pltpu.SMEM((FRAMES,), jnp.int32), pltpu.SemaphoreType.DMA((2,)),
        ],
        compiler_params=pltpu.CompilerParams(vmem_limit_bytes=VMEM_LIMIT),
    )(parity, owners, shifts, near_phases, far_phases, probe, measured, spread, gather)


def back_kernel(shears_in, shifts_in, tiles, out_hbm, table, stack, out, gathered, shears, shifts, sems):
    copies = [
        pltpu.make_async_copy(shears_in, shears, sems.at[0]),
        pltpu.make_async_copy(shifts_in, shifts, sems.at[1]),
    ]
    for copy in copies:
        copy.start()
    copies[0].wait()
    shape = (DEPTH, BWD_FINE * ANGLES)
    shear = pick_rows([shears[i] for i in range(ANGLES)], shape, 1, ANGLES)
    beam = iota(shape, 0).astype(jnp.float32)
    centre = BLOCK * 0.5 + (beam - (DEPTH - 1) * 0.5) * shear
    fine = (iota(shape, 1) // ANGLES).astype(jnp.float32)
    for j in range(BWD_COARSE):
        table[j * DEPTH : (j + 1) * DEPTH] = bell(fine + float(FIRST + BWD_FINE * j), centre)
    copies[1].wait()
    shape = (ANGLES, BLOCK)
    shift = pick_rows([shifts[i] for i in range(ANGLES)], shape, 0, ANGLES)
    lane = iota(shape, 1)
    zero = jnp.zeros(shape, jnp.float32)
    sends = []
    for k in range(TILES):
        gathered[k, :ROWS] = tiles[k].astype(jnp.float32)
    def build(p):
        for half in range(2):
            own, margin = [], []
            for k in range(TILES):
                s = p * 2 + half
                own.append(gathered[k, pl.ds(s, ANGLES, stride=SLICES_DEV), :])
                packed = gathered[k, pl.ds(OWN_ROWS + s, ANGLES // 2, stride=SLICES_DEV), :]
                margin.append(jnp.concatenate([packed, pltpu.roll(packed, BLOCK // 2, 1)], axis=0))
            whole = []
            for k in range(TILES):
                total = own[k]
                if k > 0:
                    total = total + jnp.where(lane < HALO, margin[k - 1], 0.0)
                if k < TILES - 1:
                    total = total + jnp.where(lane >= BLOCK - HALO, margin[k + 1], 0.0)
                whole.append(total.astype(jnp.bfloat16).astype(jnp.float32))
            whole = [zero] + whole + [zero, zero]
            placed = jnp.concatenate(
                [
                    jnp.where(shift == 0, whole[k + 1], jnp.where(shift > 0, whole[k + 2], whole[k]))
                    for k in range(BLOCKS + 1)
                ],
                axis=1,
            ).astype(jnp.bfloat16)
            for r in range(BWD_FINE):
                moved = jnp.concatenate([placed[:, FIRST + r :], placed[:, : FIRST + r]], axis=1)
                stack[p, r * ANGLES : (r + 1) * ANGLES, half * WIDE : (half + 1) * WIDE] = moved

    def finish(p):
        both = jnp.dot(table[...], stack[p], preferred_element_type=jnp.float32)
        for half in range(2):
            sums = both[:, half * WIDE : (half + 1) * WIDE]
            total = sums[0:DEPTH]
            for j in range(1, BWD_COARSE):
                total = total + left(sums[j * DEPTH : (j + 1) * DEPTH], BWD_FINE * j)
            out[p * 2 + half] = total[:, : BLOCKS * BLOCK]
        part = pl.ds(p * 2, 2)
        sends.append(pltpu.make_async_copy(out.at[part], out_hbm.at[part], sems.at[2 + p]))
        sends[-1].start()

    for p in range(PAIRS):
        build(p)
    for p in range(PAIRS):
        finish(p)
    for send in sends:
        send.wait()


def back_project(shears, shifts, tiles):
    hbm = pl.BlockSpec(memory_space=pltpu.HBM)
    return pl.pallas_call(
        back_kernel,
        name="back_project",
        in_specs=[hbm, hbm, pl.BlockSpec(memory_space=pltpu.VMEM)],
        out_specs=hbm,
        out_shape=jax.ShapeDtypeStruct((SLICES_DEV, DEPTH, BLOCKS * BLOCK), jnp.float32),
        scratch_shapes=[
            pltpu.VMEM((BWD_COARSE * DEPTH, BWD_FINE * ANGLES), jnp.bfloat16),
            pltpu.VMEM((PAIRS, BWD_FINE * ANGLES, 2 * WIDE), jnp.bfloat16),
            pltpu.VMEM((SLICES_DEV, DEPTH, BLOCKS * BLOCK), jnp.float32),
            pltpu.VMEM((TILES, ROWS + SLICES_DEV, BLOCK), jnp.float32),
            pltpu.SMEM((ANGLES,), jnp.float32),
            pltpu.SMEM((ANGLES,), jnp.int32),
            pltpu.SemaphoreType.DMA((2 + PAIRS,)),
        ],
        compiler_params=pltpu.CompilerParams(vmem_limit_bytes=VMEM_LIMIT),
    )(shears, shifts, tiles)


def dft_matrices():
    index = np.arange(SIDE)
    phase = (np.outer(index, index) % SIDE) * (2.0 * np.pi / SIDE)
    cos, sin = np.cos(phase), np.sin(phase)
    spread = np.block([[cos, -sin], [sin, cos]])
    gather = np.block([[cos, sin], [-sin, cos]]) / SIDE
    return jnp.asarray(spread, jnp.bfloat16), jnp.asarray(gather, jnp.bfloat16)


def copies_of(value, count):
    return jnp.broadcast_to(value, (count, *value.shape))


def between_chips(value):
    count = lax.axis_size("slab")
    groups = [list(range(core, count, 2)) for core in range(2)]
    return lax.all_to_all(value, "slab", 0, 0, tiled=True, axis_index_groups=groups)


def between_cores(value):
    return lax.ppermute(value, "slab", [(i, i ^ 1) for i in range(lax.axis_size("slab"))])


def body(volume, shears, tile_shift, illumination, measured, frame_owner, frame_shift):
    spread, gather = dft_matrices()
    shifts = tile_shift.reshape(ANGLES)
    parity = (lax.axis_index("slab") % 2).astype(jnp.int32).reshape(1)
    partials = project(shears, shifts, volume)
    landed = lax.all_to_all(partials, "tile", 0, 0, tiled=True)
    phase = jnp.sum(landed.astype(jnp.int32), axis=0)
    phase = (((phase + 32768) & 65535) - 32768).astype(jnp.int16)
    near_phases = between_chips(copies_of(phase, SLABS // 2))
    far_phases = between_cores(near_phases)
    near_grads, far_grads = frame_gradients(
        parity, frame_owner.reshape(FRAMES), frame_shift, near_phases, far_phases, illumination, measured, spread, gather
    )
    grads = near_grads.astype(jnp.float32) + between_cores(far_grads).astype(jnp.float32)
    landed = between_chips(grads.astype(jnp.bfloat16)).astype(jnp.float32)
    grad = landed[0]
    for i in range(1, SLABS // 2):
        grad = grad + landed[i]
    tiles = lax.all_to_all(copies_of(grad.astype(jnp.bfloat16), TILES), "tile", 0, 0, tiled=True)
    return back_project(shears, shifts, tiles)


def solution(mesh):
    in_specs = (
        P("slab", "tile", None),
        P(),
        P(None, "tile"),
        P(),
        P(("slab", "tile"), None, None),
        P(("slab", "tile"), None),
        P(("slab", "tile")),
    )
    out_specs = P("slab", "tile", None)
    return jax.shard_map(body, mesh=mesh, in_specs=in_specs, out_specs=out_specs, check_vma=False)
```
